32 devices in a mesh: gx: 4 (over z), gy: 4 (over y, x), gz: 2 (over core).
Axes of the slice: x: 2, y: 2, z: 4, core: 2. Of those that a mesh axis runs over, the one named last changes fastest.
Arguments:
- adjoint_residual: float32 [32, 64, 256], P('gx', 'gy', 'gz'), may hold values from -6 to 6
- face_x: float32 [32, 64, 256], P('gx', 'gy', 'gz'), may hold values from 0.03 to 30
- face_y: float32 [32, 64, 256], P('gx', 'gy', 'gz'), may hold values from 0.03 to 30
- face_z: float32 [32, 64, 256], P('gx', 'gy', 'gz'), may hold values from 0.03 to 30
Outputs:
- correction: float32 [32, 64, 256], P('gx', 'gy', 'gz')
The draws below stay inside these ranges and needn't reach their ends.
All inputs are finite; a program needn't handle non-finite values.
Results may differ from the reference program's by a relative error of at most 0.0001.
Values sent between devices are 32-bit elements; how exact they have to be, the bound alone decides.
No kernel may reach another device: no remote copies, remote signals or barrier semaphores. Data moves between devices by JAX's collectives and lax.ppermute only.
A program may use at most 64 MiB of HBM per device.

```python
import math
import jax
import jax.numpy as jnp
from jax import lax

LEVELS = 4
COARSE_ITERS = 6
NX = 32
NY = 64
NZ = 256


def level_of(stream_key, dims, pieces, smallest, largest):
    level, own = 1.0, jax.random.fold_in(stream_key, 6)
    for dim, blocks in pieces:
        heights = jnp.exp(jax.random.uniform(jax.random.fold_in(own, dim), (blocks,), jnp.float32, smallest / len(pieces), largest / len(pieces)))
        level = level * jnp.repeat(heights, dims[dim] // blocks).reshape([-1 if axis == dim else 1 for axis in range(len(dims))])
    return level


def bell_draw(key, shape, width, reach, pieces=(), dtype=jnp.bfloat16):
    values = jax.random.normal(key, shape, jnp.float32) * width
    if len(pieces) > 0:
        values = level_of(key, shape, pieces, -0.22, 0.18) * values
    return jnp.clip(values, min=-reach, max=reach).astype(dtype)


def setup_inputs(seed: int = 0) -> dict:
    keys = jax.random.split(jax.random.key(seed), 5)
    return {
        "adjoint_residual": bell_draw(keys[0], (NX, NY, NZ), 1.0, 6.0, ((0, 4), (1, 4), (2, 2)), jnp.float32),
        "face_x": jnp.clip(jnp.exp(math.log(30.0) - 6.9077553 * jax.random.uniform(keys[1], (NX, NY, NZ), jnp.float32) ** level_of(keys[1], (NX, NY, NZ), ((0, 4), (1, 4), (2, 2)), -0.2, 0.2)), 0.03, 30.0),
        "face_y": jnp.clip(jnp.exp(math.log(30.0) - 6.9077553 * jax.random.uniform(keys[2], (NX, NY, NZ), jnp.float32) ** level_of(keys[2], (NX, NY, NZ), ((0, 4), (1, 4), (2, 2)), -0.2, 0.2)), 0.03, 30.0),
        "face_z": jnp.clip(jnp.exp(math.log(30.0) - 6.9077553 * jax.random.uniform(keys[3], (NX, NY, NZ), jnp.float32) ** level_of(keys[3], (NX, NY, NZ), ((0, 4), (1, 4), (2, 2)), -0.2, 0.2)), 0.03, 30.0),
    }


damping = 2.0 / 3.0

def operate(field, coefs):
    low_x, high_x, low_y, high_y, low_z, high_z = coefs
    diagonal = low_x + high_x + low_y + high_y + low_z + high_z
    padded = jnp.pad(field, 1)
    result = diagonal * field - low_x * padded[:-2, 1:-1, 1:-1] - high_x * padded[2:, 1:-1, 1:-1]
    result = result - low_y * padded[1:-1, :-2, 1:-1] - high_y * padded[1:-1, 2:, 1:-1]
    return result - low_z * padded[1:-1, 1:-1, :-2] - high_z * padded[1:-1, 1:-1, 2:]

def blocked(values):
    return values.reshape(values.shape[0] // 2, 2, values.shape[1] // 2, 2, values.shape[2] // 2, 2)

def coarse_face(values, dim, parity):
    others = tuple((2 * k + 1 for k in range(3) if k != dim))
    summed = lax.optimization_barrier(jnp.sum(blocked(values), axis=others))
    return 0.5 * lax.index_in_dim(summed, parity, dim + 1, keepdims=False)

def coarsen(coefs):
    result = []
    for dim in range(3):
        result.append(coarse_face(coefs[2 * dim], dim, 0))
        result.append(coarse_face(coefs[2 * dim + 1], dim, 1))
    return tuple(result)

def restrict(values):
    return lax.optimization_barrier(jnp.sum(blocked(values), axis=(1, 3, 5)))

def prolong(values):
    shape_out = (values.shape[0] * 2, values.shape[1] * 2, values.shape[2] * 2)
    wide = jnp.broadcast_to(values[:, None, :, None, :, None], (values.shape[0], 2, values.shape[1], 2, values.shape[2], 2))
    return wide.reshape(shape_out)

def conj_grad(rhs, coefs):
    solution = jnp.zeros_like(rhs)
    remain = rhs
    search = rhs
    norm_now = jnp.sum(remain * remain)
    for step in range(COARSE_ITERS):
        image = operate(search, coefs)
        alpha = norm_now / jnp.sum(search * image)
        solution = solution + alpha * search
        remain = remain - alpha * image
        norm_next = jnp.sum(remain * remain)
        search = remain + norm_next / norm_now * search
        norm_now = norm_next
    return solution

def cycle(rhs, levels_left, coefs):
    if levels_left == 1:
        return conj_grad(rhs, coefs)
    diagonal = coefs[0] + coefs[1] + coefs[2] + coefs[3] + coefs[4] + coefs[5]
    field = damping * rhs / diagonal
    field = field + damping * (rhs - operate(field, coefs)) / diagonal
    remain = rhs - operate(field, coefs)
    field = field + prolong(cycle(restrict(remain), levels_left - 1, coarsen(coefs)))
    field = field + damping * (rhs - operate(field, coefs)) / diagonal
    return field

def reference(adjoint_residual, face_x, face_y, face_z):
    high_x = jnp.concatenate([face_x[1:], jnp.zeros_like(face_x[:1])], 0)
    high_y = jnp.concatenate([face_y[:, 1:], jnp.zeros_like(face_y[:, :1])], 1)
    high_z = jnp.concatenate([face_z[:, :, 1:], jnp.zeros_like(face_z[:, :, :1])], 2)
    coefs = (face_x, high_x, face_y, high_y, face_z, high_z)
    return cycle(adjoint_residual, LEVELS, coefs)
```

```python
import functools

import jax
import jax.numpy as jnp
from jax import lax
from jax.experimental import pallas as pl
from jax.experimental.pallas import tpu as pltpu
from jax.sharding import PartitionSpec as P

LEVELS = 4
COARSE_ITERS = 6


damping = 2.0 / 3.0

REACH = 3
TILE = 8


def up(v, axis):
    return pltpu.roll(v, v.shape[axis] - 1, axis)


def down(v, axis):
    return pltpu.roll(v, 1, axis)


def iota(shape, axis):
    return lax.broadcasted_iota(jnp.int32, shape, axis)


def chosen(mask):
    return jnp.where(mask, 1.0, 0.0).astype(jnp.bfloat16)


def select_dot(values, matrix):
    high = values.astype(jnp.bfloat16)
    rest = values - high.astype(jnp.float32)
    mid = rest.astype(jnp.bfloat16)
    low = (rest - mid.astype(jnp.float32)).astype(jnp.bfloat16)
    dot = functools.partial(jnp.dot, preferred_element_type=jnp.float32)
    return (dot(low, matrix) + dot(mid, matrix)) + dot(high, matrix)


def inverse(diagonal):
    return jnp.where(diagonal > 0.0, damping / jnp.where(diagonal > 0.0, diagonal, 1.0), 0.0)


def fine_kernel(own, side_x, side_y, t_out, k_out, m_out, ext, e1, rd, dg, e2, rows):
    nx, ny = own.shape[2], own.shape[3]
    nz = 2 * own.shape[4]
    half = own.shape[4]
    gx, gy, gz = lax.axis_index("gx"), lax.axis_index("gy"), lax.axis_index("gz")
    for h in range(2):
        z = slice(h * half, (h + 1) * half)
        for a in range(4):
            ext[a, REACH : REACH + nx, TILE : TILE + ny, z] = own[h, a]
            ext[a, :REACH, TILE : TILE + ny, z] = side_x[0, h, a]
            ext[a, REACH + nx :, TILE : TILE + ny, z] = side_x[1, h, a]
            ext[a, :, :TILE, z] = side_y[0, h, a]
            ext[a, :, TILE + ny :, z] = side_y[1, h, a]
    shape = (ny + 2 * TILE, nz)
    row, lane = iota(shape, 0), iota(shape, 1)
    inner_z = lane > 0
    in_y = jnp.logical_and(
        jnp.logical_or(gy > 0, row >= TILE),
        jnp.logical_or(gy < lax.axis_size("gy") - 1, row < TILE + ny),
    )

    def off(e, p):
        fy, fz = ext[2, p], jnp.where(inner_z, ext[3, p], 0.0)
        here = e[p]
        total = ext[1, p] * e[p - 1] + ext[1, p + 1] * e[p + 1]
        total = total + fy * down(here, 0) + up(fy * here, 0)
        return total + fz * down(here, 1) + up(fz * here, 1)

    for p in range(1, nx + 2 * REACH - 1):
        fy, fz = ext[2, p], ext[3, p]
        diagonal = ext[1, p] + ext[1, p + 1] + fy + up(fy, 0) + fz + up(jnp.where(inner_z, fz, 0.0), 1)
        inv = inverse(diagonal)
        dg[p], rd[p] = diagonal, inv
        e1[p] = ext[0, p] * inv
    for p in range(2, nx + 2 * REACH - 2):
        value = (2.0 - damping) * e1[p] + rd[p] * off(e1, p)
        inside = in_y
        if p < REACH:
            inside = jnp.logical_and(inside, gx > 0)
        if p >= REACH + nx:
            inside = jnp.logical_and(inside, gx < lax.axis_size("gx") - 1)
        e2[p] = jnp.where(inside, value, 0.0)

    def mine(v):
        v = v[TILE : TILE + ny]
        return jnp.where(gz == 0, v[:, :half], v[:, half:])

    sums = []
    for i in range(nx):
        p = REACH + i
        q = ext[0, p] - dg[p] * e2[p] + off(e2, p)
        fy, fz = ext[2, p], jnp.where(inner_z, ext[3, p], 0.0)
        inv = rd[p]
        t_out[i] = mine(e2[p] + inv * q)
        for n, k in enumerate((ext[1, p], ext[1, p + 1], fy, up(fy, 0), fz, up(fz, 1))):
            k_out[n, i] = mine(inv * k)
        sums.append(q[TILE : TILE + ny])
    inner = slice(TILE, TILE + ny)
    pairs = range(0, nx, 2)
    wide = [sums[i] + sums[i + 1] for i in pairs]
    wide += [0.5 * ext[1, REACH + i, inner] for i in pairs]
    wide += [0.5 * (ext[2, REACH + i, inner] + ext[2, REACH + i + 1, inner]) for i in pairs]
    thin = [0.5 * (ext[3, REACH + i, inner] + ext[3, REACH + i + 1, inner]) for i in pairs]
    fine, coarse = iota((nz, half), 0), iota((nz, half), 1)
    summed = select_dot(jnp.concatenate(wide, 0), chosen(fine // 2 == coarse))
    picked = select_dot(jnp.concatenate(thin, 0), chosen(fine == 2 * coarse))
    count = len(pairs) * ny
    rows[: 3 * count] = summed
    rows[3 * count :] = picked
    part = count // 2
    even = rows[pl.ds(0, 4 * part, stride=2)]
    odd = rows[pl.ds(1, 4 * part, stride=2)]
    kept = [even[:part] + odd[:part], even[part : 2 * part] + odd[part : 2 * part]]
    kept += [even[2 * part : 3 * part], even[3 * part :] + odd[3 * part :]]
    for a in range(2):
        m_out[a] = jnp.where(gz == 0, kept[a], kept[2 + a]).reshape(m_out.shape[1:])


def planes_of(ref):
    return [ref[p] for p in range(ref.shape[0])]


def level_parts(fx, fy, fz):
    shape = fy[0].shape
    row, lane = iota(shape, 0), iota(shape, 1)
    n = len(fx)
    zero = jnp.zeros(shape, jnp.float32)
    fym = [jnp.where(row > 0, v, 0.0) for v in fy]
    fzm = [jnp.where(lane > 0, v, 0.0) for v in fz]
    high = [fx[p + 1] if p + 1 < n else zero for p in range(n)]
    diagonal = [fx[p] + high[p] + fy[p] + up(fym[p], 0) + fz[p] + up(fzm[p], 1) for p in range(n)]

    def off(e):
        result = []
        for p in range(n):
            total = fym[p] * down(e[p], 0) + up(fym[p] * e[p], 0)
            total = total + fzm[p] * down(e[p], 1) + up(fzm[p] * e[p], 1)
            if p > 0:
                total = total + fx[p] * e[p - 1]
            if p + 1 < n:
                total = total + fx[p + 1] * e[p + 1]
            result.append(total)
        return result

    return diagonal, [inverse(d) for d in diagonal], off


def before(b, diagonal, inv, off):
    e1 = [v * r for v, r in zip(b, inv)]
    e2 = [(2.0 - damping) * e + r * o for e, r, o in zip(e1, inv, off(e1))]
    q = [v - d * e + o for v, d, e, o in zip(b, diagonal, e2, off(e2))]
    return [e + r * v for e, r, v in zip(e2, inv, q)], q


def after(t, c, inv, off):
    return [v + (1.0 - damping) * k + r * o for v, k, r, o in zip(t, c, inv, off(c))]


def coarse_solution(rhs, fx, fy, fz, depth):
    shape = rhs.shape
    row, lane = iota(shape, 0), iota(shape, 1)
    fxm = jnp.where(lane >= depth, fx, 0.0)
    fym = jnp.where(row > 0, fy, 0.0)
    fzm = jnp.where(lane % depth > 0, fz, 0.0)
    wide = shape[1]

    def up_x(v):
        return pltpu.roll(v, wide - depth, 1)

    hx, hy, hz = up_x(fxm), up(fym, 0), up(fzm, 1)
    diagonal = fx + hx + fy + hy + fz + hz

    def operate_packed(v):
        result = diagonal * v - fxm * pltpu.roll(v, depth, 1) - hx * up_x(v)
        result = result - fym * down(v, 0) - hy * up(v, 0)
        return result - fzm * down(v, 1) - hz * up(v, 1)

    def total(v):
        return jnp.sum(jnp.sum(v, axis=0, keepdims=True), axis=1, keepdims=True)

    solution = jnp.zeros_like(rhs)
    remain = rhs
    search = rhs
    norm_now = total(remain * remain)
    for step in range(COARSE_ITERS):
        image = operate_packed(search)
        alpha = norm_now / total(search * image)
        solution = solution + alpha * search
        if step + 1 < COARSE_ITERS:
            remain = remain - alpha * image
            norm_next = total(remain * remain)
            search = remain + norm_next / norm_now * search
            norm_now = norm_next
    return solution


def whole_kernel(here, there, t_in, k_in, out, grid, fold1, fold2, spread2, window, doubled):
    gx, gy, gz = lax.axis_index("gx"), lax.axis_index("gy"), lax.axis_index("gz")
    cx, cy = lax.axis_size("gx"), lax.axis_size("gy")
    bx, by = here.shape[2], here.shape[3]
    for k in range(cx * cy):
        x = jnp.bitwise_xor(gx, k % cx) * bx
        y = pl.multiple_of(jnp.bitwise_xor(gy, k // cx) * by, by)
        for a in range(2):
            grid[2 * gz + a, pl.ds(x, bx), pl.ds(y, by), :] = here[k, a]
            grid[2 * (1 - gz) + a, pl.ds(x, bx), pl.ds(y, by), :] = there[k, a]
    n1, m1, w1 = grid.shape[1:]
    b1, fx1, fy1, fz1 = (planes_of(grid.at[a]) for a in range(4))
    diagonal1, inv1, off1 = level_parts(fx1, fy1, fz1)
    t1, q1 = before(b1, diagonal1, inv1, off1)

    n2, m2 = n1 // 2, m1 // 2
    fine, coarse = iota((w1, w1), 0), iota((w1, w1), 1)
    both, even = chosen(fine // 2 == coarse), chosen(fine == 2 * coarse)
    pairs = range(0, n1, 2)
    wide = [q1[i] + q1[i + 1] for i in pairs] + [0.5 * fx1[i] for i in pairs]
    wide += [0.5 * (fy1[i] + fy1[i + 1]) for i in pairs]
    thin = [0.5 * (fz1[i] + fz1[i + 1]) for i in pairs]
    count = n2 * m1
    fold1[: 3 * count] = select_dot(jnp.concatenate(wide, 0), both)
    fold1[3 * count :] = select_dot(jnp.concatenate(thin, 0), even)
    half = n2 * m2
    low = fold1[pl.ds(0, 4 * half, stride=2)]
    top = fold1[pl.ds(1, 4 * half, stride=2)]

    def part(v):
        return [v[p * m2 : (p + 1) * m2] for p in range(n2)]

    b2 = part(low[:half] + top[:half])
    fx2 = part(low[half : 2 * half] + top[half : 2 * half])
    fy2 = part(low[2 * half : 3 * half])
    fz2 = part(low[3 * half :] + top[3 * half :])
    diagonal2, inv2, off2 = level_parts(fx2, fy2, fz2)
    t2, q2 = before(b2, diagonal2, inv2, off2)

    n3, m3 = n2 // 2, m2 // 2
    depth = w1 // n3
    packed = [0.0, 0.0, 0.0, 0.0]
    for i in range(n3):
        both = chosen((fine // 2 + i * depth == coarse) & (fine < 2 * depth))
        even = chosen((fine + 2 * i * depth == 2 * coarse) & (fine < 2 * depth))
        wide = [q2[2 * i] + q2[2 * i + 1], 0.5 * fx2[2 * i], 0.5 * (fy2[2 * i] + fy2[2 * i + 1])]
        thin = 0.5 * (fz2[2 * i] + fz2[2 * i + 1])
        summed = select_dot(jnp.concatenate(wide, 0), both)
        packed[0] = packed[0] + summed[:m2]
        packed[1] = packed[1] + summed[m2 : 2 * m2]
        packed[2] = packed[2] + summed[2 * m2 :]
        packed[3] = packed[3] + select_dot(thin, even)
    fold2[...] = jnp.concatenate(packed, 0)
    low = fold2[pl.ds(0, 4 * m3, stride=2)]
    top = fold2[pl.ds(1, 4 * m3, stride=2)]
    b3, fx3 = low[:m3] + top[:m3], low[m3 : 2 * m3] + top[m3 : 2 * m3]
    fy3, fz3 = low[2 * m3 : 3 * m3], low[3 * m3 :] + top[3 * m3 :]
    c3 = coarse_solution(b3, fx3, fy3, fz3, depth)

    for i in range(n3):
        row = select_dot(c3, chosen((coarse // 2 + i * depth == fine) & (coarse < 2 * depth)))
        spread2[pl.ds(i * m2, m3, stride=2)] = row
        spread2[pl.ds(i * m2 + 1, m3, stride=2)] = row
    up2 = [spread2[(p // 2) * m2 : (p // 2 + 1) * m2] for p in range(n2)]
    c2 = after(t2, up2, inv2, off2)

    row = select_dot(jnp.concatenate(c2, 0), chosen(coarse // 2 == fine))
    fold1[pl.ds(0, half, stride=2)] = row
    fold1[pl.ds(1, half, stride=2)] = row
    up1 = [fold1[(p // 2) * m1 : (p // 2 + 1) * m1] for p in range(n1)]
    c1 = after(t1, up1, inv1, off1)

    window[...] = jnp.zeros_like(window)
    for p in range(n1):
        window[1 + p, TILE : TILE + m1, :] = c1[p]
    y = pl.multiple_of(gy * by, by)
    near = window[pl.ds(gx * bx, bx + 2), pl.ds(y, by + 2 * TILE), :]
    tall = by + 2 * TILE
    near = near.reshape((bx + 2) * tall, w1)
    spot = gz * t_in.shape[2] + iota((w1, 3 * w1), 1) % w1 + (iota((w1, 3 * w1), 1) // w1 + 1) % 3 - 1
    wanted = iota((w1, 3 * w1), 0)
    row = select_dot(near, chosen((2 * wanted == spot) | (2 * wanted + 1 == spot)))
    for s in range(3):
        doubled[s, pl.ds(0, (bx + 2) * tall, stride=2)] = row[:, s * w1 : (s + 1) * w1]
        doubled[s, pl.ds(1, (bx + 2) * tall, stride=2)] = row[:, s * w1 : (s + 1) * w1]
    ny = t_in.shape[1]

    def at(s, i, shift):
        first = (1 + i // 2) * 2 * tall + 2 * TILE + shift
        return doubled[s, first : first + ny]

    for i in range(t_in.shape[0]):
        value = t_in[i] + (1.0 - damping) * at(0, i, 0)
        value = value + k_in[0, i] * at(0, i - 1, 0) + k_in[1, i] * at(0, i + 1, 0)
        value = value + k_in[2, i] * at(0, i, -1) + k_in[3, i] * at(0, i, 1)
        out[i] = value + k_in[4, i] * at(2, i, 0) + k_in[5, i] * at(1, i, 0)


def halves(block, axis, dim, width, reach):
    count, core = lax.axis_size(axis), lax.axis_index("gz")
    start = core * (block.shape[dim] - width)
    slab = lax.dynamic_slice_in_dim(block, start, width, dim)
    route = []
    for i in range(count - 1):
        route += [(2 * i + 1, 2 * i + 2), (2 * i + 2, 2 * i + 1)]
    taken = lax.ppermute(slab, (axis, "gz"), route)
    return lax.all_gather(taken, "gz", axis=0)


def doubled_over(block, axis):
    count = lax.axis_size(axis)
    step = 1
    while step < count:
        other = lax.ppermute(block, axis, [(i, i ^ step) for i in range(count)])
        block = jnp.concatenate([block, other], 0)
        step *= 2
    return block


def f32(*shape):
    return jax.ShapeDtypeStruct(shape, jnp.float32)


def per_device_small(adjoint_residual, face_x, face_y, face_z):
    nx, ny, nz = adjoint_residual.shape
    stacked = jnp.stack((adjoint_residual, face_x, face_y, face_z))
    own = lax.all_gather(stacked, "gz", axis=0)
    side_x = halves(own, "gx", 2, REACH, REACH)
    tall = jnp.concatenate([side_x[0], own, side_x[1]], 2)
    side_y = halves(tall, "gy", 3, TILE, REACH)
    ext_x, ext_y, wide = nx + 2 * REACH, ny + 2 * TILE, 2 * nz
    field = pltpu.VMEM((ext_x, ext_y, wide), jnp.float32)
    t, k, m = pl.pallas_call(
        fine_kernel,
        out_shape=(f32(nx, ny, nz), f32(6, nx, ny, nz), f32(2, nx // 2, ny // 2, nz)),
        scratch_shapes=[
            pltpu.VMEM((4, ext_x, ext_y, wide), jnp.float32),
            field,
            field,
            field,
            field,
            pltpu.VMEM((2 * nx * ny, nz), jnp.float32),
        ],
        name="fine",
    )(own, side_x, side_y)
    here = doubled_over(doubled_over(m[None], "gx"), "gy")
    there = lax.ppermute(here, "gz", [(0, 1), (1, 0)])
    n1, m1 = here.shape[2] * lax.axis_size("gx"), here.shape[3] * lax.axis_size("gy")
    tall = (nx // 2 + 2) * (ny // 2 + 2 * TILE)
    return pl.pallas_call(
        whole_kernel,
        out_shape=f32(nx, ny, nz),
        scratch_shapes=[
            pltpu.VMEM((4, n1, m1, nz), jnp.float32),
            pltpu.VMEM((2 * n1 * m1, nz), jnp.float32),
            pltpu.VMEM((2 * m1, nz), jnp.float32),
            pltpu.VMEM((n1 * m1 // 8, nz), jnp.float32),
            pltpu.VMEM((n1 + 2, m1 + 2 * TILE, nz), jnp.float32),
            pltpu.VMEM((3, 2 * tall, nz), jnp.float32),
        ],
        name="whole",
    )(here, there, t, k)


def extended(block, sides, width):
    for axis, dim in sides:
        count = lax.axis_size(axis)
        forward = [(i, i + 1) for i in range(count - 1)]
        backward = [(target, source) for source, target in forward]
        low = lax.ppermute(
            lax.slice_in_dim(block, block.shape[dim] - width, None, axis=dim), axis, forward
        )
        high = lax.ppermute(lax.slice_in_dim(block, 0, width, axis=dim), axis, backward)
        block = jnp.concatenate([low, block, high], axis=dim)
    return block


def from_behind(block, axis, distance):
    devices = range(lax.axis_size(axis))
    route = [(i - distance, i) for i in devices if i - distance in devices]
    return lax.ppermute(block, axis, route)


def stencil(padded, field, coefs):
    low_x, high_x, low_y, high_y, low_z, high_z = coefs
    diagonal = low_x + high_x + low_y + high_y + low_z + high_z
    result = diagonal * field - low_x * padded[:-2, 1:-1, 1:-1] - high_x * padded[2:, 1:-1, 1:-1]
    result = result - low_y * padded[1:-1, :-2, 1:-1] - high_y * padded[1:-1, 2:, 1:-1]
    return result - low_z * padded[1:-1, 1:-1, :-2] - high_z * padded[1:-1, 1:-1, 2:]


def operate(field, coefs):
    padded = extended(field, (("gx", 0), ("gy", 1), ("gz", 2)), 1)
    return stencil(padded, field, coefs)


def operate_whole(field, coefs):
    return stencil(jnp.pad(field, 1), field, coefs)


def blocked(values):
    return values.reshape(values.shape[0] // 2, 2, values.shape[1] // 2, 2, values.shape[2] // 2, 2)


def coarse_face(values, dim, parity):
    others = tuple((2 * k + 1 for k in range(3) if k != dim))
    summed = jnp.sum(blocked(values), axis=others)
    return 0.5 * lax.index_in_dim(summed, parity, dim + 1, keepdims=False)


def coarsen(coefs):
    result = []
    for dim in range(3):
        result.append(coarse_face(coefs[2 * dim], dim, 0))
        result.append(coarse_face(coefs[2 * dim + 1], dim, 1))
    return tuple(result)


def restrict(values):
    return jnp.sum(blocked(values), axis=(1, 3, 5))


def prolong(values):
    shape_out = (values.shape[0] * 2, values.shape[1] * 2, values.shape[2] * 2)
    wide = jnp.broadcast_to(
        values[:, None, :, None, :, None],
        (values.shape[0], 2, values.shape[1], 2, values.shape[2], 2),
    )
    return wide.reshape(shape_out)


def total_local(value):
    return value


def conj_grad(rhs, coefs, apply_op, total):
    solution = jnp.zeros_like(rhs)
    remain = rhs
    search = rhs
    norm_now = total(jnp.sum(remain * remain))
    for step in range(COARSE_ITERS):
        image = apply_op(search, coefs)
        alpha = norm_now / total(jnp.sum(search * image))
        solution = solution + alpha * search
        remain = remain - alpha * image
        norm_next = total(jnp.sum(remain * remain))
        search = remain + norm_next / norm_now * search
        norm_now = norm_next
    return solution


def coarse_solve(rhs, coefs):
    part_x, part_y, part_z = rhs.shape
    count_x = lax.axis_size("gx")
    count_y = lax.axis_size("gy")
    count_z = lax.axis_size("gz")
    stacked = jnp.stack((rhs,) + coefs)[None]
    whole = lax.all_gather(stacked, ("gx", "gy", "gz"), axis=0, tiled=True)
    whole = whole.reshape(count_x, count_y, count_z, 7, part_x, part_y, part_z)
    whole = whole.transpose(3, 0, 4, 1, 5, 2, 6).reshape(
        7, count_x * part_x, count_y * part_y, count_z * part_z
    )
    whole_coefs = tuple((whole[k] for k in range(1, 7)))
    solution = conj_grad(whole[0], whole_coefs, operate_whole, total_local)
    starts = (
        lax.axis_index("gx") * part_x,
        lax.axis_index("gy") * part_y,
        lax.axis_index("gz") * part_z,
    )
    return lax.dynamic_slice(solution, starts, (part_x, part_y, part_z))


def cycle(rhs, levels_left, coefs):
    if levels_left == 1:
        return coarse_solve(rhs, coefs)
    diagonal = coefs[0] + coefs[1] + coefs[2] + coefs[3] + coefs[4] + coefs[5]
    field = damping * rhs / diagonal
    field = field + damping * (rhs - operate(field, coefs)) / diagonal
    remain = rhs - operate(field, coefs)
    field = field + prolong(cycle(restrict(remain), levels_left - 1, coarsen(coefs)))
    field = field + damping * (rhs - operate(field, coefs)) / diagonal
    return field


def per_device(adjoint_residual, face_x, face_y, face_z):
    rim_x = from_behind(face_x[:1], "gx", -1)
    rim_y = from_behind(face_y[:, :1], "gy", -1)
    rim_z = from_behind(face_z[:, :, :1], "gz", -1)
    high_x = jnp.concatenate([face_x[1:], rim_x], 0)
    high_y = jnp.concatenate([face_y[:, 1:], rim_y], 1)
    high_z = jnp.concatenate([face_z[:, :, 1:], rim_z], 2)
    coefs = (face_x, high_x, face_y, high_y, face_z, high_z)
    return cycle(adjoint_residual, LEVELS, coefs)


def fits(mesh, shape):
    nx, ny, nz = shape
    cx, cy, cz = mesh.shape["gx"], mesh.shape["gy"], mesh.shape["gz"]
    powers = cx & (cx - 1) == 0 and cy & (cy - 1) == 0 and cz == 2
    blocks = nx % (8 * cx) == 0 and ny % (16 * cy) == 0 and nz == 256
    return powers and blocks and (nx // 8) * (nz // 8) == 128 and nx * ny * nz <= 2**19


def per_block(mesh, *args):
    counts = (mesh.shape["gx"], mesh.shape["gy"], mesh.shape["gz"])
    whole = tuple(n * c for n, c in zip(args[0].shape, counts))
    return (per_device_small if fits(mesh, whole) else per_device)(*args)


def solution(mesh):
    return jax.shard_map(
        functools.partial(per_block, mesh),
        mesh=mesh,
        in_specs=(
            P("gx", "gy", "gz"),
            P("gx", "gy", "gz"),
            P("gx", "gy", "gz"),
            P("gx", "gy", "gz"),
        ),
        out_specs=P("gx", "gy", "gz"),
        check_vma=False,
    )
```

```python
import functools

import jax
import jax.numpy as jnp
from jax import lax
from jax.experimental import pallas as pl
from jax.experimental.pallas import tpu as pltpu
from jax.sharding import PartitionSpec as P

LEVELS = 4
COARSE_ITERS = 6


damping = 2.0 / 3.0

REACH = 3
TILE = 8


def up(v, axis):
    return pltpu.roll(v, v.shape[axis] - 1, axis)


def down(v, axis):
    return pltpu.roll(v, 1, axis)


def iota(shape, axis):
    return lax.broadcasted_iota(jnp.int32, shape, axis)


def chosen(mask):
    return jnp.where(mask, 1.0, 0.0).astype(jnp.bfloat16)


def select_dot(values, matrix):
    high = values.astype(jnp.bfloat16)
    rest = values - high.astype(jnp.float32)
    mid = rest.astype(jnp.bfloat16)
    low = (rest - mid.astype(jnp.float32)).astype(jnp.bfloat16)
    dot = functools.partial(jnp.dot, preferred_element_type=jnp.float32)
    return (dot(low, matrix) + dot(mid, matrix)) + dot(high, matrix)


def inverse(diagonal):
    return jnp.where(diagonal > 0.0, damping / jnp.where(diagonal > 0.0, diagonal, 1.0), 0.0)


def pack_kernel(own, x_out, y_out, c0_out, c1_out):
    nx, ny = own.shape[2], own.shape[3]
    gx, gy, gz = lax.axis_index("gx"), lax.axis_index("gy"), lax.axis_index("gz")

    def start(kind):
        return jnp.where((gx + kind) % 2 == 0, nx - 2, 0)

    ahead = (gy + gz) % 2 == 0

    def edge(h, a, i):
        return jnp.where(ahead, own[h, a, i, ny - 2 :, :], own[h, a, i, :2, :])

    for h in range(2):
        for a in range(4):
            for n in range(2):
                x_out[h, 2 * a + n] = own[h, a, start(gz) + n]
            for i in range(nx):
                y_out[h, (a * nx + i) * 2 : (a * nx + i) * 2 + 2] = edge(h, a, i)
            for n in range(2):
                for kind, out in enumerate((c0_out, c1_out)):
                    out[h, (2 * a + n) * 2 : (2 * a + n) * 2 + 2] = edge(h, a, start(kind) + n)
        x_out[h, 8] = own[h, 1, 2]
        for i in range(nx):
            y_out[h, 8 * nx + i : 8 * nx + i + 1] = own[h, 2, i, 2:3, :]


def fine_kernel(own, shared, t_out, k_out, m_out, ext, e1, rd, dg, e2, rows):
    nx, ny = own.shape[2], own.shape[3]
    nz = 2 * own.shape[4]
    half = own.shape[4]
    gx, gy, gz = lax.axis_index("gx"), lax.axis_index("gy"), lax.axis_index("gz")
    first = {
        "x": 0,
        "y": 2 * 9 * ny,
        "c": 2 * 9 * ny + 2 * 9 * nx,
    }
    for a in range(4):
        for p in range(nx + 2 * REACH):
            edge = p < REACH or p >= REACH + nx
            spans = [slice(0, ny + 2 * TILE)] if edge else [slice(0, TILE), slice(TILE + ny, ny + 2 * TILE)]
            for span in spans:
                ext[a, p, span] = jnp.zeros((span.stop - span.start, nz), jnp.float32)
    sides_x = (
        (REACH - 2, jnp.where(gx > 0, 1.0, 0.0), 1 - gx % 2),
        (REACH + nx, jnp.where(gx < lax.axis_size("gx") - 1, 1.0, 0.0), gx % 2),
    )
    sides_y = (
        (TILE - 2, jnp.where(gy > 0, 1.0, 0.0), 1 - gy % 2),
        (TILE + ny, jnp.where(gy < lax.axis_size("gy") - 1, 1.0, 0.0), gy % 2),
    )
    for h in range(2):
        z = slice(h * half, (h + 1) * half)
        for a in range(4):
            ext[a, REACH : REACH + nx, TILE : TILE + ny, z] = own[h, a]
        for p, keep, kind in sides_x:
            for n in range(9):
                a, l = (n // 2, n % 2) if n < 8 else (1, 2)
                at = first["x"] + (9 * h + n) * ny
                if n < 8 or p > REACH:
                    ext[a, p + l, TILE : TILE + ny, z] = keep * shared[kind, at : at + ny]
        for r, keep, kind in sides_y:
            for i in range(nx):
                for a in range(4):
                    at = first["y"] + 9 * nx * h + (a * nx + i) * 2
                    ext[a, REACH + i, r : r + 2, z] = keep * shared[kind, at : at + 2]
                if r > TILE:
                    at = first["y"] + 9 * nx * h + 8 * nx + i
                    ext[2, REACH + i, r + 2 : r + 3, z] = keep * shared[kind, at : at + 1]
        for p, keep_x, kind_x in sides_x:
            for r, keep_y, kind_y in sides_y:
                keep = keep_x * keep_y
                at = pl.multiple_of(first["c"] + 32 * kind_x + 16 * h, 8)
                lines = keep * shared[kind_y, pl.ds(at, 16)]
                for a in range(4):
                    for l in range(2):
                        n = (2 * a + l) * 2
                        ext[a, p + l, r : r + 2, z] = lines[n : n + 2]
    shape = (ny + 2 * TILE, nz)
    row, lane = iota(shape, 0), iota(shape, 1)
    inner_z = lane > 0
    in_y = jnp.logical_and(
        jnp.logical_or(gy > 0, row >= TILE),
        jnp.logical_or(gy < lax.axis_size("gy") - 1, row < TILE + ny),
    )

    def off(e, p):
        fy, fz = ext[2, p], jnp.where(inner_z, ext[3, p], 0.0)
        here = e[p]
        total = ext[1, p] * e[p - 1] + ext[1, p + 1] * e[p + 1]
        total = total + fy * down(here, 0) + up(fy * here, 0)
        return total + fz * down(here, 1) + up(fz * here, 1)

    for p in range(1, nx + 2 * REACH - 1):
        fy, fz = ext[2, p], ext[3, p]
        diagonal = ext[1, p] + ext[1, p + 1] + fy + up(fy, 0) + fz + up(jnp.where(inner_z, fz, 0.0), 1)
        inv = inverse(diagonal)
        dg[p], rd[p] = diagonal, inv
        e1[p] = ext[0, p] * inv
    for p in range(2, nx + 2 * REACH - 2):
        value = (2.0 - damping) * e1[p] + rd[p] * off(e1, p)
        inside = in_y
        if p < REACH:
            inside = jnp.logical_and(inside, gx > 0)
        if p >= REACH + nx:
            inside = jnp.logical_and(inside, gx < lax.axis_size("gx") - 1)
        e2[p] = jnp.where(inside, value, 0.0)

    def mine(v):
        v = v[TILE : TILE + ny]
        return jnp.where(gz == 0, v[:, :half], v[:, half:])

    sums = []
    for i in range(nx):
        p = REACH + i
        q = ext[0, p] - dg[p] * e2[p] + off(e2, p)
        fy, fz = ext[2, p], jnp.where(inner_z, ext[3, p], 0.0)
        inv = rd[p]
        t_out[i] = mine(e2[p] + inv * q)
        for n, k in enumerate((ext[1, p], ext[1, p + 1], fy, up(fy, 0), fz, up(fz, 1))):
            k_out[n, i] = mine(inv * k)
        sums.append(q[TILE : TILE + ny])
    inner = slice(TILE, TILE + ny)
    pairs = range(0, nx, 2)
    wide = [sums[i] + sums[i + 1] for i in pairs]
    wide += [0.5 * ext[1, REACH + i, inner] for i in pairs]
    wide += [0.5 * (ext[2, REACH + i, inner] + ext[2, REACH + i + 1, inner]) for i in pairs]
    thin = [0.5 * (ext[3, REACH + i, inner] + ext[3, REACH + i + 1, inner]) for i in pairs]
    fine, coarse = iota((nz, half), 0), iota((nz, half), 1)
    summed = select_dot(jnp.concatenate(wide, 0), chosen(fine // 2 == coarse))
    picked = select_dot(jnp.concatenate(thin, 0), chosen(fine == 2 * coarse))
    count = len(pairs) * ny
    rows[: 3 * count] = summed
    rows[3 * count :] = picked
    part = count // 2
    even = rows[pl.ds(0, 4 * part, stride=2)]
    odd = rows[pl.ds(1, 4 * part, stride=2)]
    kept = [even[:part] + odd[:part], even[part : 2 * part] + odd[part : 2 * part]]
    kept += [even[2 * part : 3 * part], even[3 * part :] + odd[3 * part :]]
    for a in range(2):
        m_out[a] = jnp.where(gz == 0, kept[a], kept[2 + a]).reshape(m_out.shape[1:])


def planes_of(ref):
    return [ref[p] for p in range(ref.shape[0])]


def level_parts(fx, fy, fz):
    shape = fy[0].shape
    row, lane = iota(shape, 0), iota(shape, 1)
    n = len(fx)
    zero = jnp.zeros(shape, jnp.float32)
    fym = [jnp.where(row > 0, v, 0.0) for v in fy]
    fzm = [jnp.where(lane > 0, v, 0.0) for v in fz]
    high = [fx[p + 1] if p + 1 < n else zero for p in range(n)]
    diagonal = [fx[p] + high[p] + fy[p] + up(fym[p], 0) + fz[p] + up(fzm[p], 1) for p in range(n)]

    def off(e):
        result = []
        for p in range(n):
            total = fym[p] * down(e[p], 0) + up(fym[p] * e[p], 0)
            total = total + fzm[p] * down(e[p], 1) + up(fzm[p] * e[p], 1)
            if p > 0:
                total = total + fx[p] * e[p - 1]
            if p + 1 < n:
                total = total + fx[p + 1] * e[p + 1]
            result.append(total)
        return result

    return diagonal, [inverse(d) for d in diagonal], off


def before(b, diagonal, inv, off):
    e1 = [v * r for v, r in zip(b, inv)]
    e2 = [(2.0 - damping) * e + r * o for e, r, o in zip(e1, inv, off(e1))]
    q = [v - d * e + o for v, d, e, o in zip(b, diagonal, e2, off(e2))]
    return [e + r * v for e, r, v in zip(e2, inv, q)], q


def after(t, c, inv, off):
    return [v + (1.0 - damping) * k + r * o for v, k, r, o in zip(t, c, inv, off(c))]


def coarse_solution(rhs, fx, fy, fz, depth):
    shape = rhs.shape
    row, lane = iota(shape, 0), iota(shape, 1)
    fxm = jnp.where(lane >= depth, fx, 0.0)
    fym = jnp.where(row > 0, fy, 0.0)
    fzm = jnp.where(lane % depth > 0, fz, 0.0)
    wide = shape[1]

    def up_x(v):
        return pltpu.roll(v, wide - depth, 1)

    hx, hy, hz = up_x(fxm), up(fym, 0), up(fzm, 1)
    diagonal = fx + hx + fy + hy + fz + hz

    def operate_packed(v):
        result = diagonal * v - fxm * pltpu.roll(v, depth, 1) - hx * up_x(v)
        result = result - fym * down(v, 0) - hy * up(v, 0)
        return result - fzm * down(v, 1) - hz * up(v, 1)

    def total(v):
        return jnp.sum(jnp.sum(v, axis=0, keepdims=True), axis=1, keepdims=True)

    solution = jnp.zeros_like(rhs)
    remain = rhs
    search = rhs
    norm_now = total(remain * remain)
    for step in range(COARSE_ITERS):
        image = operate_packed(search)
        alpha = norm_now / total(search * image)
        solution = solution + alpha * search
        if step + 1 < COARSE_ITERS:
            remain = remain - alpha * image
            norm_next = total(remain * remain)
            search = remain + norm_next / norm_now * search
            norm_now = norm_next
    return solution


def whole_kernel(here, there, t_in, k_in, out, grid, fold1, fold2, spread2, window, doubled):
    gx, gy, gz = lax.axis_index("gx"), lax.axis_index("gy"), lax.axis_index("gz")
    cx, cy = lax.axis_size("gx"), lax.axis_size("gy")
    bx, by = here.shape[2], here.shape[3]
    for k in range(cx * cy):
        x = jnp.bitwise_xor(gx, k % cx) * bx
        y = pl.multiple_of(jnp.bitwise_xor(gy, k // cx) * by, by)
        for a in range(2):
            grid[2 * gz + a, pl.ds(x, bx), pl.ds(y, by), :] = here[k, a]
            grid[2 * (1 - gz) + a, pl.ds(x, bx), pl.ds(y, by), :] = there[k, a]
    n1, m1, w1 = grid.shape[1:]
    b1, fx1, fy1, fz1 = (planes_of(grid.at[a]) for a in range(4))
    diagonal1, inv1, off1 = level_parts(fx1, fy1, fz1)
    t1, q1 = before(b1, diagonal1, inv1, off1)

    n2, m2 = n1 // 2, m1 // 2
    fine, coarse = iota((w1, w1), 0), iota((w1, w1), 1)
    both, even = chosen(fine // 2 == coarse), chosen(fine == 2 * coarse)
    pairs = range(0, n1, 2)
    wide = [q1[i] + q1[i + 1] for i in pairs] + [0.5 * fx1[i] for i in pairs]
    wide += [0.5 * (fy1[i] + fy1[i + 1]) for i in pairs]
    thin = [0.5 * (fz1[i] + fz1[i + 1]) for i in pairs]
    count = n2 * m1
    fold1[: 3 * count] = select_dot(jnp.concatenate(wide, 0), both)
    fold1[3 * count :] = select_dot(jnp.concatenate(thin, 0), even)
    half = n2 * m2
    low = fold1[pl.ds(0, 4 * half, stride=2)]
    top = fold1[pl.ds(1, 4 * half, stride=2)]

    def part(v):
        return [v[p * m2 : (p + 1) * m2] for p in range(n2)]

    b2 = part(low[:half] + top[:half])
    fx2 = part(low[half : 2 * half] + top[half : 2 * half])
    fy2 = part(low[2 * half : 3 * half])
    fz2 = part(low[3 * half :] + top[3 * half :])
    diagonal2, inv2, off2 = level_parts(fx2, fy2, fz2)
    t2, q2 = before(b2, diagonal2, inv2, off2)

    n3, m3 = n2 // 2, m2 // 2
    depth = w1 // n3
    packed = [0.0, 0.0, 0.0, 0.0]
    for i in range(n3):
        both = chosen((fine // 2 + i * depth == coarse) & (fine < 2 * depth))
        even = chosen((fine + 2 * i * depth == 2 * coarse) & (fine < 2 * depth))
        wide = [q2[2 * i] + q2[2 * i + 1], 0.5 * fx2[2 * i], 0.5 * (fy2[2 * i] + fy2[2 * i + 1])]
        thin = 0.5 * (fz2[2 * i] + fz2[2 * i + 1])
        summed = select_dot(jnp.concatenate(wide, 0), both)
        packed[0] = packed[0] + summed[:m2]
        packed[1] = packed[1] + summed[m2 : 2 * m2]
        packed[2] = packed[2] + summed[2 * m2 :]
        packed[3] = packed[3] + select_dot(thin, even)
    fold2[...] = jnp.concatenate(packed, 0)
    low = fold2[pl.ds(0, 4 * m3, stride=2)]
    top = fold2[pl.ds(1, 4 * m3, stride=2)]
    b3, fx3 = low[:m3] + top[:m3], low[m3 : 2 * m3] + top[m3 : 2 * m3]
    fy3, fz3 = low[2 * m3 : 3 * m3], low[3 * m3 :] + top[3 * m3 :]
    c3 = coarse_solution(b3, fx3, fy3, fz3, depth)

    for i in range(n3):
        row = select_dot(c3, chosen((coarse // 2 + i * depth == fine) & (coarse < 2 * depth)))
        spread2[pl.ds(i * m2, m3, stride=2)] = row
        spread2[pl.ds(i * m2 + 1, m3, stride=2)] = row
    up2 = [spread2[(p // 2) * m2 : (p // 2 + 1) * m2] for p in range(n2)]
    c2 = after(t2, up2, inv2, off2)

    row = select_dot(jnp.concatenate(c2, 0), chosen(coarse // 2 == fine))
    fold1[pl.ds(0, half, stride=2)] = row
    fold1[pl.ds(1, half, stride=2)] = row
    up1 = [fold1[(p // 2) * m1 : (p // 2 + 1) * m1] for p in range(n1)]
    c1 = after(t1, up1, inv1, off1)

    window[...] = jnp.zeros_like(window)
    for p in range(n1):
        window[1 + p, TILE : TILE + m1, :] = c1[p]
    y = pl.multiple_of(gy * by, by)
    near = window[pl.ds(gx * bx, bx + 2), pl.ds(y, by + 2 * TILE), :]
    tall = by + 2 * TILE
    near = near.reshape((bx + 2) * tall, w1)
    spot = gz * t_in.shape[2] + iota((w1, 3 * w1), 1) % w1 + (iota((w1, 3 * w1), 1) // w1 + 1) % 3 - 1
    wanted = iota((w1, 3 * w1), 0)
    row = select_dot(near, chosen((2 * wanted == spot) | (2 * wanted + 1 == spot)))
    for s in range(3):
        doubled[s, pl.ds(0, (bx + 2) * tall, stride=2)] = row[:, s * w1 : (s + 1) * w1]
        doubled[s, pl.ds(1, (bx + 2) * tall, stride=2)] = row[:, s * w1 : (s + 1) * w1]
    ny = t_in.shape[1]

    def at(s, i, shift):
        first = (1 + i // 2) * 2 * tall + 2 * TILE + shift
        return doubled[s, first : first + ny]

    for i in range(t_in.shape[0]):
        value = t_in[i] + (1.0 - damping) * at(0, i, 0)
        value = value + k_in[0, i] * at(0, i - 1, 0) + k_in[1, i] * at(0, i + 1, 0)
        value = value + k_in[2, i] * at(0, i, -1) + k_in[3, i] * at(0, i, 1)
        out[i] = value + k_in[4, i] * at(2, i, 0) + k_in[5, i] * at(1, i, 0)


def pair(i, kind, count):
    return i ^ 1 if kind == 0 else (i + 1 if i % 2 else i - 1) % count


def swap(block, to):
    cx, cy, cz = (lax.axis_size(axis) for axis in ("gx", "gy", "gz"))
    route = []
    for i in range(cx):
        for j in range(cy):
            for c in range(cz):
                x, y, z = to(i, j, c)
                route.append(((i * cy + j) * cz + c, (x * cy + y) * cz + z))
    return lax.ppermute(block, ("gx", "gy", "gz"), route)


def gathered(block, axis):
    count = lax.axis_size(axis)
    parts = [lax.ppermute(block, axis, [(i, i ^ k) for i in range(count)]) for k in range(1, count)]
    return jnp.concatenate([block] + parts, 0)


def f32(*shape):
    return jax.ShapeDtypeStruct(shape, jnp.float32)


def per_device_small(adjoint_residual, face_x, face_y, face_z):
    nx, ny, nz = adjoint_residual.shape
    stacked = jnp.stack((adjoint_residual, face_x, face_y, face_z))
    own = lax.all_gather(stacked, "gz", axis=0)
    cx, cy = lax.axis_size("gx"), lax.axis_size("gy")
    packed = pl.pallas_call(
        pack_kernel,
        out_shape=(f32(2, 9, ny, nz), f32(2, 9 * nx, nz), f32(2, 16, nz), f32(2, 16, nz)),
        name="pack",
    )(own)
    routes = (
        lambda i, j, c: (pair(i, c, cx), j, c),
        lambda i, j, c: (i, pair(j, c, cy), c),
        lambda i, j, c: (pair(i, 0, cx), pair(j, c, cy), c),
        lambda i, j, c: (pair(i, 1, cx), pair(j, c, cy), c),
    )
    taken = [swap(block.reshape(-1, nz), route) for block, route in zip(packed, routes)]
    shared = lax.all_gather(jnp.concatenate(taken, 0), "gz", axis=0)
    ext_x, ext_y, wide = nx + 2 * REACH, ny + 2 * TILE, 2 * nz
    field = pltpu.VMEM((ext_x, ext_y, wide), jnp.float32)
    t, k, m = pl.pallas_call(
        fine_kernel,
        out_shape=(f32(nx, ny, nz), f32(6, nx, ny, nz), f32(2, nx // 2, ny // 2, nz)),
        scratch_shapes=[
            pltpu.VMEM((4, ext_x, ext_y, wide), jnp.float32),
            field,
            field,
            field,
            field,
            pltpu.VMEM((2 * nx * ny, nz), jnp.float32),
        ],
        name="fine",
    )(own, shared)
    here = gathered(gathered(m[None], "gx"), "gy")
    there = lax.ppermute(here, "gz", [(0, 1), (1, 0)])
    n1, m1 = here.shape[2] * lax.axis_size("gx"), here.shape[3] * lax.axis_size("gy")
    tall = (nx // 2 + 2) * (ny // 2 + 2 * TILE)
    return pl.pallas_call(
        whole_kernel,
        out_shape=f32(nx, ny, nz),
        scratch_shapes=[
            pltpu.VMEM((4, n1, m1, nz), jnp.float32),
            pltpu.VMEM((2 * n1 * m1, nz), jnp.float32),
            pltpu.VMEM((2 * m1, nz), jnp.float32),
            pltpu.VMEM((n1 * m1 // 8, nz), jnp.float32),
            pltpu.VMEM((n1 + 2, m1 + 2 * TILE, nz), jnp.float32),
            pltpu.VMEM((3, 2 * tall, nz), jnp.float32),
        ],
        name="whole",
    )(here, there, t, k)


def extended(block, sides, width):
    for axis, dim in sides:
        count = lax.axis_size(axis)
        forward = [(i, i + 1) for i in range(count - 1)]
        backward = [(target, source) for source, target in forward]
        low = lax.ppermute(
            lax.slice_in_dim(block, block.shape[dim] - width, None, axis=dim), axis, forward
        )
        high = lax.ppermute(lax.slice_in_dim(block, 0, width, axis=dim), axis, backward)
        block = jnp.concatenate([low, block, high], axis=dim)
    return block


def from_behind(block, axis, distance):
    devices = range(lax.axis_size(axis))
    route = [(i - distance, i) for i in devices if i - distance in devices]
    return lax.ppermute(block, axis, route)


def stencil(padded, field, coefs):
    low_x, high_x, low_y, high_y, low_z, high_z = coefs
    diagonal = low_x + high_x + low_y + high_y + low_z + high_z
    result = diagonal * field - low_x * padded[:-2, 1:-1, 1:-1] - high_x * padded[2:, 1:-1, 1:-1]
    result = result - low_y * padded[1:-1, :-2, 1:-1] - high_y * padded[1:-1, 2:, 1:-1]
    return result - low_z * padded[1:-1, 1:-1, :-2] - high_z * padded[1:-1, 1:-1, 2:]


def operate(field, coefs):
    padded = extended(field, (("gx", 0), ("gy", 1), ("gz", 2)), 1)
    return stencil(padded, field, coefs)


def operate_whole(field, coefs):
    return stencil(jnp.pad(field, 1), field, coefs)


def blocked(values):
    return values.reshape(values.shape[0] // 2, 2, values.shape[1] // 2, 2, values.shape[2] // 2, 2)


def coarse_face(values, dim, parity):
    others = tuple((2 * k + 1 for k in range(3) if k != dim))
    summed = jnp.sum(blocked(values), axis=others)
    return 0.5 * lax.index_in_dim(summed, parity, dim + 1, keepdims=False)


def coarsen(coefs):
    result = []
    for dim in range(3):
        result.append(coarse_face(coefs[2 * dim], dim, 0))
        result.append(coarse_face(coefs[2 * dim + 1], dim, 1))
    return tuple(result)


def restrict(values):
    return jnp.sum(blocked(values), axis=(1, 3, 5))


def prolong(values):
    shape_out = (values.shape[0] * 2, values.shape[1] * 2, values.shape[2] * 2)
    wide = jnp.broadcast_to(
        values[:, None, :, None, :, None],
        (values.shape[0], 2, values.shape[1], 2, values.shape[2], 2),
    )
    return wide.reshape(shape_out)


def total_local(value):
    return value


def conj_grad(rhs, coefs, apply_op, total):
    solution = jnp.zeros_like(rhs)
    remain = rhs
    search = rhs
    norm_now = total(jnp.sum(remain * remain))
    for step in range(COARSE_ITERS):
        image = apply_op(search, coefs)
        alpha = norm_now / total(jnp.sum(search * image))
        solution = solution + alpha * search
        remain = remain - alpha * image
        norm_next = total(jnp.sum(remain * remain))
        search = remain + norm_next / norm_now * search
        norm_now = norm_next
    return solution


def coarse_solve(rhs, coefs):
    part_x, part_y, part_z = rhs.shape
    count_x = lax.axis_size("gx")
    count_y = lax.axis_size("gy")
    count_z = lax.axis_size("gz")
    stacked = jnp.stack((rhs,) + coefs)[None]
    whole = lax.all_gather(stacked, ("gx", "gy", "gz"), axis=0, tiled=True)
    whole = whole.reshape(count_x, count_y, count_z, 7, part_x, part_y, part_z)
    whole = whole.transpose(3, 0, 4, 1, 5, 2, 6).reshape(
        7, count_x * part_x, count_y * part_y, count_z * part_z
    )
    whole_coefs = tuple((whole[k] for k in range(1, 7)))
    solution = conj_grad(whole[0], whole_coefs, operate_whole, total_local)
    starts = (
        lax.axis_index("gx") * part_x,
        lax.axis_index("gy") * part_y,
        lax.axis_index("gz") * part_z,
    )
    return lax.dynamic_slice(solution, starts, (part_x, part_y, part_z))


def cycle(rhs, levels_left, coefs):
    if levels_left == 1:
        return coarse_solve(rhs, coefs)
    diagonal = coefs[0] + coefs[1] + coefs[2] + coefs[3] + coefs[4] + coefs[5]
    field = damping * rhs / diagonal
    field = field + damping * (rhs - operate(field, coefs)) / diagonal
    remain = rhs - operate(field, coefs)
    field = field + prolong(cycle(restrict(remain), levels_left - 1, coarsen(coefs)))
    field = field + damping * (rhs - operate(field, coefs)) / diagonal
    return field


def per_device(adjoint_residual, face_x, face_y, face_z):
    rim_x = from_behind(face_x[:1], "gx", -1)
    rim_y = from_behind(face_y[:, :1], "gy", -1)
    rim_z = from_behind(face_z[:, :, :1], "gz", -1)
    high_x = jnp.concatenate([face_x[1:], rim_x], 0)
    high_y = jnp.concatenate([face_y[:, 1:], rim_y], 1)
    high_z = jnp.concatenate([face_z[:, :, 1:], rim_z], 2)
    coefs = (face_x, high_x, face_y, high_y, face_z, high_z)
    return cycle(adjoint_residual, LEVELS, coefs)


def fits(mesh, shape):
    nx, ny, nz = shape
    cx, cy, cz = mesh.shape["gx"], mesh.shape["gy"], mesh.shape["gz"]
    powers = cx & (cx - 1) == 0 and cy & (cy - 1) == 0 and cz == 2
    blocks = nx % (8 * cx) == 0 and ny % (16 * cy) == 0 and nz == 256
    return powers and blocks and (nx // 8) * (nz // 8) == 128 and nx * ny * nz <= 2**19


def per_block(mesh, *args):
    counts = (mesh.shape["gx"], mesh.shape["gy"], mesh.shape["gz"])
    whole = tuple(n * c for n, c in zip(args[0].shape, counts))
    return (per_device_small if fits(mesh, whole) else per_device)(*args)


def solution(mesh):
    return jax.shard_map(
        functools.partial(per_block, mesh),
        mesh=mesh,
        in_specs=(
            P("gx", "gy", "gz"),
            P("gx", "gy", "gz"),
            P("gx", "gy", "gz"),
            P("gx", "gy", "gz"),
        ),
        out_specs=P("gx", "gy", "gz"),
        check_vma=False,
    )
```

```python
import functools

import jax
import jax.numpy as jnp
from jax import lax
from jax.experimental import pallas as pl
from jax.experimental.pallas import tpu as pltpu
from jax.sharding import PartitionSpec as P

LEVELS = 4
COARSE_ITERS = 6


damping = 2.0 / 3.0

REACH = 3
TILE = 8
PARAMS = pltpu.CompilerParams(vmem_limit_bytes=16 * 2**20)


def up(v, axis):
    return pltpu.roll(v, v.shape[axis] - 1, axis)


def down(v, axis):
    return pltpu.roll(v, 1, axis)


def iota(shape, axis):
    return lax.broadcasted_iota(jnp.int32, shape, axis)


def chosen(mask):
    return jnp.where(mask, 1.0, 0.0).astype(jnp.bfloat16)


def select_dot(values, matrix):
    high = values.astype(jnp.bfloat16)
    rest = values - high.astype(jnp.float32)
    mid = rest.astype(jnp.bfloat16)
    low = (rest - mid.astype(jnp.float32)).astype(jnp.bfloat16)
    dot = functools.partial(jnp.dot, preferred_element_type=jnp.float32)
    return (dot(low, matrix) + dot(mid, matrix)) + dot(high, matrix)


def inverse(diagonal):
    return jnp.where(diagonal > 0.0, damping / jnp.where(diagonal > 0.0, diagonal, 1.0), 0.0)


def pack_kernel(own, x_out, y_out, c0_out, c1_out):
    nx, ny = own.shape[2], own.shape[3]
    gx, gy, gz = lax.axis_index("gx"), lax.axis_index("gy"), lax.axis_index("gz")

    def start(kind):
        return jnp.where((gx + kind) % 2 == 0, nx - 2, 0)

    ahead = (gy + gz) % 2 == 0

    def edge(h, a, i):
        return jnp.where(ahead, own[h, a, i, ny - 2 :, :], own[h, a, i, :2, :])

    for h in range(2):
        for a in range(4):
            for n in range(2):
                x_out[h, 2 * a + n] = own[h, a, start(gz) + n]
            for i in range(nx):
                y_out[h, (a * nx + i) * 2 : (a * nx + i) * 2 + 2] = edge(h, a, i)
            for n in range(2):
                for kind, out in enumerate((c0_out, c1_out)):
                    out[h, (2 * a + n) * 2 : (2 * a + n) * 2 + 2] = edge(h, a, start(kind) + n)
        x_out[h, 8] = own[h, 1, 2]
        for i in range(nx):
            y_out[h, 8 * nx + i : 8 * nx + i + 1] = own[h, 2, i, 2:3, :]


def fine_kernel(own, shared, t_out, k_out, m_out, ext, e1, rd, dg, e2, rows):
    nx, ny = own.shape[2], own.shape[3]
    nz = 2 * own.shape[4]
    half = own.shape[4]
    gx, gy, gz = lax.axis_index("gx"), lax.axis_index("gy"), lax.axis_index("gz")
    first = {
        "x": 0,
        "y": 2 * 9 * ny,
        "c": 2 * 9 * ny + 2 * 9 * nx,
    }
    for a in range(4):
        for p in range(nx + 2 * REACH):
            edge = p < REACH or p >= REACH + nx
            spans = [slice(0, ny + 2 * TILE)] if edge else [slice(0, TILE), slice(TILE + ny, ny + 2 * TILE)]
            for span in spans:
                ext[a, p, span] = jnp.zeros((span.stop - span.start, nz), jnp.float32)
    sides_x = (
        (REACH - 2, jnp.where(gx > 0, 1.0, 0.0), 1 - gx % 2),
        (REACH + nx, jnp.where(gx < lax.axis_size("gx") - 1, 1.0, 0.0), gx % 2),
    )
    sides_y = (
        (TILE - 2, jnp.where(gy > 0, 1.0, 0.0), 1 - gy % 2),
        (TILE + ny, jnp.where(gy < lax.axis_size("gy") - 1, 1.0, 0.0), gy % 2),
    )
    for h in range(2):
        z = slice(h * half, (h + 1) * half)
        for a in range(4):
            ext[a, REACH : REACH + nx, TILE : TILE + ny, z] = own[h, a]
        for p, keep, kind in sides_x:
            for n in range(9):
                a, l = (n // 2, n % 2) if n < 8 else (1, 2)
                at = first["x"] + (9 * h + n) * ny
                if n < 8 or p > REACH:
                    ext[a, p + l, TILE : TILE + ny, z] = keep * shared[kind, at : at + ny]
        for r, keep, kind in sides_y:
            for i in range(nx):
                for a in range(4):
                    at = first["y"] + 9 * nx * h + (a * nx + i) * 2
                    ext[a, REACH + i, r : r + 2, z] = keep * shared[kind, at : at + 2]
                if r > TILE:
                    at = first["y"] + 9 * nx * h + 8 * nx + i
                    ext[2, REACH + i, r + 2 : r + 3, z] = keep * shared[kind, at : at + 1]
        for p, keep_x, kind_x in sides_x:
            for r, keep_y, kind_y in sides_y:
                keep = keep_x * keep_y
                at = pl.multiple_of(first["c"] + 32 * kind_x + 16 * h, 8)
                lines = keep * shared[kind_y, pl.ds(at, 16)]
                for a in range(4):
                    for l in range(2):
                        n = (2 * a + l) * 2
                        ext[a, p + l, r : r + 2, z] = lines[n : n + 2]
    shape = (ny + 2 * TILE, nz)
    row, lane = iota(shape, 0), iota(shape, 1)
    inner_z = lane > 0
    in_y = jnp.logical_and(
        jnp.logical_or(gy > 0, row >= TILE),
        jnp.logical_or(gy < lax.axis_size("gy") - 1, row < TILE + ny),
    )

    def off(e, p):
        fy, fz = ext[2, p], jnp.where(inner_z, ext[3, p], 0.0)
        here = e[p]
        total = ext[1, p] * e[p - 1] + ext[1, p + 1] * e[p + 1]
        total = total + fy * down(here, 0) + up(fy * here, 0)
        return total + fz * down(here, 1) + up(fz * here, 1)

    for p in range(1, nx + 2 * REACH - 1):
        fy, fz = ext[2, p], ext[3, p]
        diagonal = ext[1, p] + ext[1, p + 1] + fy + up(fy, 0) + fz + up(jnp.where(inner_z, fz, 0.0), 1)
        inv = inverse(diagonal)
        dg[p], rd[p] = diagonal, inv
        e1[p] = ext[0, p] * inv
    for p in range(2, nx + 2 * REACH - 2):
        value = (2.0 - damping) * e1[p] + rd[p] * off(e1, p)
        inside = in_y
        if p < REACH:
            inside = jnp.logical_and(inside, gx > 0)
        if p >= REACH + nx:
            inside = jnp.logical_and(inside, gx < lax.axis_size("gx") - 1)
        e2[p] = jnp.where(inside, value, 0.0)

    def mine(v):
        v = v[TILE : TILE + ny]
        return jnp.where(gz == 0, v[:, :half], v[:, half:])

    sums = []
    for i in range(nx):
        p = REACH + i
        q = ext[0, p] - dg[p] * e2[p] + off(e2, p)
        fy, fz = ext[2, p], jnp.where(inner_z, ext[3, p], 0.0)
        inv = rd[p]
        t_out[i] = mine(e2[p] + inv * q)
        for n, k in enumerate((ext[1, p], ext[1, p + 1], fy, up(fy, 0), fz, up(fz, 1))):
            k_out[n, i] = mine(inv * k)
        sums.append(q[TILE : TILE + ny])
    inner = slice(TILE, TILE + ny)
    pairs = range(0, nx, 2)
    wide = [sums[i] + sums[i + 1] for i in pairs]
    wide += [0.5 * ext[1, REACH + i, inner] for i in pairs]
    wide += [0.5 * (ext[2, REACH + i, inner] + ext[2, REACH + i + 1, inner]) for i in pairs]
    thin = [0.5 * (ext[3, REACH + i, inner] + ext[3, REACH + i + 1, inner]) for i in pairs]
    fine, coarse = iota((nz, half), 0), iota((nz, half), 1)
    summed = select_dot(jnp.concatenate(wide, 0), chosen(fine // 2 == coarse))
    picked = select_dot(jnp.concatenate(thin, 0), chosen(fine == 2 * coarse))
    count = len(pairs) * ny
    rows[: 3 * count] = summed
    rows[3 * count :] = picked
    part = count // 2
    even = rows[pl.ds(0, 4 * part, stride=2)]
    odd = rows[pl.ds(1, 4 * part, stride=2)]
    kept = [even[:part] + odd[:part], even[part : 2 * part] + odd[part : 2 * part]]
    kept += [even[2 * part : 3 * part], even[3 * part :] + odd[3 * part :]]
    for a in range(2):
        m_out[a] = jnp.where(gz == 0, kept[a], kept[2 + a]).reshape(m_out.shape[1:])


def planes_of(ref):
    return [ref[p] for p in range(ref.shape[0])]


def level_parts(fx, fy, fz):
    shape = fy[0].shape
    row, lane = iota(shape, 0), iota(shape, 1)
    n = len(fx)
    zero = jnp.zeros(shape, jnp.float32)
    fym = [jnp.where(row > 0, v, 0.0) for v in fy]
    fzm = [jnp.where(lane > 0, v, 0.0) for v in fz]
    high = [fx[p + 1] if p + 1 < n else zero for p in range(n)]
    diagonal = [fx[p] + high[p] + fy[p] + up(fym[p], 0) + fz[p] + up(fzm[p], 1) for p in range(n)]

    def off(e):
        result = []
        for p in range(n):
            total = fym[p] * down(e[p], 0) + up(fym[p] * e[p], 0)
            total = total + fzm[p] * down(e[p], 1) + up(fzm[p] * e[p], 1)
            if p > 0:
                total = total + fx[p] * e[p - 1]
            if p + 1 < n:
                total = total + fx[p + 1] * e[p + 1]
            result.append(total)
        return result

    return diagonal, [inverse(d) for d in diagonal], off


def before(b, diagonal, inv, off):
    e1 = [v * r for v, r in zip(b, inv)]
    e2 = [(2.0 - damping) * e + r * o for e, r, o in zip(e1, inv, off(e1))]
    q = [v - d * e + o for v, d, e, o in zip(b, diagonal, e2, off(e2))]
    return [e + r * v for e, r, v in zip(e2, inv, q)], q


def after(t, c, inv, off):
    return [v + (1.0 - damping) * k + r * o for v, k, r, o in zip(t, c, inv, off(c))]


def coarse_solution(rhs, fx, fy, fz, depth):
    shape = rhs.shape
    row, lane = iota(shape, 0), iota(shape, 1)
    fxm = jnp.where(lane >= depth, fx, 0.0)
    fym = jnp.where(row > 0, fy, 0.0)
    fzm = jnp.where(lane % depth > 0, fz, 0.0)
    wide = shape[1]

    def up_x(v):
        return pltpu.roll(v, wide - depth, 1)

    hx, hy, hz = up_x(fxm), up(fym, 0), up(fzm, 1)
    diagonal = fx + hx + fy + hy + fz + hz

    def operate_packed(v):
        result = diagonal * v - fxm * pltpu.roll(v, depth, 1) - hx * up_x(v)
        result = result - fym * down(v, 0) - hy * up(v, 0)
        return result - fzm * down(v, 1) - hz * up(v, 1)

    def total(v):
        return jnp.sum(jnp.sum(v, axis=0, keepdims=True), axis=1, keepdims=True)

    solution = jnp.zeros_like(rhs)
    remain = rhs
    search = rhs
    norm_now = total(remain * remain)
    for step in range(COARSE_ITERS):
        image = operate_packed(search)
        alpha = norm_now / total(search * image)
        solution = solution + alpha * search
        if step + 1 < COARSE_ITERS:
            remain = remain - alpha * image
            norm_next = total(remain * remain)
            search = remain + norm_next / norm_now * search
            norm_now = norm_next
    return solution


def whole_kernel(here, there, t_in, k_in, out, grid, fold1, fold2, spread2, window, doubled):
    gx, gy, gz = lax.axis_index("gx"), lax.axis_index("gy"), lax.axis_index("gz")
    cx, cy = lax.axis_size("gx"), lax.axis_size("gy")
    bx, by = here.shape[2], here.shape[3]
    for k in range(cx * cy):
        x = jnp.bitwise_xor(gx, k % cx) * bx
        y = pl.multiple_of(jnp.bitwise_xor(gy, k // cx) * by, by)
        for a in range(2):
            grid[2 * gz + a, pl.ds(x, bx), pl.ds(y, by), :] = here[k, a]
            grid[2 * (1 - gz) + a, pl.ds(x, bx), pl.ds(y, by), :] = there[k, a]
    n1, m1, w1 = grid.shape[1:]
    b1, fx1, fy1, fz1 = (planes_of(grid.at[a]) for a in range(4))
    diagonal1, inv1, off1 = level_parts(fx1, fy1, fz1)
    t1, q1 = before(b1, diagonal1, inv1, off1)

    n2, m2 = n1 // 2, m1 // 2
    fine, coarse = iota((w1, w1), 0), iota((w1, w1), 1)
    both, even = chosen(fine // 2 == coarse), chosen(fine == 2 * coarse)
    pairs = range(0, n1, 2)
    wide = [q1[i] + q1[i + 1] for i in pairs] + [0.5 * fx1[i] for i in pairs]
    wide += [0.5 * (fy1[i] + fy1[i + 1]) for i in pairs]
    thin = [0.5 * (fz1[i] + fz1[i + 1]) for i in pairs]
    count = n2 * m1
    fold1[: 3 * count] = select_dot(jnp.concatenate(wide, 0), both)
    fold1[3 * count :] = select_dot(jnp.concatenate(thin, 0), even)
    half = n2 * m2
    low = fold1[pl.ds(0, 4 * half, stride=2)]
    top = fold1[pl.ds(1, 4 * half, stride=2)]

    def part(v):
        return [v[p * m2 : (p + 1) * m2] for p in range(n2)]

    b2 = part(low[:half] + top[:half])
    fx2 = part(low[half : 2 * half] + top[half : 2 * half])
    fy2 = part(low[2 * half : 3 * half])
    fz2 = part(low[3 * half :] + top[3 * half :])
    diagonal2, inv2, off2 = level_parts(fx2, fy2, fz2)
    t2, q2 = before(b2, diagonal2, inv2, off2)

    n3, m3 = n2 // 2, m2 // 2
    depth = w1 // n3
    packed = [0.0, 0.0, 0.0, 0.0]
    for i in range(n3):
        both = chosen((fine // 2 + i * depth == coarse) & (fine < 2 * depth))
        even = chosen((fine + 2 * i * depth == 2 * coarse) & (fine < 2 * depth))
        wide = [q2[2 * i] + q2[2 * i + 1], 0.5 * fx2[2 * i], 0.5 * (fy2[2 * i] + fy2[2 * i + 1])]
        thin = 0.5 * (fz2[2 * i] + fz2[2 * i + 1])
        summed = select_dot(jnp.concatenate(wide, 0), both)
        packed[0] = packed[0] + summed[:m2]
        packed[1] = packed[1] + summed[m2 : 2 * m2]
        packed[2] = packed[2] + summed[2 * m2 :]
        packed[3] = packed[3] + select_dot(thin, even)
    fold2[...] = jnp.concatenate(packed, 0)
    low = fold2[pl.ds(0, 4 * m3, stride=2)]
    top = fold2[pl.ds(1, 4 * m3, stride=2)]
    b3, fx3 = low[:m3] + top[:m3], low[m3 : 2 * m3] + top[m3 : 2 * m3]
    fy3, fz3 = low[2 * m3 : 3 * m3], low[3 * m3 :] + top[3 * m3 :]
    c3 = coarse_solution(b3, fx3, fy3, fz3, depth)

    for i in range(n3):
        row = select_dot(c3, chosen((coarse // 2 + i * depth == fine) & (coarse < 2 * depth)))
        spread2[pl.ds(i * m2, m3, stride=2)] = row
        spread2[pl.ds(i * m2 + 1, m3, stride=2)] = row
    up2 = [spread2[(p // 2) * m2 : (p // 2 + 1) * m2] for p in range(n2)]
    c2 = after(t2, up2, inv2, off2)

    row = select_dot(jnp.concatenate(c2, 0), chosen(coarse // 2 == fine))
    fold1[pl.ds(0, half, stride=2)] = row
    fold1[pl.ds(1, half, stride=2)] = row
    up1 = [fold1[(p // 2) * m1 : (p // 2 + 1) * m1] for p in range(n1)]
    c1 = after(t1, up1, inv1, off1)

    window[...] = jnp.zeros_like(window)
    for p in range(n1):
        window[1 + p, TILE : TILE + m1, :] = c1[p]
    y = pl.multiple_of(gy * by, by)
    near = window[pl.ds(gx * bx, bx + 2), pl.ds(y, by + 2 * TILE), :]
    tall = by + 2 * TILE
    near = near.reshape((bx + 2) * tall, w1)
    spot = gz * t_in.shape[2] + iota((w1, 3 * w1), 1) % w1 + (iota((w1, 3 * w1), 1) // w1 + 1) % 3 - 1
    wanted = iota((w1, 3 * w1), 0)
    row = select_dot(near, chosen((2 * wanted == spot) | (2 * wanted + 1 == spot)))
    for s in range(3):
        doubled[s, pl.ds(0, (bx + 2) * tall, stride=2)] = row[:, s * w1 : (s + 1) * w1]
        doubled[s, pl.ds(1, (bx + 2) * tall, stride=2)] = row[:, s * w1 : (s + 1) * w1]
    ny = t_in.shape[1]

    def at(s, i, shift):
        first = (1 + i // 2) * 2 * tall + 2 * TILE + shift
        return doubled[s, first : first + ny]

    for i in range(t_in.shape[0]):
        value = t_in[i] + (1.0 - damping) * at(0, i, 0)
        value = value + k_in[0, i] * at(0, i - 1, 0) + k_in[1, i] * at(0, i + 1, 0)
        value = value + k_in[2, i] * at(0, i, -1) + k_in[3, i] * at(0, i, 1)
        out[i] = value + k_in[4, i] * at(2, i, 0) + k_in[5, i] * at(1, i, 0)


def pair(i, kind, count):
    return i ^ 1 if kind == 0 else (i + 1 if i % 2 else i - 1) % count


def swap(block, to):
    cx, cy, cz = (lax.axis_size(axis) for axis in ("gx", "gy", "gz"))
    route = []
    for i in range(cx):
        for j in range(cy):
            for c in range(cz):
                x, y, z = to(i, j, c)
                route.append(((i * cy + j) * cz + c, (x * cy + y) * cz + z))
    return lax.ppermute(block, ("gx", "gy", "gz"), route)


def gathered(block, axis):
    count = lax.axis_size(axis)
    parts = [lax.ppermute(block, axis, [(i, i ^ k) for i in range(count)]) for k in range(1, count)]
    return jnp.concatenate([block] + parts, 0)


def f32(*shape):
    return jax.ShapeDtypeStruct(shape, jnp.float32)


def per_device_small(adjoint_residual, face_x, face_y, face_z):
    nx, ny, nz = adjoint_residual.shape
    stacked = jnp.stack((adjoint_residual, face_x, face_y, face_z))
    own = lax.all_gather(stacked, "gz", axis=0)
    cx, cy = lax.axis_size("gx"), lax.axis_size("gy")
    packed = pl.pallas_call(
        pack_kernel,
        out_shape=(f32(2, 9, ny, nz), f32(2, 9 * nx, nz), f32(2, 16, nz), f32(2, 16, nz)),
        compiler_params=PARAMS,
        name="pack",
    )(own)
    routes = (
        lambda i, j, c: (pair(i, c, cx), j, c),
        lambda i, j, c: (i, pair(j, c, cy), c),
        lambda i, j, c: (pair(i, 0, cx), pair(j, c, cy), c),
        lambda i, j, c: (pair(i, 1, cx), pair(j, c, cy), c),
    )
    taken = [swap(block.reshape(-1, nz), route) for block, route in zip(packed, routes)]
    shared = lax.all_gather(jnp.concatenate(taken, 0), "gz", axis=0)
    ext_x, ext_y, wide = nx + 2 * REACH, ny + 2 * TILE, 2 * nz
    field = pltpu.VMEM((ext_x, ext_y, wide), jnp.float32)
    t, k, m = pl.pallas_call(
        fine_kernel,
        out_shape=(f32(nx, ny, nz), f32(6, nx, ny, nz), f32(2, nx // 2, ny // 2, nz)),
        scratch_shapes=[
            pltpu.VMEM((4, ext_x, ext_y, wide), jnp.float32),
            field,
            field,
            field,
            field,
            pltpu.VMEM((2 * nx * ny, nz), jnp.float32),
        ],
        compiler_params=PARAMS,
        name="fine",
    )(own, shared)
    here = gathered(gathered(m[None], "gx"), "gy")
    there = lax.ppermute(here, "gz", [(0, 1), (1, 0)])
    n1, m1 = here.shape[2] * lax.axis_size("gx"), here.shape[3] * lax.axis_size("gy")
    tall = (nx // 2 + 2) * (ny // 2 + 2 * TILE)
    return pl.pallas_call(
        whole_kernel,
        out_shape=f32(nx, ny, nz),
        scratch_shapes=[
            pltpu.VMEM((4, n1, m1, nz), jnp.float32),
            pltpu.VMEM((2 * n1 * m1, nz), jnp.float32),
            pltpu.VMEM((2 * m1, nz), jnp.float32),
            pltpu.VMEM((n1 * m1 // 8, nz), jnp.float32),
            pltpu.VMEM((n1 + 2, m1 + 2 * TILE, nz), jnp.float32),
            pltpu.VMEM((3, 2 * tall, nz), jnp.float32),
        ],
        compiler_params=PARAMS,
        name="whole",
    )(here, there, t, k)


def extended(block, sides, width):
    for axis, dim in sides:
        count = lax.axis_size(axis)
        forward = [(i, i + 1) for i in range(count - 1)]
        backward = [(target, source) for source, target in forward]
        low = lax.ppermute(
            lax.slice_in_dim(block, block.shape[dim] - width, None, axis=dim), axis, forward
        )
        high = lax.ppermute(lax.slice_in_dim(block, 0, width, axis=dim), axis, backward)
        block = jnp.concatenate([low, block, high], axis=dim)
    return block


def from_behind(block, axis, distance):
    devices = range(lax.axis_size(axis))
    route = [(i - distance, i) for i in devices if i - distance in devices]
    return lax.ppermute(block, axis, route)


def stencil(padded, field, coefs):
    low_x, high_x, low_y, high_y, low_z, high_z = coefs
    diagonal = low_x + high_x + low_y + high_y + low_z + high_z
    result = diagonal * field - low_x * padded[:-2, 1:-1, 1:-1] - high_x * padded[2:, 1:-1, 1:-1]
    result = result - low_y * padded[1:-1, :-2, 1:-1] - high_y * padded[1:-1, 2:, 1:-1]
    return result - low_z * padded[1:-1, 1:-1, :-2] - high_z * padded[1:-1, 1:-1, 2:]


def operate(field, coefs):
    padded = extended(field, (("gx", 0), ("gy", 1), ("gz", 2)), 1)
    return stencil(padded, field, coefs)


def operate_whole(field, coefs):
    return stencil(jnp.pad(field, 1), field, coefs)


def blocked(values):
    return values.reshape(values.shape[0] // 2, 2, values.shape[1] // 2, 2, values.shape[2] // 2, 2)


def coarse_face(values, dim, parity):
    others = tuple((2 * k + 1 for k in range(3) if k != dim))
    summed = jnp.sum(blocked(values), axis=others)
    return 0.5 * lax.index_in_dim(summed, parity, dim + 1, keepdims=False)


def coarsen(coefs):
    result = []
    for dim in range(3):
        result.append(coarse_face(coefs[2 * dim], dim, 0))
        result.append(coarse_face(coefs[2 * dim + 1], dim, 1))
    return tuple(result)


def restrict(values):
    return jnp.sum(blocked(values), axis=(1, 3, 5))


def prolong(values):
    shape_out = (values.shape[0] * 2, values.shape[1] * 2, values.shape[2] * 2)
    wide = jnp.broadcast_to(
        values[:, None, :, None, :, None],
        (values.shape[0], 2, values.shape[1], 2, values.shape[2], 2),
    )
    return wide.reshape(shape_out)


def total_local(value):
    return value


def conj_grad(rhs, coefs, apply_op, total):
    solution = jnp.zeros_like(rhs)
    remain = rhs
    search = rhs
    norm_now = total(jnp.sum(remain * remain))
    for step in range(COARSE_ITERS):
        image = apply_op(search, coefs)
        alpha = norm_now / total(jnp.sum(search * image))
        solution = solution + alpha * search
        remain = remain - alpha * image
        norm_next = total(jnp.sum(remain * remain))
        search = remain + norm_next / norm_now * search
        norm_now = norm_next
    return solution


def coarse_solve(rhs, coefs):
    part_x, part_y, part_z = rhs.shape
    count_x = lax.axis_size("gx")
    count_y = lax.axis_size("gy")
    count_z = lax.axis_size("gz")
    stacked = jnp.stack((rhs,) + coefs)[None]
    whole = lax.all_gather(stacked, ("gx", "gy", "gz"), axis=0, tiled=True)
    whole = whole.reshape(count_x, count_y, count_z, 7, part_x, part_y, part_z)
    whole = whole.transpose(3, 0, 4, 1, 5, 2, 6).reshape(
        7, count_x * part_x, count_y * part_y, count_z * part_z
    )
    whole_coefs = tuple((whole[k] for k in range(1, 7)))
    solution = conj_grad(whole[0], whole_coefs, operate_whole, total_local)
    starts = (
        lax.axis_index("gx") * part_x,
        lax.axis_index("gy") * part_y,
        lax.axis_index("gz") * part_z,
    )
    return lax.dynamic_slice(solution, starts, (part_x, part_y, part_z))


def cycle(rhs, levels_left, coefs):
    if levels_left == 1:
        return coarse_solve(rhs, coefs)
    diagonal = coefs[0] + coefs[1] + coefs[2] + coefs[3] + coefs[4] + coefs[5]
    field = damping * rhs / diagonal
    field = field + damping * (rhs - operate(field, coefs)) / diagonal
    remain = rhs - operate(field, coefs)
    field = field + prolong(cycle(restrict(remain), levels_left - 1, coarsen(coefs)))
    field = field + damping * (rhs - operate(field, coefs)) / diagonal
    return field


def per_device(adjoint_residual, face_x, face_y, face_z):
    rim_x = from_behind(face_x[:1], "gx", -1)
    rim_y = from_behind(face_y[:, :1], "gy", -1)
    rim_z = from_behind(face_z[:, :, :1], "gz", -1)
    high_x = jnp.concatenate([face_x[1:], rim_x], 0)
    high_y = jnp.concatenate([face_y[:, 1:], rim_y], 1)
    high_z = jnp.concatenate([face_z[:, :, 1:], rim_z], 2)
    coefs = (face_x, high_x, face_y, high_y, face_z, high_z)
    return cycle(adjoint_residual, LEVELS, coefs)


def fits(mesh, shape):
    nx, ny, nz = shape
    cx, cy, cz = mesh.shape["gx"], mesh.shape["gy"], mesh.shape["gz"]
    powers = cx & (cx - 1) == 0 and cy & (cy - 1) == 0 and cz == 2
    blocks = nx % (8 * cx) == 0 and ny % (16 * cy) == 0 and nz == 256
    return powers and blocks and (nx // 8) * (nz // 8) == 128 and nx * ny * nz <= 2**19


def per_block(mesh, *args):
    counts = (mesh.shape["gx"], mesh.shape["gy"], mesh.shape["gz"])
    whole = tuple(n * c for n, c in zip(args[0].shape, counts))
    return (per_device_small if fits(mesh, whole) else per_device)(*args)


def solution(mesh):
    return jax.shard_map(
        functools.partial(per_block, mesh),
        mesh=mesh,
        in_specs=(
            P("gx", "gy", "gz"),
            P("gx", "gy", "gz"),
            P("gx", "gy", "gz"),
            P("gx", "gy", "gz"),
        ),
        out_specs=P("gx", "gy", "gz"),
        check_vma=False,
    )
```

```python
import functools

import jax
import jax.numpy as jnp
from jax import lax
from jax.experimental import pallas as pl
from jax.experimental.pallas import tpu as pltpu
from jax.sharding import PartitionSpec as P

LEVELS = 4
COARSE_ITERS = 6


damping = 2.0 / 3.0

REACH = 3
TILE = 8
PARAMS = pltpu.CompilerParams(vmem_limit_bytes=16 * 2**20)


def up(v, axis):
    return pltpu.roll(v, v.shape[axis] - 1, axis)


def down(v, axis):
    return pltpu.roll(v, 1, axis)


def iota(shape, axis):
    return lax.broadcasted_iota(jnp.int32, shape, axis)


def chosen(mask):
    return jnp.where(mask, 1.0, 0.0).astype(jnp.bfloat16)


def select_dot(values, matrix):
    high = values.astype(jnp.bfloat16)
    rest = values - high.astype(jnp.float32)
    mid = rest.astype(jnp.bfloat16)
    low = (rest - mid.astype(jnp.float32)).astype(jnp.bfloat16)
    dot = functools.partial(jnp.dot, preferred_element_type=jnp.float32)
    return (dot(low, matrix) + dot(mid, matrix)) + dot(high, matrix)


def inverse(diagonal):
    return jnp.where(diagonal > 0.0, damping / jnp.where(diagonal > 0.0, diagonal, 1.0), 0.0)


def side(axis):
    here = lax.axis_index(axis)
    first = jnp.where(here > 0, 1.0, 0.0)
    last = jnp.where(here < lax.axis_size(axis) - 1, 1.0, 0.0)
    return (here % 2 == 1, first), (here % 2 == 0, last)


def x_kernel(own, *slabs):
    nx, gx = own.shape[1], lax.axis_index("gx")
    for kind, out in enumerate(slabs):
        start = jnp.where((gx + kind) % 2 == 0, nx - 2, 0)
        for a in range(4):
            for n in range(2):
                out[2 * a + n] = own[a, start + n]
        out[8] = own[1, 2]


def sides_x(slabs, before, behind):
    for (even, keep), out in zip(side("gx"), (before, behind)):
        for n in range(9):
            out[n] = keep * jnp.where(even, slabs[0][n], slabs[1][n])


def y_kernel(own, s0, s1, o0, o1, before, behind):
    nx, ny = own.shape[1], own.shape[2]
    gy = lax.axis_index("gy")
    sides_x((s0, s1), before, behind)
    for kind, out in enumerate((o0, o1)):
        ahead = (gy + kind) % 2 == 0
        for p in range(nx + 4):
            for a in range(4):
                if p < 2:
                    v = before[2 * a + p]
                elif p < nx + 2:
                    v = own[a, p - 2]
                else:
                    v = behind[2 * a + p - nx - 2]
                at = (a * (nx + 4) + p) * 2
                out[at : at + 2] = jnp.where(ahead, v[ny - 2 :], v[:2])
                if a == 2:
                    out[8 * (nx + 4) + p : 8 * (nx + 4) + p + 1] = v[2:3]
        used = 9 * (nx + 4)
        out[used:] = jnp.zeros((out.shape[0] - used, out.shape[1]), jnp.float32)


def z_kernel(own, s0, s1, o0, o1, ext, edge, before, behind, lines):
    nx, ny, nz = own.shape[1:]
    gz = lax.axis_index("gz")
    sides_x((s0, s1), before, behind)
    zero = jnp.zeros((TILE, nz), jnp.float32)
    empty = jnp.zeros((ny + 2 * TILE, nz), jnp.float32)
    for a in range(4):
        for p in range(nx + 2 * REACH):
            q = p - REACH
            if 0 <= q < nx:
                v = own[a, q]
            elif -2 <= q < 0:
                v = before[2 * a + q + 2]
            elif nx <= q < nx + 2:
                v = behind[2 * a + q - nx]
            elif q == nx + 2 and a == 1:
                v = behind[8]
            else:
                ext[a, p] = empty
                continue
            ext[a, p, :TILE] = zero
            ext[a, p, TILE + ny :] = zero
            ext[a, p, TILE : TILE + ny] = v
    for (even, keep), r in zip(side("gy"), (TILE - 2, TILE + ny)):
        lines[...] = keep * jnp.where(even, o0[...], o1[...])
        for p in range(nx + 4):
            for a in range(4):
                at = (a * (nx + 4) + p) * 2
                ext[a, 1 + p, r : r + 2] = lines[at : at + 2]
            if r > TILE:
                at = 8 * (nx + 4) + p
                ext[2, 1 + p, r + 2 : r + 3] = lines[at : at + 1]
    lane = iota((ny + 2 * TILE, nz), 1)
    for p in range(nx + 4):
        packed = ext[0, 1 + p]
        for a in range(1, 4):
            first = jnp.where(gz == 0, nz - 3 - 3 * a, 3 * a)
            moved = pltpu.roll(ext[a, 1 + p], jnp.where(gz == 0, nz - 3 * a, 3 * a), 1)
            packed = jnp.where((lane >= first) & (lane < first + 3), moved, packed)
        edge[p] = packed


def fine_kernel(local, edges, t_out, k_out, m_out, ext, e1, rd, dg, e2, rows):
    nx, ny, half = t_out.shape
    nz = 2 * half
    gx, gy, gz = lax.axis_index("gx"), lax.axis_index("gy"), lax.axis_index("gz")
    spot = iota((ny + 2 * TILE, half), 1)
    given = jnp.logical_or((gz == 0) & (spot < 3), (gz == 1) & (spot >= half - 3))
    for p in range(nx + 2 * REACH):
        for a in range(4):
            ext[a, p, :, :half] = local[a, p]
            if 1 <= p < nx + 5:
                v = edges[1 - gz, p - 1]
                if a > 0:
                    v = pltpu.roll(v, jnp.where(gz == 0, half - 3 * a, 3 * a), 1)
                ext[a, p, :, half:] = jnp.where(given, v, 0.0)
            else:
                ext[a, p, :, half:] = jnp.zeros((ny + 2 * TILE, half), jnp.float32)
    shape = (ny + 2 * TILE, nz)
    row, lane = iota(shape, 0), iota(shape, 1)
    inner_z = jnp.logical_or(lane > 0, gz > 0)
    in_y = jnp.logical_and(
        jnp.logical_or(gy > 0, row >= TILE),
        jnp.logical_or(gy < lax.axis_size("gy") - 1, row < TILE + ny),
    )

    def off(e, p):
        fy, fz = ext[2, p], jnp.where(inner_z, ext[3, p], 0.0)
        here = e[p]
        total = ext[1, p] * e[p - 1] + ext[1, p + 1] * e[p + 1]
        total = total + fy * down(here, 0) + up(fy * here, 0)
        return total + fz * down(here, 1) + up(fz * here, 1)

    for p in range(1, nx + 2 * REACH - 1):
        fy, fz = ext[2, p], ext[3, p]
        diagonal = ext[1, p] + ext[1, p + 1] + fy + up(fy, 0) + fz + up(jnp.where(inner_z, fz, 0.0), 1)
        inv = inverse(diagonal)
        dg[p], rd[p] = diagonal, inv
        e1[p] = ext[0, p] * inv
    for p in range(2, nx + 2 * REACH - 2):
        value = (2.0 - damping) * e1[p] + rd[p] * off(e1, p)
        inside = in_y
        if p < REACH:
            inside = jnp.logical_and(inside, gx > 0)
        if p >= REACH + nx:
            inside = jnp.logical_and(inside, gx < lax.axis_size("gx") - 1)
        e2[p] = jnp.where(inside, value, 0.0)

    def mine(v):
        return v[TILE : TILE + ny, :half]

    sums = []
    for i in range(nx):
        p = REACH + i
        q = ext[0, p] - dg[p] * e2[p] + off(e2, p)
        fy, fz = ext[2, p], jnp.where(inner_z, ext[3, p], 0.0)
        inv = rd[p]
        t_out[i] = mine(e2[p] + inv * q)
        for n, k in enumerate((ext[1, p], ext[1, p + 1], fy, up(fy, 0), fz, up(fz, 1))):
            k_out[n, i] = mine(inv * k)
        sums.append(mine(q))
    def face(d, i):
        return 0.5 * ext[d, REACH + i, TILE : TILE + ny, :half]

    pairs = range(0, nx, 2)
    fine, coarse = iota((half, half), 0), iota((half, half), 1)
    both_low, both_high = chosen(fine // 2 == coarse), chosen(fine // 2 + half // 2 == coarse)
    even_high = chosen(fine + half == 2 * coarse)
    count = len(pairs) * ny
    rows[:count] = select_dot(jnp.concatenate([sums[i] + sums[i + 1] for i in pairs], 0), both_low) + select_dot(
        jnp.concatenate([face(1, i) for i in pairs], 0), both_high
    )
    rows[count:] = select_dot(jnp.concatenate([face(2, i) + face(2, i + 1) for i in pairs], 0), both_low) + select_dot(
        jnp.concatenate([face(3, i) + face(3, i + 1) for i in pairs], 0), even_high
    )
    part = count // 2
    even = rows[pl.ds(0, 2 * part, stride=2)]
    odd = rows[pl.ds(1, 2 * part, stride=2)]
    spot = iota((part, half), 1)
    m_out[0] = (even[:part] + odd[:part]).reshape(m_out.shape[1:])
    m_out[1] = (even[part:] + jnp.where(spot < half // 2, 0.0, odd[part:])).reshape(m_out.shape[1:])


def planes_of(ref):
    return [ref[p] for p in range(ref.shape[0])]


def level_parts(fx, fy, fz):
    shape = fy[0].shape
    row, lane = iota(shape, 0), iota(shape, 1)
    n = len(fx)
    zero = jnp.zeros(shape, jnp.float32)
    fym = [jnp.where(row > 0, v, 0.0) for v in fy]
    fzm = [jnp.where(lane > 0, v, 0.0) for v in fz]
    high = [fx[p + 1] if p + 1 < n else zero for p in range(n)]
    diagonal = [fx[p] + high[p] + fy[p] + up(fym[p], 0) + fz[p] + up(fzm[p], 1) for p in range(n)]

    def off(e):
        result = []
        for p in range(n):
            total = fym[p] * down(e[p], 0) + up(fym[p] * e[p], 0)
            total = total + fzm[p] * down(e[p], 1) + up(fzm[p] * e[p], 1)
            if p > 0:
                total = total + fx[p] * e[p - 1]
            if p + 1 < n:
                total = total + fx[p + 1] * e[p + 1]
            result.append(total)
        return result

    return diagonal, [inverse(d) for d in diagonal], off


def before(b, diagonal, inv, off):
    e1 = [v * r for v, r in zip(b, inv)]
    e2 = [(2.0 - damping) * e + r * o for e, r, o in zip(e1, inv, off(e1))]
    q = [v - d * e + o for v, d, e, o in zip(b, diagonal, e2, off(e2))]
    return [e + r * v for e, r, v in zip(e2, inv, q)], q


def after(t, c, inv, off):
    return [v + (1.0 - damping) * k + r * o for v, k, r, o in zip(t, c, inv, off(c))]


def coarse_solution(rhs, fx, fy, fz, depth):
    shape = rhs.shape
    row, lane = iota(shape, 0), iota(shape, 1)
    fxm = jnp.where(lane >= depth, fx, 0.0)
    fym = jnp.where(row > 0, fy, 0.0)
    fzm = jnp.where(lane % depth > 0, fz, 0.0)
    wide = shape[1]

    def up_x(v):
        return pltpu.roll(v, wide - depth, 1)

    hx, hy, hz = up_x(fxm), up(fym, 0), up(fzm, 1)
    diagonal = fx + hx + fy + hy + fz + hz

    def operate_packed(v):
        result = diagonal * v - fxm * pltpu.roll(v, depth, 1) - hx * up_x(v)
        result = result - fym * down(v, 0) - hy * up(v, 0)
        return result - fzm * down(v, 1) - hz * up(v, 1)

    def total(v):
        return jnp.sum(jnp.sum(v, axis=0, keepdims=True), axis=1, keepdims=True)

    solution = jnp.zeros_like(rhs)
    remain = rhs
    search = rhs
    norm_now = total(remain * remain)
    for step in range(COARSE_ITERS):
        image = operate_packed(search)
        alpha = norm_now / total(search * image)
        solution = solution + alpha * search
        if step + 1 < COARSE_ITERS:
            remain = remain - alpha * image
            norm_next = total(remain * remain)
            search = remain + norm_next / norm_now * search
            norm_now = norm_next
    return solution


def whole_kernel(here, there, t_in, k_in, out, grid, fold1, fold2, spread2, window, doubled):
    gx, gy, gz = lax.axis_index("gx"), lax.axis_index("gy"), lax.axis_index("gz")
    cx, cy = lax.axis_size("gx"), lax.axis_size("gy")
    bx, by = here.shape[2], here.shape[3]
    w1 = here.shape[4]
    for k in range(cx * cy):
        x = jnp.bitwise_xor(gx, k % cx) * bx
        y = pl.multiple_of(jnp.bitwise_xor(gy, k // cx) * by, by)
        for a in range(2):
            low = jnp.where(gz == 0, here[k, a], there[k, a]).reshape(bx * by, w1)
            top = jnp.where(gz == 0, there[k, a], here[k, a]).reshape(bx * by, w1)
            left = iota((bx * by, w1), 1) < w1 // 2
            one = jnp.where(left, low, pltpu.roll(top, w1 // 2, 1))
            two = jnp.where(left, pltpu.roll(low, w1 // 2, 1), top)
            grid[2 * a, pl.ds(x, bx), pl.ds(y, by), :] = one.reshape(bx, by, w1)
            grid[2 * a + 1, pl.ds(x, bx), pl.ds(y, by), :] = two.reshape(bx, by, w1)
    n1, m1, w1 = grid.shape[1:]
    b1, fx1, fy1, fz1 = (planes_of(grid.at[a]) for a in range(4))
    diagonal1, inv1, off1 = level_parts(fx1, fy1, fz1)
    t1, q1 = before(b1, diagonal1, inv1, off1)

    n2, m2 = n1 // 2, m1 // 2
    fine, coarse = iota((w1, w1), 0), iota((w1, w1), 1)
    both, even = chosen(fine // 2 == coarse), chosen(fine == 2 * coarse)
    pairs = range(0, n1, 2)
    wide = [q1[i] + q1[i + 1] for i in pairs] + [0.5 * fx1[i] for i in pairs]
    wide += [0.5 * (fy1[i] + fy1[i + 1]) for i in pairs]
    thin = [0.5 * (fz1[i] + fz1[i + 1]) for i in pairs]
    count = n2 * m1
    fold1[: 3 * count] = select_dot(jnp.concatenate(wide, 0), both)
    fold1[3 * count :] = select_dot(jnp.concatenate(thin, 0), even)
    half = n2 * m2
    low = fold1[pl.ds(0, 4 * half, stride=2)]
    top = fold1[pl.ds(1, 4 * half, stride=2)]

    def part(v):
        return [v[p * m2 : (p + 1) * m2] for p in range(n2)]

    b2 = part(low[:half] + top[:half])
    fx2 = part(low[half : 2 * half] + top[half : 2 * half])
    fy2 = part(low[2 * half : 3 * half])
    fz2 = part(low[3 * half :] + top[3 * half :])
    diagonal2, inv2, off2 = level_parts(fx2, fy2, fz2)
    t2, q2 = before(b2, diagonal2, inv2, off2)

    n3, m3 = n2 // 2, m2 // 2
    depth = w1 // n3
    packed = [0.0, 0.0, 0.0, 0.0]
    for i in range(n3):
        both = chosen((fine // 2 + i * depth == coarse) & (fine < 2 * depth))
        even = chosen((fine + 2 * i * depth == 2 * coarse) & (fine < 2 * depth))
        wide = [q2[2 * i] + q2[2 * i + 1], 0.5 * fx2[2 * i], 0.5 * (fy2[2 * i] + fy2[2 * i + 1])]
        thin = 0.5 * (fz2[2 * i] + fz2[2 * i + 1])
        summed = select_dot(jnp.concatenate(wide, 0), both)
        packed[0] = packed[0] + summed[:m2]
        packed[1] = packed[1] + summed[m2 : 2 * m2]
        packed[2] = packed[2] + summed[2 * m2 :]
        packed[3] = packed[3] + select_dot(thin, even)
    fold2[...] = jnp.concatenate(packed, 0)
    low = fold2[pl.ds(0, 4 * m3, stride=2)]
    top = fold2[pl.ds(1, 4 * m3, stride=2)]
    b3, fx3 = low[:m3] + top[:m3], low[m3 : 2 * m3] + top[m3 : 2 * m3]
    fy3, fz3 = low[2 * m3 : 3 * m3], low[3 * m3 :] + top[3 * m3 :]
    c3 = coarse_solution(b3, fx3, fy3, fz3, depth)

    for i in range(n3):
        row = select_dot(c3, chosen((coarse // 2 + i * depth == fine) & (coarse < 2 * depth)))
        spread2[pl.ds(i * m2, m3, stride=2)] = row
        spread2[pl.ds(i * m2 + 1, m3, stride=2)] = row
    up2 = [spread2[(p // 2) * m2 : (p // 2 + 1) * m2] for p in range(n2)]
    c2 = after(t2, up2, inv2, off2)

    row = select_dot(jnp.concatenate(c2, 0), chosen(coarse // 2 == fine))
    fold1[pl.ds(0, half, stride=2)] = row
    fold1[pl.ds(1, half, stride=2)] = row
    up1 = [fold1[(p // 2) * m1 : (p // 2 + 1) * m1] for p in range(n1)]
    c1 = after(t1, up1, inv1, off1)

    window[...] = jnp.zeros_like(window)
    for p in range(n1):
        window[1 + p, TILE : TILE + m1, :] = c1[p]
    y = pl.multiple_of(gy * by, by)
    near = window[pl.ds(gx * bx, bx + 2), pl.ds(y, by + 2 * TILE), :]
    tall = by + 2 * TILE
    near = near.reshape((bx + 2) * tall, w1)
    spot = gz * t_in.shape[2] + iota((w1, 3 * w1), 1) % w1 + (iota((w1, 3 * w1), 1) // w1 + 1) % 3 - 1
    wanted = iota((w1, 3 * w1), 0)
    row = select_dot(near, chosen((2 * wanted == spot) | (2 * wanted + 1 == spot)))
    for s in range(3):
        doubled[s, pl.ds(0, (bx + 2) * tall, stride=2)] = row[:, s * w1 : (s + 1) * w1]
        doubled[s, pl.ds(1, (bx + 2) * tall, stride=2)] = row[:, s * w1 : (s + 1) * w1]
    ny = t_in.shape[1]

    def at(s, i, shift):
        first = (1 + i // 2) * 2 * tall + 2 * TILE + shift
        return doubled[s, first : first + ny]

    for i in range(t_in.shape[0]):
        value = t_in[i] + (1.0 - damping) * at(0, i, 0)
        value = value + k_in[0, i] * at(0, i - 1, 0) + k_in[1, i] * at(0, i + 1, 0)
        value = value + k_in[2, i] * at(0, i, -1) + k_in[3, i] * at(0, i, 1)
        out[i] = value + k_in[4, i] * at(2, i, 0) + k_in[5, i] * at(1, i, 0)


def traded(blocks, axis):
    count, cores = lax.axis_size(axis), lax.axis_size("gz")
    taken = []
    for kind, block in enumerate(blocks):
        route = []
        for i in range(count):
            other = i + 1 if (i + kind) % 2 == 0 else i - 1
            for c in range(cores):
                to = other * cores + c if 0 <= other < count else i * cores + cores - 1 - c
                route.append((i * cores + c, to))
        taken.append(lax.ppermute(block, (axis, "gz"), route))
    return taken


def gathered(block, axis):
    count = lax.axis_size(axis)
    parts = [lax.ppermute(block, axis, [(i, i ^ k) for i in range(count)]) for k in range(1, count)]
    return jnp.concatenate([block] + parts, 0)


def doubled_over(block, axis):
    count = lax.axis_size(axis)
    step = 1
    while step < count:
        other = lax.ppermute(block, axis, [(i, i ^ step) for i in range(count)])
        block = jnp.concatenate([block, other], 0)
        step *= 2
    return block


def f32(*shape):
    return jax.ShapeDtypeStruct(shape, jnp.float32)


def per_device_small(adjoint_residual, face_x, face_y, face_z):
    nx, ny, nz = adjoint_residual.shape
    near = [pltpu.VMEM((9, ny, nz), jnp.float32)] * 2
    own = jnp.stack((adjoint_residual, face_x, face_y, face_z))
    slabs = pl.pallas_call(
        x_kernel,
        out_shape=(f32(9, ny, nz), f32(9, ny, nz)),
        compiler_params=PARAMS,
        name="slabs_x",
    )(own)
    slabs = traded(slabs, "gx")
    count = -(-9 * (nx + 4) // 8) * 8
    lines = pl.pallas_call(
        y_kernel,
        out_shape=(f32(count, nz), f32(count, nz)),
        scratch_shapes=near,
        compiler_params=PARAMS,
        name="slabs_y",
    )(own, *slabs)
    lines = traded(lines, "gy")
    local, edge = pl.pallas_call(
        z_kernel,
        out_shape=(f32(4, nx + 2 * REACH, ny + 2 * TILE, nz), f32(nx + 4, ny + 2 * TILE, nz)),
        scratch_shapes=near + [pltpu.VMEM((count, nz), jnp.float32)],
        compiler_params=PARAMS,
        name="edges_z",
    )(own, *slabs, *lines)
    edges = lax.all_gather(edge, "gz", axis=0)
    ext_x, ext_y, wide = nx + 2 * REACH, ny + 2 * TILE, 2 * nz
    field = pltpu.VMEM((ext_x, ext_y, wide), jnp.float32)
    t, k, m = pl.pallas_call(
        fine_kernel,
        out_shape=(f32(nx, ny, nz), f32(6, nx, ny, nz), f32(2, nx // 2, ny // 2, nz)),
        scratch_shapes=[
            pltpu.VMEM((4, ext_x, ext_y, wide), jnp.float32),
            field,
            field,
            field,
            field,
            pltpu.VMEM((nx * ny, nz), jnp.float32),
        ],
        compiler_params=PARAMS,
        name="fine",
    )(local, edges)
    here = gathered(doubled_over(m[None], "gx"), "gy")
    there = lax.ppermute(here, "gz", [(0, 1), (1, 0)])
    n1, m1 = here.shape[2] * lax.axis_size("gx"), here.shape[3] * lax.axis_size("gy")
    tall = (nx // 2 + 2) * (ny // 2 + 2 * TILE)
    return pl.pallas_call(
        whole_kernel,
        out_shape=f32(nx, ny, nz),
        scratch_shapes=[
            pltpu.VMEM((4, n1, m1, nz), jnp.float32),
            pltpu.VMEM((2 * n1 * m1, nz), jnp.float32),
            pltpu.VMEM((2 * m1, nz), jnp.float32),
            pltpu.VMEM((n1 * m1 // 8, nz), jnp.float32),
            pltpu.VMEM((n1 + 2, m1 + 2 * TILE, nz), jnp.float32),
            pltpu.VMEM((3, 2 * tall, nz), jnp.float32),
        ],
        compiler_params=PARAMS,
        name="whole",
    )(here, there, t, k)


def extended(block, sides, width):
    for axis, dim in sides:
        count = lax.axis_size(axis)
        forward = [(i, i + 1) for i in range(count - 1)]
        backward = [(target, source) for source, target in forward]
        low = lax.ppermute(
            lax.slice_in_dim(block, block.shape[dim] - width, None, axis=dim), axis, forward
        )
        high = lax.ppermute(lax.slice_in_dim(block, 0, width, axis=dim), axis, backward)
        block = jnp.concatenate([low, block, high], axis=dim)
    return block


def from_behind(block, axis, distance):
    devices = range(lax.axis_size(axis))
    route = [(i - distance, i) for i in devices if i - distance in devices]
    return lax.ppermute(block, axis, route)


def stencil(padded, field, coefs):
    low_x, high_x, low_y, high_y, low_z, high_z = coefs
    diagonal = low_x + high_x + low_y + high_y + low_z + high_z
    result = diagonal * field - low_x * padded[:-2, 1:-1, 1:-1] - high_x * padded[2:, 1:-1, 1:-1]
    result = result - low_y * padded[1:-1, :-2, 1:-1] - high_y * padded[1:-1, 2:, 1:-1]
    return result - low_z * padded[1:-1, 1:-1, :-2] - high_z * padded[1:-1, 1:-1, 2:]


def operate(field, coefs):
    padded = extended(field, (("gx", 0), ("gy", 1), ("gz", 2)), 1)
    return stencil(padded, field, coefs)


def operate_whole(field, coefs):
    return stencil(jnp.pad(field, 1), field, coefs)


def blocked(values):
    return values.reshape(values.shape[0] // 2, 2, values.shape[1] // 2, 2, values.shape[2] // 2, 2)


def coarse_face(values, dim, parity):
    others = tuple((2 * k + 1 for k in range(3) if k != dim))
    summed = jnp.sum(blocked(values), axis=others)
    return 0.5 * lax.index_in_dim(summed, parity, dim + 1, keepdims=False)


def coarsen(coefs):
    result = []
    for dim in range(3):
        result.append(coarse_face(coefs[2 * dim], dim, 0))
        result.append(coarse_face(coefs[2 * dim + 1], dim, 1))
    return tuple(result)


def restrict(values):
    return jnp.sum(blocked(values), axis=(1, 3, 5))


def prolong(values):
    shape_out = (values.shape[0] * 2, values.shape[1] * 2, values.shape[2] * 2)
    wide = jnp.broadcast_to(
        values[:, None, :, None, :, None],
        (values.shape[0], 2, values.shape[1], 2, values.shape[2], 2),
    )
    return wide.reshape(shape_out)


def total_local(value):
    return value


def conj_grad(rhs, coefs, apply_op, total):
    solution = jnp.zeros_like(rhs)
    remain = rhs
    search = rhs
    norm_now = total(jnp.sum(remain * remain))
    for step in range(COARSE_ITERS):
        image = apply_op(search, coefs)
        alpha = norm_now / total(jnp.sum(search * image))
        solution = solution + alpha * search
        remain = remain - alpha * image
        norm_next = total(jnp.sum(remain * remain))
        search = remain + norm_next / norm_now * search
        norm_now = norm_next
    return solution


def coarse_solve(rhs, coefs):
    part_x, part_y, part_z = rhs.shape
    count_x = lax.axis_size("gx")
    count_y = lax.axis_size("gy")
    count_z = lax.axis_size("gz")
    stacked = jnp.stack((rhs,) + coefs)[None]
    whole = lax.all_gather(stacked, ("gx", "gy", "gz"), axis=0, tiled=True)
    whole = whole.reshape(count_x, count_y, count_z, 7, part_x, part_y, part_z)
    whole = whole.transpose(3, 0, 4, 1, 5, 2, 6).reshape(
        7, count_x * part_x, count_y * part_y, count_z * part_z
    )
    whole_coefs = tuple((whole[k] for k in range(1, 7)))
    solution = conj_grad(whole[0], whole_coefs, operate_whole, total_local)
    starts = (
        lax.axis_index("gx") * part_x,
        lax.axis_index("gy") * part_y,
        lax.axis_index("gz") * part_z,
    )
    return lax.dynamic_slice(solution, starts, (part_x, part_y, part_z))


def cycle(rhs, levels_left, coefs):
    if levels_left == 1:
        return coarse_solve(rhs, coefs)
    diagonal = coefs[0] + coefs[1] + coefs[2] + coefs[3] + coefs[4] + coefs[5]
    field = damping * rhs / diagonal
    field = field + damping * (rhs - operate(field, coefs)) / diagonal
    remain = rhs - operate(field, coefs)
    field = field + prolong(cycle(restrict(remain), levels_left - 1, coarsen(coefs)))
    field = field + damping * (rhs - operate(field, coefs)) / diagonal
    return field


def per_device(adjoint_residual, face_x, face_y, face_z):
    rim_x = from_behind(face_x[:1], "gx", -1)
    rim_y = from_behind(face_y[:, :1], "gy", -1)
    rim_z = from_behind(face_z[:, :, :1], "gz", -1)
    high_x = jnp.concatenate([face_x[1:], rim_x], 0)
    high_y = jnp.concatenate([face_y[:, 1:], rim_y], 1)
    high_z = jnp.concatenate([face_z[:, :, 1:], rim_z], 2)
    coefs = (face_x, high_x, face_y, high_y, face_z, high_z)
    return cycle(adjoint_residual, LEVELS, coefs)


def fits(mesh, shape):
    nx, ny, nz = shape
    cx, cy, cz = mesh.shape["gx"], mesh.shape["gy"], mesh.shape["gz"]
    powers = cx & (cx - 1) == 0 and cy & (cy - 1) == 0 and cz == 2
    blocks = nx % (8 * cx) == 0 and ny % (16 * cy) == 0 and nz == 256
    return powers and blocks and (nx // 8) * (nz // 8) == 128 and nx * ny * nz <= 2**19


def per_block(mesh, *args):
    counts = (mesh.shape["gx"], mesh.shape["gy"], mesh.shape["gz"])
    whole = tuple(n * c for n, c in zip(args[0].shape, counts))
    return (per_device_small if fits(mesh, whole) else per_device)(*args)


def solution(mesh):
    return jax.shard_map(
        functools.partial(per_block, mesh),
        mesh=mesh,
        in_specs=(
            P("gx", "gy", "gz"),
            P("gx", "gy", "gz"),
            P("gx", "gy", "gz"),
            P("gx", "gy", "gz"),
        ),
        out_specs=P("gx", "gy", "gz"),
        check_vma=False,
    )
```

```python
import functools

import jax
import jax.numpy as jnp
from jax import lax
from jax.experimental import pallas as pl
from jax.experimental.pallas import tpu as pltpu
from jax.sharding import PartitionSpec as P

LEVELS = 4
COARSE_ITERS = 6


damping = 2.0 / 3.0

REACH = 3
TILE = 8
PARAMS = pltpu.CompilerParams(vmem_limit_bytes=16 * 2**20)


def up(v, axis):
    return pltpu.roll(v, v.shape[axis] - 1, axis)


def down(v, axis):
    return pltpu.roll(v, 1, axis)


def iota(shape, axis):
    return lax.broadcasted_iota(jnp.int32, shape, axis)


def chosen(mask):
    return jnp.where(mask, 1.0, 0.0).astype(jnp.bfloat16)


def select_dot(values, matrix):
    count = values.shape[0]
    high = values.astype(jnp.bfloat16).astype(jnp.float32)
    rest = values - high
    mid = rest.astype(jnp.bfloat16).astype(jnp.float32)
    parts = jnp.concatenate([high, mid, rest - mid], 0).astype(jnp.bfloat16)
    product = jnp.dot(parts, matrix, preferred_element_type=jnp.float32)
    return (product[2 * count :] + product[count : 2 * count]) + product[:count]


def inverse(diagonal):
    return jnp.where(diagonal > 0.0, damping / jnp.where(diagonal > 0.0, diagonal, 1.0), 0.0)


def side(axis):
    here = lax.axis_index(axis)
    first = jnp.where(here > 0, 1.0, 0.0)
    last = jnp.where(here < lax.axis_size(axis) - 1, 1.0, 0.0)
    return (here % 2 == 1, first), (here % 2 == 0, last)


def x_kernel(own, *slabs):
    nx, gx = own.shape[1], lax.axis_index("gx")
    for kind, out in enumerate(slabs):
        start = jnp.where((gx + kind) % 2 == 0, nx - 2, 0)
        for a in range(4):
            for n in range(2):
                out[2 * a + n] = own[a, start + n]
        out[8] = own[1, 2]


def sides_x(slabs, before, behind):
    for (even, keep), out in zip(side("gx"), (before, behind)):
        for n in range(9):
            out[n] = keep * jnp.where(even, slabs[0][n], slabs[1][n])


def y_kernel(own, s0, s1, o0, o1, before, behind):
    nx, ny = own.shape[1], own.shape[2]
    gy = lax.axis_index("gy")
    sides_x((s0, s1), before, behind)
    for kind, out in enumerate((o0, o1)):
        ahead = (gy + kind) % 2 == 0
        for p in range(nx + 4):
            for a in range(4):
                if p < 2:
                    v = before[2 * a + p]
                elif p < nx + 2:
                    v = own[a, p - 2]
                else:
                    v = behind[2 * a + p - nx - 2]
                at = (a * (nx + 4) + p) * 2
                out[at : at + 2] = jnp.where(ahead, v[ny - 2 :], v[:2])
                if a == 2:
                    out[8 * (nx + 4) + p : 8 * (nx + 4) + p + 1] = v[2:3]
        used = 9 * (nx + 4)
        out[used:] = jnp.zeros((out.shape[0] - used, out.shape[1]), jnp.float32)


def z_kernel(own, s0, s1, o0, o1, ext, edge, before, behind, lines):
    nx, ny, nz = own.shape[1:]
    gz = lax.axis_index("gz")
    sides_x((s0, s1), before, behind)
    zero = jnp.zeros((TILE, nz), jnp.float32)
    empty = jnp.zeros((ny + 2 * TILE, nz), jnp.float32)
    for a in range(4):
        for p in range(nx + 2 * REACH):
            q = p - REACH
            if 0 <= q < nx:
                v = own[a, q]
            elif -2 <= q < 0:
                v = before[2 * a + q + 2]
            elif nx <= q < nx + 2:
                v = behind[2 * a + q - nx]
            elif q == nx + 2 and a == 1:
                v = behind[8]
            else:
                ext[a, p] = empty
                continue
            ext[a, p, :TILE] = zero
            ext[a, p, TILE + ny :] = zero
            ext[a, p, TILE : TILE + ny] = v
    for (even, keep), r in zip(side("gy"), (TILE - 2, TILE + ny)):
        lines[...] = keep * jnp.where(even, o0[...], o1[...])
        for p in range(nx + 4):
            for a in range(4):
                at = (a * (nx + 4) + p) * 2
                ext[a, 1 + p, r : r + 2] = lines[at : at + 2]
            if r > TILE:
                at = 8 * (nx + 4) + p
                ext[2, 1 + p, r + 2 : r + 3] = lines[at : at + 1]
    lane = iota((ny + 2 * TILE, nz), 1)
    for p in range(nx + 4):
        packed = ext[0, 1 + p]
        for a in range(1, 4):
            first = jnp.where(gz == 0, nz - 3 - 3 * a, 3 * a)
            moved = pltpu.roll(ext[a, 1 + p], jnp.where(gz == 0, nz - 3 * a, 3 * a), 1)
            packed = jnp.where((lane >= first) & (lane < first + 3), moved, packed)
        edge[p] = packed


def fine_kernel(local, edges, t_out, k_out, m_out, ext, e1, rd, dg, e2, rows):
    nx, ny, half = t_out.shape
    nz = 2 * half
    gx, gy, gz = lax.axis_index("gx"), lax.axis_index("gy"), lax.axis_index("gz")
    spot = iota((ny + 2 * TILE, half), 1)
    given = jnp.logical_or((gz == 0) & (spot < 3), (gz == 1) & (spot >= half - 3))
    for p in range(nx + 2 * REACH):
        for a in range(4):
            ext[a, p, :, :half] = local[a, p]
            if 1 <= p < nx + 5:
                v = edges[1 - gz, p - 1]
                if a > 0:
                    v = pltpu.roll(v, jnp.where(gz == 0, half - 3 * a, 3 * a), 1)
                ext[a, p, :, half:] = jnp.where(given, v, 0.0)
            else:
                ext[a, p, :, half:] = jnp.zeros((ny + 2 * TILE, half), jnp.float32)
    shape = (ny + 2 * TILE, nz)
    row, lane = iota(shape, 0), iota(shape, 1)
    inner_z = jnp.logical_or(lane > 0, gz > 0)
    in_y = jnp.logical_and(
        jnp.logical_or(gy > 0, row >= TILE),
        jnp.logical_or(gy < lax.axis_size("gy") - 1, row < TILE + ny),
    )

    def off(e, p):
        fy, fz = ext[2, p], jnp.where(inner_z, ext[3, p], 0.0)
        here = e[p]
        total = ext[1, p] * e[p - 1] + ext[1, p + 1] * e[p + 1]
        total = total + fy * down(here, 0) + up(fy * here, 0)
        return total + fz * down(here, 1) + up(fz * here, 1)

    for p in range(1, nx + 2 * REACH - 1):
        fy, fz = ext[2, p], ext[3, p]
        diagonal = ext[1, p] + ext[1, p + 1] + fy + up(fy, 0) + fz + up(jnp.where(inner_z, fz, 0.0), 1)
        inv = inverse(diagonal)
        dg[p], rd[p] = diagonal, inv
        e1[p] = ext[0, p] * inv
    for p in range(2, nx + 2 * REACH - 2):
        value = (2.0 - damping) * e1[p] + rd[p] * off(e1, p)
        inside = in_y
        if p < REACH:
            inside = jnp.logical_and(inside, gx > 0)
        if p >= REACH + nx:
            inside = jnp.logical_and(inside, gx < lax.axis_size("gx") - 1)
        e2[p] = jnp.where(inside, value, 0.0)

    def mine(v):
        return v[TILE : TILE + ny, :half]

    sums = []
    for i in range(nx):
        p = REACH + i
        q = ext[0, p] - dg[p] * e2[p] + off(e2, p)
        fy, fz = ext[2, p], jnp.where(inner_z, ext[3, p], 0.0)
        inv = rd[p]
        t_out[i] = mine(e2[p] + inv * q)
        for n, k in enumerate((ext[1, p], ext[1, p + 1], fy, up(fy, 0), fz, up(fz, 1))):
            k_out[n, i] = mine(inv * k)
        sums.append(mine(q))
    def face(d, i):
        return 0.5 * ext[d, REACH + i, TILE : TILE + ny, :half]

    pairs = range(0, nx, 2)
    fine, coarse = iota((half, half), 0), iota((half, half), 1)
    both_low, both_high = chosen(fine // 2 == coarse), chosen(fine // 2 + half // 2 == coarse)
    even_high = chosen(fine + half == 2 * coarse)
    count = len(pairs) * ny
    rows[:count] = select_dot(jnp.concatenate([sums[i] + sums[i + 1] for i in pairs], 0), both_low) + select_dot(
        jnp.concatenate([face(1, i) for i in pairs], 0), both_high
    )
    rows[count:] = select_dot(jnp.concatenate([face(2, i) + face(2, i + 1) for i in pairs], 0), both_low) + select_dot(
        jnp.concatenate([face(3, i) + face(3, i + 1) for i in pairs], 0), even_high
    )
    part = count // 2
    even = rows[pl.ds(0, 2 * part, stride=2)]
    odd = rows[pl.ds(1, 2 * part, stride=2)]
    spot = iota((part, half), 1)
    m_out[0] = (even[:part] + odd[:part]).reshape(m_out.shape[1:])
    m_out[1] = (even[part:] + jnp.where(spot < half // 2, 0.0, odd[part:])).reshape(m_out.shape[1:])


def planes_of(ref):
    return [ref[p] for p in range(ref.shape[0])]


def level_parts(fx, fy, fz):
    shape = fy[0].shape
    row, lane = iota(shape, 0), iota(shape, 1)
    n = len(fx)
    zero = jnp.zeros(shape, jnp.float32)
    fym = [jnp.where(row > 0, v, 0.0) for v in fy]
    fzm = [jnp.where(lane > 0, v, 0.0) for v in fz]
    high = [fx[p + 1] if p + 1 < n else zero for p in range(n)]
    diagonal = [fx[p] + high[p] + fy[p] + up(fym[p], 0) + fz[p] + up(fzm[p], 1) for p in range(n)]

    def off(e):
        result = []
        for p in range(n):
            total = fym[p] * down(e[p], 0) + up(fym[p] * e[p], 0)
            total = total + fzm[p] * down(e[p], 1) + up(fzm[p] * e[p], 1)
            if p > 0:
                total = total + fx[p] * e[p - 1]
            if p + 1 < n:
                total = total + fx[p + 1] * e[p + 1]
            result.append(total)
        return result

    return diagonal, [inverse(d) for d in diagonal], off


def before(b, diagonal, inv, off):
    e1 = [v * r for v, r in zip(b, inv)]
    e2 = [(2.0 - damping) * e + r * o for e, r, o in zip(e1, inv, off(e1))]
    q = [v - d * e + o for v, d, e, o in zip(b, diagonal, e2, off(e2))]
    return [e + r * v for e, r, v in zip(e2, inv, q)], q


def after(t, c, inv, off):
    return [v + (1.0 - damping) * k + r * o for v, k, r, o in zip(t, c, inv, off(c))]


def coarse_solution(rhs, fx, fy, fz, depth):
    shape = rhs.shape
    row, lane = iota(shape, 0), iota(shape, 1)
    fxm = jnp.where(lane >= depth, fx, 0.0)
    fym = jnp.where(row > 0, fy, 0.0)
    fzm = jnp.where(lane % depth > 0, fz, 0.0)
    wide = shape[1]

    def up_x(v):
        return pltpu.roll(v, wide - depth, 1)

    hx, hy, hz = up_x(fxm), up(fym, 0), up(fzm, 1)
    diagonal = fx + hx + fy + hy + fz + hz

    def operate_packed(v):
        result = diagonal * v - fxm * pltpu.roll(v, depth, 1) - hx * up_x(v)
        result = result - fym * down(v, 0) - hy * up(v, 0)
        return result - fzm * down(v, 1) - hz * up(v, 1)

    def total(v):
        v = jnp.broadcast_to(jnp.sum(v, axis=1, keepdims=True), v.shape)
        for shift in (4, 2, 1):
            v = v + pltpu.roll(v, shift, 0)
        return v

    remain, search = rhs, rhs
    image = operate_packed(rhs)
    norm_now, energy = total(rhs * rhs), total(rhs * image)
    alpha = norm_now / energy
    solution = alpha * search
    for step in range(COARSE_ITERS - 1):
        remain = remain - alpha * image
        across = operate_packed(remain)
        norm_next, own, mixed = total(remain * remain), total(remain * across), total(remain * image)
        beta = norm_next / norm_now
        energy = own + beta * (2.0 * mixed + beta * energy)
        search = remain + beta * search
        image = across + beta * image
        norm_now = norm_next
        alpha = norm_now / energy
        solution = solution + alpha * search
    return solution


def whole_kernel(here, there, t_in, k_in, out, grid, fold1, fold2, spread2, window, doubled):
    gx, gy, gz = lax.axis_index("gx"), lax.axis_index("gy"), lax.axis_index("gz")
    cx, cy = lax.axis_size("gx"), lax.axis_size("gy")
    bx, by = here.shape[2], here.shape[3]
    w1 = here.shape[4]
    for k in range(cx * cy):
        x = jnp.bitwise_xor(gx, k % cx) * bx
        y = pl.multiple_of(jnp.bitwise_xor(gy, k // cx) * by, by)
        for a in range(2):
            low = jnp.where(gz == 0, here[k, a], there[k, a]).reshape(bx * by, w1)
            top = jnp.where(gz == 0, there[k, a], here[k, a]).reshape(bx * by, w1)
            left = iota((bx * by, w1), 1) < w1 // 2
            one = jnp.where(left, low, pltpu.roll(top, w1 // 2, 1))
            two = jnp.where(left, pltpu.roll(low, w1 // 2, 1), top)
            grid[2 * a, pl.ds(x, bx), pl.ds(y, by), :] = one.reshape(bx, by, w1)
            grid[2 * a + 1, pl.ds(x, bx), pl.ds(y, by), :] = two.reshape(bx, by, w1)
    n1, m1, w1 = grid.shape[1:]
    b1, fx1, fy1, fz1 = (planes_of(grid.at[a]) for a in range(4))
    diagonal1, inv1, off1 = level_parts(fx1, fy1, fz1)
    t1, q1 = before(b1, diagonal1, inv1, off1)

    n2, m2 = n1 // 2, m1 // 2
    pairs = range(0, n1, 2)
    fold1[...] = jnp.concatenate(
        [q1[i] + q1[i + 1] for i in pairs]
        + [0.5 * fx1[i] for i in pairs]
        + [0.5 * (fy1[i] + fy1[i + 1]) for i in pairs]
        + [0.5 * (fz1[i] + fz1[i + 1]) for i in pairs],
        0,
    )
    half = n2 * m2
    low = fold1[pl.ds(0, 4 * half, stride=2)]
    top = fold1[pl.ds(1, 4 * half, stride=2)]
    fine, coarse = iota((w1, w1), 0), iota((w1, w1), 1)
    both, even = chosen(fine // 2 == coarse), chosen(fine == 2 * coarse)
    summed = jnp.concatenate([low[: 2 * half] + top[: 2 * half], low[2 * half : 3 * half]], 0)
    summed = select_dot(summed, both)

    def part(v):
        return [v[p * m2 : (p + 1) * m2] for p in range(n2)]

    b2, fx2, fy2 = (part(summed[i * half : (i + 1) * half]) for i in range(3))
    fz2 = part(select_dot(low[3 * half :] + top[3 * half :], even))
    diagonal2, inv2, off2 = level_parts(fx2, fy2, fz2)
    t2, q2 = before(b2, diagonal2, inv2, off2)

    n3, m3 = n2 // 2, m2 // 2
    depth = w1 // n3
    fine, coarse = iota((n3 * w1, w1), 0), iota((n3 * w1, w1), 1)
    block, fine = fine // w1, fine % w1
    both = chosen((fine // 2 + block * depth == coarse) & (fine < 2 * depth))
    even = chosen((fine + 2 * block * depth == 2 * coarse) & (fine < 2 * depth))
    blocks = range(0, n2, 2)
    wide = [
        jnp.concatenate([q2[i] + q2[i + 1] for i in blocks], 1),
        jnp.concatenate([0.5 * fx2[i] for i in blocks], 1),
        jnp.concatenate([0.5 * (fy2[i] + fy2[i + 1]) for i in blocks], 1),
    ]
    thin = jnp.concatenate([0.5 * (fz2[i] + fz2[i + 1]) for i in blocks], 1)
    packed = [select_dot(jnp.concatenate(wide, 0), both), select_dot(thin, even)]
    fold2[...] = jnp.concatenate(packed, 0)
    low = fold2[pl.ds(0, 4 * m3, stride=2)]
    top = fold2[pl.ds(1, 4 * m3, stride=2)]
    b3, fx3 = low[:m3] + top[:m3], low[m3 : 2 * m3] + top[m3 : 2 * m3]
    fy3, fz3 = low[2 * m3 : 3 * m3], low[3 * m3 :] + top[3 * m3 :]
    c3 = coarse_solution(b3, fx3, fy3, fz3, depth)

    fine, coarse = iota((w1, n3 * w1), 1), iota((w1, n3 * w1), 0)
    block, fine = fine // w1, fine % w1
    row = select_dot(c3, chosen((fine // 2 + block * depth == coarse) & (fine < 2 * depth)))
    for i in range(n3):
        spread2[pl.ds(i * m2, m3, stride=2)] = row[:, i * w1 : (i + 1) * w1]
        spread2[pl.ds(i * m2 + 1, m3, stride=2)] = row[:, i * w1 : (i + 1) * w1]
    up2 = [spread2[(p // 2) * m2 : (p // 2 + 1) * m2] for p in range(n2)]
    c2 = after(t2, up2, inv2, off2)

    fine, coarse = iota((w1, w1), 1), iota((w1, w1), 0)
    row = select_dot(jnp.concatenate(c2, 0), chosen(fine // 2 == coarse))
    fold1[pl.ds(0, half, stride=2)] = row
    fold1[pl.ds(1, half, stride=2)] = row
    up1 = [fold1[(p // 2) * m1 : (p // 2 + 1) * m1] for p in range(n1)]
    c1 = after(t1, up1, inv1, off1)

    window[...] = jnp.zeros_like(window)
    for p in range(n1):
        window[1 + p, TILE : TILE + m1, :] = c1[p]
    y = pl.multiple_of(gy * by, by)
    near = window[pl.ds(gx * bx, bx + 2), pl.ds(y, by + 2 * TILE), :]
    tall = by + 2 * TILE
    near = near.reshape((bx + 2) * tall, w1)
    spot = gz * t_in.shape[2] + iota((w1, 3 * w1), 1) % w1 + (iota((w1, 3 * w1), 1) // w1 + 1) % 3 - 1
    wanted = iota((w1, 3 * w1), 0)
    row = select_dot(near, chosen((2 * wanted == spot) | (2 * wanted + 1 == spot)))
    for s in range(3):
        doubled[s, pl.ds(0, (bx + 2) * tall, stride=2)] = row[:, s * w1 : (s + 1) * w1]
        doubled[s, pl.ds(1, (bx + 2) * tall, stride=2)] = row[:, s * w1 : (s + 1) * w1]
    ny = t_in.shape[1]

    def at(s, i, shift):
        first = (1 + i // 2) * 2 * tall + 2 * TILE + shift
        return doubled[s, first : first + ny]

    for i in range(t_in.shape[0]):
        value = t_in[i] + (1.0 - damping) * at(0, i, 0)
        value = value + k_in[0, i] * at(0, i - 1, 0) + k_in[1, i] * at(0, i + 1, 0)
        value = value + k_in[2, i] * at(0, i, -1) + k_in[3, i] * at(0, i, 1)
        out[i] = value + k_in[4, i] * at(2, i, 0) + k_in[5, i] * at(1, i, 0)


def traded(blocks, axis):
    count, cores = lax.axis_size(axis), lax.axis_size("gz")
    taken = []
    for kind, block in enumerate(blocks):
        route = []
        for i in range(count):
            other = i + 1 if (i + kind) % 2 == 0 else i - 1
            for c in range(cores):
                to = other * cores + c if 0 <= other < count else i * cores + cores - 1 - c
                route.append((i * cores + c, to))
        taken.append(lax.ppermute(block, (axis, "gz"), route))
    return taken


def gathered(block, axis):
    count = lax.axis_size(axis)
    parts = [lax.ppermute(block, axis, [(i, i ^ k) for i in range(count)]) for k in range(1, count)]
    return jnp.concatenate([block] + parts, 0)


def doubled_over(block, axis):
    count = lax.axis_size(axis)
    step = 1
    while step < count:
        other = lax.ppermute(block, axis, [(i, i ^ step) for i in range(count)])
        block = jnp.concatenate([block, other], 0)
        step *= 2
    return block


def f32(*shape):
    return jax.ShapeDtypeStruct(shape, jnp.float32)


def per_device_small(adjoint_residual, face_x, face_y, face_z):
    nx, ny, nz = adjoint_residual.shape
    near = [pltpu.VMEM((9, ny, nz), jnp.float32)] * 2
    own = jnp.stack((adjoint_residual, face_x, face_y, face_z))
    slabs = pl.pallas_call(
        x_kernel,
        out_shape=(f32(9, ny, nz), f32(9, ny, nz)),
        compiler_params=PARAMS,
        name="slabs_x",
    )(own)
    slabs = traded(slabs, "gx")
    count = -(-9 * (nx + 4) // 8) * 8
    lines = pl.pallas_call(
        y_kernel,
        out_shape=(f32(count, nz), f32(count, nz)),
        scratch_shapes=near,
        compiler_params=PARAMS,
        name="slabs_y",
    )(own, *slabs)
    lines = traded(lines, "gy")
    local, edge = pl.pallas_call(
        z_kernel,
        out_shape=(f32(4, nx + 2 * REACH, ny + 2 * TILE, nz), f32(nx + 4, ny + 2 * TILE, nz)),
        scratch_shapes=near + [pltpu.VMEM((count, nz), jnp.float32)],
        compiler_params=PARAMS,
        name="edges_z",
    )(own, *slabs, *lines)
    edges = lax.all_gather(edge, "gz", axis=0)
    ext_x, ext_y, wide = nx + 2 * REACH, ny + 2 * TILE, 2 * nz
    field = pltpu.VMEM((ext_x, ext_y, wide), jnp.float32)
    t, k, m = pl.pallas_call(
        fine_kernel,
        out_shape=(f32(nx, ny, nz), f32(6, nx, ny, nz), f32(2, nx // 2, ny // 2, nz)),
        scratch_shapes=[
            pltpu.VMEM((4, ext_x, ext_y, wide), jnp.float32),
            field,
            field,
            field,
            field,
            pltpu.VMEM((nx * ny, nz), jnp.float32),
        ],
        compiler_params=PARAMS,
        name="fine",
    )(local, edges)
    here = gathered(doubled_over(m[None], "gx"), "gy")
    there = lax.ppermute(here, "gz", [(0, 1), (1, 0)])
    n1, m1 = here.shape[2] * lax.axis_size("gx"), here.shape[3] * lax.axis_size("gy")
    tall = (nx // 2 + 2) * (ny // 2 + 2 * TILE)
    return pl.pallas_call(
        whole_kernel,
        out_shape=f32(nx, ny, nz),
        scratch_shapes=[
            pltpu.VMEM((4, n1, m1, nz), jnp.float32),
            pltpu.VMEM((2 * n1 * m1, nz), jnp.float32),
            pltpu.VMEM((2 * m1, nz), jnp.float32),
            pltpu.VMEM((n1 * m1 // 8, nz), jnp.float32),
            pltpu.VMEM((n1 + 2, m1 + 2 * TILE, nz), jnp.float32),
            pltpu.VMEM((3, 2 * tall, nz), jnp.float32),
        ],
        compiler_params=PARAMS,
        name="whole",
    )(here, there, t, k)


def extended(block, sides, width):
    for axis, dim in sides:
        count = lax.axis_size(axis)
        forward = [(i, i + 1) for i in range(count - 1)]
        backward = [(target, source) for source, target in forward]
        low = lax.ppermute(
            lax.slice_in_dim(block, block.shape[dim] - width, None, axis=dim), axis, forward
        )
        high = lax.ppermute(lax.slice_in_dim(block, 0, width, axis=dim), axis, backward)
        block = jnp.concatenate([low, block, high], axis=dim)
    return block


def from_behind(block, axis, distance):
    devices = range(lax.axis_size(axis))
    route = [(i - distance, i) for i in devices if i - distance in devices]
    return lax.ppermute(block, axis, route)


def stencil(padded, field, coefs):
    low_x, high_x, low_y, high_y, low_z, high_z = coefs
    diagonal = low_x + high_x + low_y + high_y + low_z + high_z
    result = diagonal * field - low_x * padded[:-2, 1:-1, 1:-1] - high_x * padded[2:, 1:-1, 1:-1]
    result = result - low_y * padded[1:-1, :-2, 1:-1] - high_y * padded[1:-1, 2:, 1:-1]
    return result - low_z * padded[1:-1, 1:-1, :-2] - high_z * padded[1:-1, 1:-1, 2:]


def operate(field, coefs):
    padded = extended(field, (("gx", 0), ("gy", 1), ("gz", 2)), 1)
    return stencil(padded, field, coefs)


def operate_whole(field, coefs):
    return stencil(jnp.pad(field, 1), field, coefs)


def blocked(values):
    return values.reshape(values.shape[0] // 2, 2, values.shape[1] // 2, 2, values.shape[2] // 2, 2)


def coarse_face(values, dim, parity):
    others = tuple((2 * k + 1 for k in range(3) if k != dim))
    summed = jnp.sum(blocked(values), axis=others)
    return 0.5 * lax.index_in_dim(summed, parity, dim + 1, keepdims=False)


def coarsen(coefs):
    result = []
    for dim in range(3):
        result.append(coarse_face(coefs[2 * dim], dim, 0))
        result.append(coarse_face(coefs[2 * dim + 1], dim, 1))
    return tuple(result)


def restrict(values):
    return jnp.sum(blocked(values), axis=(1, 3, 5))


def prolong(values):
    shape_out = (values.shape[0] * 2, values.shape[1] * 2, values.shape[2] * 2)
    wide = jnp.broadcast_to(
        values[:, None, :, None, :, None],
        (values.shape[0], 2, values.shape[1], 2, values.shape[2], 2),
    )
    return wide.reshape(shape_out)


def total_local(value):
    return value


def conj_grad(rhs, coefs, apply_op, total):
    solution = jnp.zeros_like(rhs)
    remain = rhs
    search = rhs
    norm_now = total(jnp.sum(remain * remain))
    for step in range(COARSE_ITERS):
        image = apply_op(search, coefs)
        alpha = norm_now / total(jnp.sum(search * image))
        solution = solution + alpha * search
        remain = remain - alpha * image
        norm_next = total(jnp.sum(remain * remain))
        search = remain + norm_next / norm_now * search
        norm_now = norm_next
    return solution


def coarse_solve(rhs, coefs):
    part_x, part_y, part_z = rhs.shape
    count_x = lax.axis_size("gx")
    count_y = lax.axis_size("gy")
    count_z = lax.axis_size("gz")
    stacked = jnp.stack((rhs,) + coefs)[None]
    whole = lax.all_gather(stacked, ("gx", "gy", "gz"), axis=0, tiled=True)
    whole = whole.reshape(count_x, count_y, count_z, 7, part_x, part_y, part_z)
    whole = whole.transpose(3, 0, 4, 1, 5, 2, 6).reshape(
        7, count_x * part_x, count_y * part_y, count_z * part_z
    )
    whole_coefs = tuple((whole[k] for k in range(1, 7)))
    solution = conj_grad(whole[0], whole_coefs, operate_whole, total_local)
    starts = (
        lax.axis_index("gx") * part_x,
        lax.axis_index("gy") * part_y,
        lax.axis_index("gz") * part_z,
    )
    return lax.dynamic_slice(solution, starts, (part_x, part_y, part_z))


def cycle(rhs, levels_left, coefs):
    if levels_left == 1:
        return coarse_solve(rhs, coefs)
    diagonal = coefs[0] + coefs[1] + coefs[2] + coefs[3] + coefs[4] + coefs[5]
    field = damping * rhs / diagonal
    field = field + damping * (rhs - operate(field, coefs)) / diagonal
    remain = rhs - operate(field, coefs)
    field = field + prolong(cycle(restrict(remain), levels_left - 1, coarsen(coefs)))
    field = field + damping * (rhs - operate(field, coefs)) / diagonal
    return field


def per_device(adjoint_residual, face_x, face_y, face_z):
    rim_x = from_behind(face_x[:1], "gx", -1)
    rim_y = from_behind(face_y[:, :1], "gy", -1)
    rim_z = from_behind(face_z[:, :, :1], "gz", -1)
    high_x = jnp.concatenate([face_x[1:], rim_x], 0)
    high_y = jnp.concatenate([face_y[:, 1:], rim_y], 1)
    high_z = jnp.concatenate([face_z[:, :, 1:], rim_z], 2)
    coefs = (face_x, high_x, face_y, high_y, face_z, high_z)
    return cycle(adjoint_residual, LEVELS, coefs)


def fits(mesh, shape):
    nx, ny, nz = shape
    cx, cy, cz = mesh.shape["gx"], mesh.shape["gy"], mesh.shape["gz"]
    powers = cx & (cx - 1) == 0 and cy & (cy - 1) == 0 and cz == 2
    blocks = nx % (8 * cx) == 0 and ny % (16 * cy) == 0 and nz == 256
    return powers and blocks and (nx // 8) * (nz // 8) == 128 and nx * ny * nz <= 2**19


def per_block(mesh, *args):
    counts = (mesh.shape["gx"], mesh.shape["gy"], mesh.shape["gz"])
    whole = tuple(n * c for n, c in zip(args[0].shape, counts))
    return (per_device_small if fits(mesh, whole) else per_device)(*args)


def solution(mesh):
    return jax.shard_map(
        functools.partial(per_block, mesh),
        mesh=mesh,
        in_specs=(
            P("gx", "gy", "gz"),
            P("gx", "gy", "gz"),
            P("gx", "gy", "gz"),
            P("gx", "gy", "gz"),
        ),
        out_specs=P("gx", "gy", "gz"),
        check_vma=False,
    )
```

```python
import functools

import jax
import jax.numpy as jnp
from jax import lax
from jax.experimental import pallas as pl
from jax.experimental.pallas import tpu as pltpu
from jax.sharding import PartitionSpec as P

LEVELS = 4
COARSE_ITERS = 6


damping = 2.0 / 3.0

REACH = 3
TILE = 8
PAD = 4
PARAMS = pltpu.CompilerParams(vmem_limit_bytes=16 * 2**20)


def up(v, axis):
    return pltpu.roll(v, v.shape[axis] - 1, axis)


def down(v, axis):
    return pltpu.roll(v, 1, axis)


def iota(shape, axis):
    return lax.broadcasted_iota(jnp.int32, shape, axis)


def chosen(mask):
    return jnp.where(mask, 1.0, 0.0).astype(jnp.bfloat16)


def select_dot(values, matrix):
    count = values.shape[0]
    high = values.astype(jnp.bfloat16).astype(jnp.float32)
    rest = values - high
    mid = rest.astype(jnp.bfloat16).astype(jnp.float32)
    parts = jnp.concatenate([high, mid, rest - mid], 0).astype(jnp.bfloat16)
    product = jnp.dot(parts, matrix, preferred_element_type=jnp.float32)
    return (product[2 * count :] + product[count : 2 * count]) + product[:count]


def inverse(diagonal):
    return jnp.where(diagonal > 0.0, damping / jnp.where(diagonal > 0.0, diagonal, 1.0), 0.0)


def side(axis):
    here = lax.axis_index(axis)
    first = jnp.where(here > 0, 1.0, 0.0)
    last = jnp.where(here < lax.axis_size(axis) - 1, 1.0, 0.0)
    return (here % 2 == 1, first), (here % 2 == 0, last)


def x_kernel(own, *slabs):
    nx, gx = own.shape[1], lax.axis_index("gx")
    for kind, out in enumerate(slabs):
        start = jnp.where((gx + kind) % 2 == 0, nx - 2, 0)
        for a in range(4):
            for n in range(2):
                out[2 * a + n] = own[a, start + n]
        out[8] = own[1, 2]


def sides_x(slabs, before, behind):
    for (even, keep), out in zip(side("gx"), (before, behind)):
        for n in range(9):
            out[n] = keep * jnp.where(even, slabs[0][n], slabs[1][n])


def y_kernel(own, s0, s1, o0, o1, before, behind):
    nx, ny = own.shape[1], own.shape[2]
    gy = lax.axis_index("gy")
    sides_x((s0, s1), before, behind)
    for kind, out in enumerate((o0, o1)):
        ahead = (gy + kind) % 2 == 0
        for p in range(nx + 4):
            for a in range(4):
                if p < 2:
                    v = before[2 * a + p]
                elif p < nx + 2:
                    v = own[a, p - 2]
                else:
                    v = behind[2 * a + p - nx - 2]
                at = (a * (nx + 4) + p) * 2
                out[at : at + 2] = jnp.where(ahead, v[ny - 2 :], v[:2])
                if a == 2:
                    out[8 * (nx + 4) + p : 8 * (nx + 4) + p + 1] = v[2:3]
        used = 9 * (nx + 4)
        out[used:] = jnp.zeros((out.shape[0] - used, out.shape[1]), jnp.float32)


def z_kernel(own, s0, s1, o0, o1, ext, edge, before, behind, lines):
    nx, ny, nz = own.shape[1:]
    gz = lax.axis_index("gz")
    sides_x((s0, s1), before, behind)
    zero = jnp.zeros((PAD, nz), jnp.float32)
    empty = jnp.zeros((ny + 2 * PAD, nz), jnp.float32)
    for a in range(4):
        for p in range(nx + 2 * REACH):
            q = p - REACH
            if 0 <= q < nx:
                v = own[a, q]
            elif -2 <= q < 0:
                v = before[2 * a + q + 2]
            elif nx <= q < nx + 2:
                v = behind[2 * a + q - nx]
            elif q == nx + 2 and a == 1:
                v = behind[8]
            else:
                ext[a, p] = empty
                continue
            ext[a, p, :PAD] = zero
            ext[a, p, PAD + ny :] = zero
            ext[a, p, PAD : PAD + ny] = v
    for (even, keep), r in zip(side("gy"), (PAD - 2, PAD + ny)):
        lines[...] = keep * jnp.where(even, o0[...], o1[...])
        for p in range(nx + 4):
            for a in range(4):
                at = (a * (nx + 4) + p) * 2
                ext[a, 1 + p, r : r + 2] = lines[at : at + 2]
            if r > PAD:
                at = 8 * (nx + 4) + p
                ext[2, 1 + p, r + 2 : r + 3] = lines[at : at + 1]
    lane = iota((ny + 2 * PAD, nz), 1)
    for p in range(nx + 4):
        packed = ext[0, 1 + p]
        for a in range(1, 4):
            first = jnp.where(gz == 0, nz - 3 - 3 * a, 3 * a)
            moved = pltpu.roll(ext[a, 1 + p], jnp.where(gz == 0, nz - 3 * a, 3 * a), 1)
            packed = jnp.where((lane >= first) & (lane < first + 3), moved, packed)
        edge[p] = packed


def fine_kernel(local, edges, t_out, k_out, m_out, ext, e1, rd, dg, e2, rows):
    nx, ny, half = t_out.shape
    nz = 2 * half
    gx, gy, gz = lax.axis_index("gx"), lax.axis_index("gy"), lax.axis_index("gz")
    spot = iota((ny + 2 * PAD, half), 1)
    given = jnp.logical_or((gz == 0) & (spot < 3), (gz == 1) & (spot >= half - 3))
    for p in range(nx + 2 * REACH):
        for a in range(4):
            ext[a, p, :, :half] = local[a, p]
            if 1 <= p < nx + 5:
                v = edges[p - 1]
                if a > 0:
                    v = pltpu.roll(v, jnp.where(gz == 0, half - 3 * a, 3 * a), 1)
                ext[a, p, :, half:] = jnp.where(given, v, 0.0)
            else:
                ext[a, p, :, half:] = jnp.zeros((ny + 2 * PAD, half), jnp.float32)
    shape = (ny + 2 * PAD, nz)
    row, lane = iota(shape, 0), iota(shape, 1)
    inner_z = jnp.logical_or(lane > 0, gz > 0)
    in_y = jnp.logical_and(
        jnp.logical_or(gy > 0, row >= PAD),
        jnp.logical_or(gy < lax.axis_size("gy") - 1, row < PAD + ny),
    )

    def off(e, p):
        fy, fz = ext[2, p], jnp.where(inner_z, ext[3, p], 0.0)
        here = e[p]
        total = ext[1, p] * e[p - 1] + ext[1, p + 1] * e[p + 1]
        total = total + fy * down(here, 0) + up(fy * here, 0)
        return total + fz * down(here, 1) + up(fz * here, 1)

    for p in range(1, nx + 2 * REACH - 1):
        fy, fz = ext[2, p], ext[3, p]
        diagonal = ext[1, p] + ext[1, p + 1] + fy + up(fy, 0) + fz + up(jnp.where(inner_z, fz, 0.0), 1)
        inv = inverse(diagonal)
        dg[p], rd[p] = diagonal, inv
        e1[p] = ext[0, p] * inv
    for p in range(2, nx + 2 * REACH - 2):
        value = (2.0 - damping) * e1[p] + rd[p] * off(e1, p)
        inside = in_y
        if p < REACH:
            inside = jnp.logical_and(inside, gx > 0)
        if p >= REACH + nx:
            inside = jnp.logical_and(inside, gx < lax.axis_size("gx") - 1)
        e2[p] = jnp.where(inside, value, 0.0)

    def mine(v):
        return v[PAD : PAD + ny, :half]

    sums = []
    for i in range(nx):
        p = REACH + i
        q = ext[0, p] - dg[p] * e2[p] + off(e2, p)
        fy, fz = ext[2, p], jnp.where(inner_z, ext[3, p], 0.0)
        inv = rd[p]
        t_out[i] = mine(e2[p] + inv * q)
        for n, k in enumerate((ext[1, p], ext[1, p + 1], fy, up(fy, 0), fz, up(fz, 1))):
            k_out[n, i] = mine(inv * k)
        sums.append(mine(q))
    def face(d, i):
        return 0.5 * ext[d, REACH + i, PAD : PAD + ny, :half]

    pairs = range(0, nx, 2)
    fine, coarse = iota((half, half), 0), iota((half, half), 1)
    both_low, both_high = chosen(fine // 2 == coarse), chosen(fine // 2 + half // 2 == coarse)
    even_high = chosen(fine + half == 2 * coarse)
    count = len(pairs) * ny
    rows[:count] = select_dot(jnp.concatenate([sums[i] + sums[i + 1] for i in pairs], 0), both_low) + select_dot(
        jnp.concatenate([face(1, i) for i in pairs], 0), both_high
    )
    rows[count:] = select_dot(jnp.concatenate([face(2, i) + face(2, i + 1) for i in pairs], 0), both_low) + select_dot(
        jnp.concatenate([face(3, i) + face(3, i + 1) for i in pairs], 0), even_high
    )
    part = count // 2
    even = rows[pl.ds(0, 2 * part, stride=2)]
    odd = rows[pl.ds(1, 2 * part, stride=2)]
    spot = iota((part, half), 1)
    m_out[0] = (even[:part] + odd[:part]).reshape(m_out.shape[1:])
    m_out[1] = (even[part:] + jnp.where(spot < half // 2, 0.0, odd[part:])).reshape(m_out.shape[1:])


def planes_of(ref):
    return [ref[p] for p in range(ref.shape[0])]


def level_parts(fx, fy, fz):
    shape = fy[0].shape
    row, lane = iota(shape, 0), iota(shape, 1)
    n = len(fx)
    zero = jnp.zeros(shape, jnp.float32)
    fym = [jnp.where(row > 0, v, 0.0) for v in fy]
    fzm = [jnp.where(lane > 0, v, 0.0) for v in fz]
    high = [fx[p + 1] if p + 1 < n else zero for p in range(n)]
    diagonal = [fx[p] + high[p] + fy[p] + up(fym[p], 0) + fz[p] + up(fzm[p], 1) for p in range(n)]

    def off(e):
        result = []
        for p in range(n):
            total = fym[p] * down(e[p], 0) + up(fym[p] * e[p], 0)
            total = total + fzm[p] * down(e[p], 1) + up(fzm[p] * e[p], 1)
            if p > 0:
                total = total + fx[p] * e[p - 1]
            if p + 1 < n:
                total = total + fx[p + 1] * e[p + 1]
            result.append(total)
        return result

    return diagonal, [inverse(d) for d in diagonal], off


def before(b, diagonal, inv, off):
    e1 = [v * r for v, r in zip(b, inv)]
    e2 = [(2.0 - damping) * e + r * o for e, r, o in zip(e1, inv, off(e1))]
    q = [v - d * e + o for v, d, e, o in zip(b, diagonal, e2, off(e2))]
    return [e + r * v for e, r, v in zip(e2, inv, q)], q


def after(t, c, inv, off):
    return [v + (1.0 - damping) * k + r * o for v, k, r, o in zip(t, c, inv, off(c))]


def coarse_operator(fx, fy, fz, depth):
    row, lane = iota(fx.shape, 0), iota(fx.shape, 1)
    fxm = jnp.where(lane >= depth, fx, 0.0)
    fym = jnp.where(row > 0, fy, 0.0)
    fzm = jnp.where(lane % depth > 0, fz, 0.0)
    wide = fx.shape[1]

    def up_x(v):
        return pltpu.roll(v, wide - depth, 1)

    hx, hy, hz = up_x(fxm), up(fym, 0), up(fzm, 1)
    diagonal = (fx + hx) + (fy + hy) + (fz + hz)

    def operate_packed(v):
        along_x = fxm * pltpu.roll(v, depth, 1) + hx * up_x(v)
        along_y = fym * down(v, 0) + hy * up(v, 0)
        along_z = fzm * down(v, 1) + hz * up(v, 1)
        return (diagonal * v - along_y) - (along_x + along_z)

    return operate_packed


def coarse_solution(rhs, operate_packed):
    def total(v):
        v = jnp.broadcast_to(jnp.sum(v, axis=1, keepdims=True), v.shape)
        for shift in (4, 2, 1):
            v = v + pltpu.roll(v, shift, 0)
        return v

    remain, search = rhs, rhs
    image = operate_packed(rhs)
    norm_now, energy = total(rhs * rhs), total(rhs * image)
    alpha = norm_now / energy
    solution = alpha * search
    for step in range(COARSE_ITERS - 1):
        inverse_norm = 1.0 / norm_now
        remain = remain - alpha * image
        across = operate_packed(remain)
        norm_next, own, mixed = total(remain * remain), total(remain * across), total(remain * image)
        beta = norm_next * inverse_norm
        energy = own + beta * (2.0 * mixed + beta * energy)
        search = remain + beta * search
        image = across + beta * image
        norm_now = norm_next
        alpha = norm_now / energy
        solution = solution + alpha * search
    return solution


def mirrored(k, count):
    result = 0
    while count > 1:
        result, k, count = 2 * result + k % 2, k // 2, count // 2
    return result


def whole_kernel(here, there, t_in, k_in, out, grid, fold1, folds1, fold2, folds2, spread2, held2, spread1, kept, doubled):
    gx, gy, gz = lax.axis_index("gx"), lax.axis_index("gy"), lax.axis_index("gz")
    cx, cy = lax.axis_size("gx"), lax.axis_size("gy")
    bx, by = here.shape[2], here.shape[3]
    w1 = here.shape[4]
    for k in range(cx * cy):
        x = jnp.bitwise_xor(gx, k % cx) * bx
        y = pl.multiple_of(jnp.bitwise_xor(gy, k // cx) * by, by)
        other = mirrored(k % cx, cx) + k // cx * cx
        for a in range(2):
            low = jnp.where(gz == 0, here[k, a], there[k, a]).reshape(bx * by, w1)
            top = jnp.where(gz == 0, there[other, a], here[other, a]).reshape(bx * by, w1)
            left = iota((bx * by, w1), 1) < w1 // 2
            one = jnp.where(left, low, pltpu.roll(top, w1 // 2, 1))
            two = jnp.where(left, pltpu.roll(low, w1 // 2, 1), top)
            spot = (pl.ds(x + 2, bx), pl.ds(y + TILE, by))
            grid[(2 * a, *spot)] = one.reshape(bx, by, w1)
            grid[(2 * a + 1, *spot)] = two.reshape(bx, by, w1)
    n1, m1 = cx * bx, cy * by
    inner = slice(TILE, TILE + m1)
    for ref in (grid.at[1], grid.at[2], grid.at[3], kept.at[0], kept.at[1]):
        for p in range(n1 + 4):
            if p < 2 or p >= n1 + 2:
                ref[p] = jnp.zeros((m1 + 2 * TILE, w1), jnp.float32)
            else:
                ref[p, :TILE] = jnp.zeros((TILE, w1), jnp.float32)
                ref[p, TILE + m1 :] = jnp.zeros((TILE, w1), jnp.float32)
    b1, fx1, fy1, fz1 = ([grid[a, 2 + p, inner] for p in range(n1)] for a in range(4))
    n2, m2 = n1 // 2, m1 // 2
    half = n2 * m2
    pairs = range(0, n1, 2)
    folds1[...] = jnp.concatenate(
        [0.5 * fx1[i] for i in pairs]
        + [0.5 * (fy1[i] + fy1[i + 1]) for i in pairs]
        + [0.5 * (fz1[i] + fz1[i + 1]) for i in pairs],
        0,
    )
    fine, coarse = iota((w1, w1), 0), iota((w1, w1), 1)
    both1, even = chosen(fine // 2 == coarse), chosen(fine == 2 * coarse)
    low, top = folds1[pl.ds(0, 3 * half, stride=2)], folds1[pl.ds(1, 3 * half, stride=2)]
    summed = select_dot(jnp.concatenate([low[:half] + top[:half], low[half : 2 * half]], 0), both1)

    def part(v):
        return [v[p * m2 : (p + 1) * m2] for p in range(n2)]

    fx2, fy2 = part(summed[:half]), part(summed[half:])
    fz2 = part(select_dot(low[2 * half :] + top[2 * half :], even))
    diagonal1, inv1, off1 = level_parts(fx1, fy1, fz1)
    t1, q1 = before(b1, diagonal1, inv1, off1)
    for p in range(n1):
        kept[0, 2 + p, inner] = t1[p]
        kept[1, 2 + p, inner] = inv1[p]
    diagonal2, inv2, off2 = level_parts(fx2, fy2, fz2)

    n3, m3 = n2 // 2, m2 // 2
    depth = w1 // n3
    fine, coarse = iota((n3 * w1, w1), 0), iota((n3 * w1, w1), 1)
    block, fine = fine // w1, fine % w1
    both2 = chosen((fine // 2 + block * depth == coarse) & (fine < 2 * depth))
    even = chosen((fine + 2 * block * depth == 2 * coarse) & (fine < 2 * depth))
    blocks = range(0, n2, 2)
    wide = [
        jnp.concatenate([0.5 * fx2[i] for i in blocks], 1),
        jnp.concatenate([0.5 * (fy2[i] + fy2[i + 1]) for i in blocks], 1),
    ]
    thin = jnp.concatenate([0.5 * (fz2[i] + fz2[i + 1]) for i in blocks], 1)
    folds2[: 2 * m2] = select_dot(jnp.concatenate(wide, 0), both2)
    folds2[2 * m2 :] = select_dot(thin, even)
    low, top = folds2[pl.ds(0, 3 * m3, stride=2)], folds2[pl.ds(1, 3 * m3, stride=2)]
    operate3 = coarse_operator(low[:m3] + top[:m3], low[m3 : 2 * m3], low[2 * m3 :] + top[2 * m3 :], depth)

    fold1[...] = jnp.concatenate([q1[i] + q1[i + 1] for i in pairs], 0)
    b2 = part(select_dot(fold1[pl.ds(0, half, stride=2)] + fold1[pl.ds(1, half, stride=2)], both1))
    t2, q2 = before(b2, diagonal2, inv2, off2)
    fold2[...] = select_dot(jnp.concatenate([q2[i] + q2[i + 1] for i in blocks], 1), both2)
    c3 = coarse_solution(fold2[pl.ds(0, m3, stride=2)] + fold2[pl.ds(1, m3, stride=2)], operate3)

    fine, coarse = iota((w1, n3 * w1), 1), iota((w1, n3 * w1), 0)
    block, fine = fine // w1, fine % w1
    row = select_dot(c3, chosen((fine // 2 + block * depth == coarse) & (fine < 2 * depth)))
    for i in range(n3):
        spread2[pl.ds(i * m2, m3, stride=2)] = row[:, i * w1 : (i + 1) * w1]
        spread2[pl.ds(i * m2 + 1, m3, stride=2)] = row[:, i * w1 : (i + 1) * w1]
    up2 = [spread2[(p // 2) * m2 : (p // 2 + 1) * m2] for p in range(n2)]
    c2 = after(t2, up2, inv2, off2)

    held2[0] = jnp.zeros((m2, w1), jnp.float32)
    held2[n2 + 1] = jnp.zeros((m2, w1), jnp.float32)
    for p in range(n2):
        held2[1 + p] = c2[p]
    few = bx // 2 + 2
    near = held2[pl.ds(gx * (bx // 2), few)].reshape(few * m2, w1)
    fine, coarse = iota((w1, w1), 1), iota((w1, w1), 0)
    row = select_dot(near, chosen(fine // 2 == coarse))
    for p in range(few):
        spread1[p, :TILE] = jnp.zeros((TILE, w1), jnp.float32)
        spread1[p, TILE + m1 :] = jnp.zeros((TILE, w1), jnp.float32)
        spread1[p, pl.ds(TILE, m2, stride=2)] = row[p * m2 : (p + 1) * m2]
        spread1[p, pl.ds(TILE + 1, m2, stride=2)] = row[p * m2 : (p + 1) * m2]
    tall = by + 2 * TILE
    rows = pl.ds(pl.multiple_of(gy * by, by), tall)
    inner_z = iota((tall, w1), 1) > 0
    up1 = [spread1[p, rows] for p in range(few)]
    near = []
    for p in range(1, bx + 3):
        x = gx * bx + p
        e = up1[p // 2]
        fy, fz = grid[2, x, rows], jnp.where(inner_z, grid[3, x, rows], 0.0)
        total = grid[1, x, rows] * up1[(p - 1) // 2] + grid[1, x + 1, rows] * up1[(p + 1) // 2]
        total = total + fy * down(e, 0) + up(fy * e, 0) + fz * down(e, 1) + up(fz * e, 1)
        value = kept[0, x, rows] + (1.0 - damping) * e + kept[1, x, rows] * total
        near.append(value[TILE - 1 : TILE - 1 + by + TILE])
    tall = by + TILE
    spot = gz * t_in.shape[2] + iota((w1, 3 * w1), 1) % w1 + (iota((w1, 3 * w1), 1) // w1 + 1) % 3 - 1
    wanted = iota((w1, 3 * w1), 0)
    row = select_dot(jnp.concatenate(near, 0), chosen((2 * wanted == spot) | (2 * wanted + 1 == spot)))
    for s in range(3):
        doubled[s, pl.ds(0, (bx + 2) * tall, stride=2)] = row[:, s * w1 : (s + 1) * w1]
        doubled[s, pl.ds(1, (bx + 2) * tall, stride=2)] = row[:, s * w1 : (s + 1) * w1]
    ny = t_in.shape[1]

    def at(s, i, shift):
        first = (1 + i // 2) * 2 * tall + 2 + shift
        return doubled[s, first : first + ny]

    for i in range(t_in.shape[0]):
        value = t_in[i] + (1.0 - damping) * at(0, i, 0)
        value = value + k_in[0, i] * at(0, i - 1, 0) + k_in[1, i] * at(0, i + 1, 0)
        value = value + k_in[2, i] * at(0, i, -1) + k_in[3, i] * at(0, i, 1)
        out[i] = value + k_in[4, i] * at(2, i, 0) + k_in[5, i] * at(1, i, 0)


def traded(blocks, axis):
    count, cores = lax.axis_size(axis), lax.axis_size("gz")
    taken = []
    for kind, block in enumerate(blocks):
        route = []
        for i in range(count):
            other = i + 1 if (i + kind) % 2 == 0 else i - 1
            for c in range(cores):
                to = other * cores + c if 0 <= other < count else i * cores + cores - 1 - c
                route.append((i * cores + c, to))
        taken.append(lax.ppermute(block, (axis, "gz"), route))
    return taken


def gathered(block, axis):
    count = lax.axis_size(axis)
    parts = [lax.ppermute(block, axis, [(i, i ^ k) for i in range(count)]) for k in range(1, count)]
    return jnp.concatenate([block] + parts, 0)


def doubled_over(block, axis):
    count, cores = lax.axis_size(axis), lax.axis_size("gz")
    steps = [1 << n for n in range(count.bit_length() - 1)]
    for up_step, down_step in zip(steps, reversed(steps)):
        route = [(i * cores + c, (i ^ (down_step if c else up_step)) * cores + c) for i in range(count) for c in range(cores)]
        block = jnp.concatenate([block, lax.ppermute(block, (axis, "gz"), route)], 0)
    return block


def f32(*shape):
    return jax.ShapeDtypeStruct(shape, jnp.float32)


def per_device_small(adjoint_residual, face_x, face_y, face_z):
    nx, ny, nz = adjoint_residual.shape
    near = [pltpu.VMEM((9, ny, nz), jnp.float32)] * 2
    own = jnp.stack((adjoint_residual, face_x, face_y, face_z))
    slabs = pl.pallas_call(
        x_kernel,
        out_shape=(f32(9, ny, nz), f32(9, ny, nz)),
        compiler_params=PARAMS,
        name="slabs_x",
    )(own)
    slabs = traded(slabs, "gx")
    count = -(-9 * (nx + 4) // 8) * 8
    lines = pl.pallas_call(
        y_kernel,
        out_shape=(f32(count, nz), f32(count, nz)),
        scratch_shapes=near,
        compiler_params=PARAMS,
        name="slabs_y",
    )(own, *slabs)
    lines = traded(lines, "gy")
    local, edge = pl.pallas_call(
        z_kernel,
        out_shape=(f32(4, nx + 2 * REACH, ny + 2 * PAD, nz), f32(nx + 4, ny + 2 * PAD, nz)),
        scratch_shapes=near + [pltpu.VMEM((count, nz), jnp.float32)],
        compiler_params=PARAMS,
        name="edges_z",
    )(own, *slabs, *lines)
    edges = lax.ppermute(edge, "gz", [(0, 1), (1, 0)])
    ext_x, ext_y, wide = nx + 2 * REACH, ny + 2 * PAD, 2 * nz
    field = pltpu.VMEM((ext_x, ext_y, wide), jnp.float32)
    t, k, m = pl.pallas_call(
        fine_kernel,
        out_shape=(f32(nx, ny, nz), f32(6, nx, ny, nz), f32(2, nx // 2, ny // 2, nz)),
        scratch_shapes=[
            pltpu.VMEM((4, ext_x, ext_y, wide), jnp.float32),
            field,
            field,
            field,
            field,
            pltpu.VMEM((nx * ny, nz), jnp.float32),
        ],
        compiler_params=PARAMS,
        name="fine",
    )(local, edges)
    here = gathered(doubled_over(m[None], "gx"), "gy")
    there = lax.ppermute(here, "gz", [(0, 1), (1, 0)])
    n1, m1 = here.shape[2] * lax.axis_size("gx"), here.shape[3] * lax.axis_size("gy")
    n2, m2 = n1 // 2, m1 // 2
    tall = (nx // 2 + 2) * (ny // 2 + TILE)
    return pl.pallas_call(
        whole_kernel,
        out_shape=f32(nx, ny, nz),
        scratch_shapes=[
            pltpu.VMEM((4, n1 + 4, m1 + 2 * TILE, nz), jnp.float32),
            pltpu.VMEM((n2 * m1, nz), jnp.float32),
            pltpu.VMEM((3 * n2 * m1, nz), jnp.float32),
            pltpu.VMEM((m2, nz), jnp.float32),
            pltpu.VMEM((3 * m2, nz), jnp.float32),
            pltpu.VMEM((n1 * m1 // 8, nz), jnp.float32),
            pltpu.VMEM((n2 + 2, m2, nz), jnp.float32),
            pltpu.VMEM((nx // 4 + 2, m1 + 2 * TILE, nz), jnp.float32),
            pltpu.VMEM((2, n1 + 4, m1 + 2 * TILE, nz), jnp.float32),
            pltpu.VMEM((3, 2 * tall, nz), jnp.float32),
        ],
        compiler_params=PARAMS,
        name="whole",
    )(here, there, t, k)


def extended(block, sides, width):
    for axis, dim in sides:
        count = lax.axis_size(axis)
        forward = [(i, i + 1) for i in range(count - 1)]
        backward = [(target, source) for source, target in forward]
        low = lax.ppermute(
            lax.slice_in_dim(block, block.shape[dim] - width, None, axis=dim), axis, forward
        )
        high = lax.ppermute(lax.slice_in_dim(block, 0, width, axis=dim), axis, backward)
        block = jnp.concatenate([low, block, high], axis=dim)
    return block


def from_behind(block, axis, distance):
    devices = range(lax.axis_size(axis))
    route = [(i - distance, i) for i in devices if i - distance in devices]
    return lax.ppermute(block, axis, route)


def stencil(padded, field, coefs):
    low_x, high_x, low_y, high_y, low_z, high_z = coefs
    diagonal = low_x + high_x + low_y + high_y + low_z + high_z
    result = diagonal * field - low_x * padded[:-2, 1:-1, 1:-1] - high_x * padded[2:, 1:-1, 1:-1]
    result = result - low_y * padded[1:-1, :-2, 1:-1] - high_y * padded[1:-1, 2:, 1:-1]
    return result - low_z * padded[1:-1, 1:-1, :-2] - high_z * padded[1:-1, 1:-1, 2:]


def operate(field, coefs):
    padded = extended(field, (("gx", 0), ("gy", 1), ("gz", 2)), 1)
    return stencil(padded, field, coefs)


def operate_whole(field, coefs):
    return stencil(jnp.pad(field, 1), field, coefs)


def blocked(values):
    return values.reshape(values.shape[0] // 2, 2, values.shape[1] // 2, 2, values.shape[2] // 2, 2)


def coarse_face(values, dim, parity):
    others = tuple((2 * k + 1 for k in range(3) if k != dim))
    summed = jnp.sum(blocked(values), axis=others)
    return 0.5 * lax.index_in_dim(summed, parity, dim + 1, keepdims=False)


def coarsen(coefs):
    result = []
    for dim in range(3):
        result.append(coarse_face(coefs[2 * dim], dim, 0))
        result.append(coarse_face(coefs[2 * dim + 1], dim, 1))
    return tuple(result)


def restrict(values):
    return jnp.sum(blocked(values), axis=(1, 3, 5))


def prolong(values):
    shape_out = (values.shape[0] * 2, values.shape[1] * 2, values.shape[2] * 2)
    wide = jnp.broadcast_to(
        values[:, None, :, None, :, None],
        (values.shape[0], 2, values.shape[1], 2, values.shape[2], 2),
    )
    return wide.reshape(shape_out)


def total_local(value):
    return value


def conj_grad(rhs, coefs, apply_op, total):
    solution = jnp.zeros_like(rhs)
    remain = rhs
    search = rhs
    norm_now = total(jnp.sum(remain * remain))
    for step in range(COARSE_ITERS):
        image = apply_op(search, coefs)
        alpha = norm_now / total(jnp.sum(search * image))
        solution = solution + alpha * search
        remain = remain - alpha * image
        norm_next = total(jnp.sum(remain * remain))
        search = remain + norm_next / norm_now * search
        norm_now = norm_next
    return solution


def coarse_solve(rhs, coefs):
    part_x, part_y, part_z = rhs.shape
    count_x = lax.axis_size("gx")
    count_y = lax.axis_size("gy")
    count_z = lax.axis_size("gz")
    stacked = jnp.stack((rhs,) + coefs)[None]
    whole = lax.all_gather(stacked, ("gx", "gy", "gz"), axis=0, tiled=True)
    whole = whole.reshape(count_x, count_y, count_z, 7, part_x, part_y, part_z)
    whole = whole.transpose(3, 0, 4, 1, 5, 2, 6).reshape(
        7, count_x * part_x, count_y * part_y, count_z * part_z
    )
    whole_coefs = tuple((whole[k] for k in range(1, 7)))
    solution = conj_grad(whole[0], whole_coefs, operate_whole, total_local)
    starts = (
        lax.axis_index("gx") * part_x,
        lax.axis_index("gy") * part_y,
        lax.axis_index("gz") * part_z,
    )
    return lax.dynamic_slice(solution, starts, (part_x, part_y, part_z))


def cycle(rhs, levels_left, coefs):
    if levels_left == 1:
        return coarse_solve(rhs, coefs)
    diagonal = coefs[0] + coefs[1] + coefs[2] + coefs[3] + coefs[4] + coefs[5]
    field = damping * rhs / diagonal
    field = field + damping * (rhs - operate(field, coefs)) / diagonal
    remain = rhs - operate(field, coefs)
    field = field + prolong(cycle(restrict(remain), levels_left - 1, coarsen(coefs)))
    field = field + damping * (rhs - operate(field, coefs)) / diagonal
    return field


def per_device(adjoint_residual, face_x, face_y, face_z):
    rim_x = from_behind(face_x[:1], "gx", -1)
    rim_y = from_behind(face_y[:, :1], "gy", -1)
    rim_z = from_behind(face_z[:, :, :1], "gz", -1)
    high_x = jnp.concatenate([face_x[1:], rim_x], 0)
    high_y = jnp.concatenate([face_y[:, 1:], rim_y], 1)
    high_z = jnp.concatenate([face_z[:, :, 1:], rim_z], 2)
    coefs = (face_x, high_x, face_y, high_y, face_z, high_z)
    return cycle(adjoint_residual, LEVELS, coefs)


def fits(mesh, shape):
    nx, ny, nz = shape
    cx, cy, cz = mesh.shape["gx"], mesh.shape["gy"], mesh.shape["gz"]
    powers = cx & (cx - 1) == 0 and cy & (cy - 1) == 0 and cz == 2
    blocks = nx % (8 * cx) == 0 and ny % (16 * cy) == 0 and nz == 256
    return powers and blocks and (nx // 8) * (nz // 8) == 128 and nx * ny * nz <= 2**19


def per_block(mesh, *args):
    counts = (mesh.shape["gx"], mesh.shape["gy"], mesh.shape["gz"])
    whole = tuple(n * c for n, c in zip(args[0].shape, counts))
    return (per_device_small if fits(mesh, whole) else per_device)(*args)


def solution(mesh):
    return jax.shard_map(
        functools.partial(per_block, mesh),
        mesh=mesh,
        in_specs=(
            P("gx", "gy", "gz"),
            P("gx", "gy", "gz"),
            P("gx", "gy", "gz"),
            P("gx", "gy", "gz"),
        ),
        out_specs=P("gx", "gy", "gz"),
        check_vma=False,
    )
```

```python
import functools

import jax
import jax.numpy as jnp
from jax import lax
from jax.experimental import pallas as pl
from jax.experimental.pallas import tpu as pltpu
from jax.sharding import PartitionSpec as P

LEVELS = 4
COARSE_ITERS = 6


damping = 2.0 / 3.0

REACH = 3
TILE = 8
PAD = 4
SMALL = pl.CostEstimate(flops=2**20, bytes_accessed=2**20, transcendentals=0)
PARAMS = pltpu.CompilerParams(vmem_limit_bytes=16 * 2**20)


def up(v, axis):
    return pltpu.roll(v, v.shape[axis] - 1, axis)


def down(v, axis):
    return pltpu.roll(v, 1, axis)


def iota(shape, axis):
    return lax.broadcasted_iota(jnp.int32, shape, axis)


def chosen(mask):
    return jnp.where(mask, 1.0, 0.0).astype(jnp.bfloat16)


def select_dot(values, matrix):
    count = values.shape[0]
    high = values.astype(jnp.bfloat16).astype(jnp.float32)
    rest = values - high
    mid = rest.astype(jnp.bfloat16).astype(jnp.float32)
    parts = jnp.concatenate([high, mid, rest - mid], 0).astype(jnp.bfloat16)
    product = jnp.dot(parts, matrix, preferred_element_type=jnp.float32)
    return (product[2 * count :] + product[count : 2 * count]) + product[:count]


def inverse(diagonal):
    return jnp.where(diagonal > 0.0, damping / jnp.where(diagonal > 0.0, diagonal, 1.0), 0.0)


def side(axis):
    here = lax.axis_index(axis)
    first = jnp.where(here > 0, 1.0, 0.0)
    last = jnp.where(here < lax.axis_size(axis) - 1, 1.0, 0.0)
    return (here % 2 == 1, first), (here % 2 == 0, last)


def x_kernel(own, *slabs):
    nx, gx = own.shape[1], lax.axis_index("gx")
    for kind, out in enumerate(slabs):
        start = jnp.where((gx + kind) % 2 == 0, nx - 2, 0)
        for a in range(4):
            for n in range(2):
                out[2 * a + n] = own[a, start + n]
        out[8] = own[1, 2]


def sides_x(slabs, before, behind):
    for (even, keep), out in zip(side("gx"), (before, behind)):
        for n in range(9):
            out[n] = keep * jnp.where(even, slabs[0][n], slabs[1][n])


def y_kernel(own, s0, s1, o0, o1, before, behind):
    nx, ny = own.shape[1], own.shape[2]
    gy = lax.axis_index("gy")
    sides_x((s0, s1), before, behind)
    for kind, out in enumerate((o0, o1)):
        ahead = (gy + kind) % 2 == 0
        for p in range(nx + 4):
            for a in range(4):
                if p < 2:
                    v = before[2 * a + p]
                elif p < nx + 2:
                    v = own[a, p - 2]
                else:
                    v = behind[2 * a + p - nx - 2]
                at = (a * (nx + 4) + p) * 2
                out[at : at + 2] = jnp.where(ahead, v[ny - 2 :], v[:2])
                if a == 2:
                    out[8 * (nx + 4) + p : 8 * (nx + 4) + p + 1] = v[2:3]
        used = 9 * (nx + 4)
        out[used:] = jnp.zeros((out.shape[0] - used, out.shape[1]), jnp.float32)


def z_kernel(own, s0, s1, o0, o1, ext, edge, before, behind, lines):
    nx, ny, nz = own.shape[1:]
    gz = lax.axis_index("gz")
    sides_x((s0, s1), before, behind)
    zero = jnp.zeros((PAD, nz), jnp.float32)
    empty = jnp.zeros((ny + 2 * PAD, nz), jnp.float32)
    for a in range(4):
        for p in range(nx + 2 * REACH):
            q = p - REACH
            if 0 <= q < nx:
                v = own[a, q]
            elif -2 <= q < 0:
                v = before[2 * a + q + 2]
            elif nx <= q < nx + 2:
                v = behind[2 * a + q - nx]
            elif q == nx + 2 and a == 1:
                v = behind[8]
            else:
                ext[a, p] = empty
                continue
            ext[a, p, :PAD] = zero
            ext[a, p, PAD + ny :] = zero
            ext[a, p, PAD : PAD + ny] = v
    for (even, keep), r in zip(side("gy"), (PAD - 2, PAD + ny)):
        lines[...] = keep * jnp.where(even, o0[...], o1[...])
        for p in range(nx + 4):
            for a in range(4):
                at = (a * (nx + 4) + p) * 2
                ext[a, 1 + p, r : r + 2] = lines[at : at + 2]
            if r > PAD:
                at = 8 * (nx + 4) + p
                ext[2, 1 + p, r + 2 : r + 3] = lines[at : at + 1]
    lane = iota((ny + 2 * PAD, nz), 1)
    for p in range(nx + 4):
        packed = ext[0, 1 + p]
        for a in range(1, 4):
            first = jnp.where(gz == 0, nz - 3 - 3 * a, 3 * a)
            moved = pltpu.roll(ext[a, 1 + p], jnp.where(gz == 0, nz - 3 * a, 3 * a), 1)
            packed = jnp.where((lane >= first) & (lane < first + 3), moved, packed)
        edge[p] = packed


def fine_kernel(local, edges, faces, e_out, q_out, r_out, m_out, ext, e1, rd, dg, e2, rows):
    nx, ny, half = e_out.shape
    nz = 2 * half
    gx, gy, gz = lax.axis_index("gx"), lax.axis_index("gy"), lax.axis_index("gz")
    spot = iota((ny + 2 * PAD, half), 1)
    given = jnp.logical_or((gz == 0) & (spot < 3), (gz == 1) & (spot >= half - 3))
    for p in range(nx + 2 * REACH):
        for a in range(4):
            ext[a, p, :, :half] = local[a, p]
            if 1 <= p < nx + 5:
                v = edges[p - 1]
                if a > 0:
                    v = pltpu.roll(v, jnp.where(gz == 0, half - 3 * a, 3 * a), 1)
                ext[a, p, :, half:] = jnp.where(given, v, 0.0)
            else:
                ext[a, p, :, half:] = jnp.zeros((ny + 2 * PAD, half), jnp.float32)
    shape = (ny + 2 * PAD, nz)
    row, lane = iota(shape, 0), iota(shape, 1)
    inner_z = jnp.logical_or(lane > 0, gz > 0)
    in_y = jnp.logical_and(
        jnp.logical_or(gy > 0, row >= PAD),
        jnp.logical_or(gy < lax.axis_size("gy") - 1, row < PAD + ny),
    )

    def off(e, p):
        fy, fz = ext[2, p], jnp.where(inner_z, ext[3, p], 0.0)
        here = e[p]
        total = ext[1, p] * e[p - 1] + ext[1, p + 1] * e[p + 1]
        total = total + fy * down(here, 0) + up(fy * here, 0)
        return total + fz * down(here, 1) + up(fz * here, 1)

    for p in range(1, nx + 2 * REACH - 1):
        fy, fz = ext[2, p], ext[3, p]
        diagonal = ext[1, p] + ext[1, p + 1] + fy + up(fy, 0) + fz + up(jnp.where(inner_z, fz, 0.0), 1)
        inv = inverse(diagonal)
        dg[p], rd[p] = diagonal, inv
        e1[p] = ext[0, p] * inv
    for p in range(2, nx + 2 * REACH - 2):
        value = (2.0 - damping) * e1[p] + rd[p] * off(e1, p)
        inside = in_y
        if p < REACH:
            inside = jnp.logical_and(inside, gx > 0)
        if p >= REACH + nx:
            inside = jnp.logical_and(inside, gx < lax.axis_size("gx") - 1)
        e2[p] = jnp.where(inside, value, 0.0)

    def mine(v):
        return v[PAD : PAD + ny, :half]

    sums = []
    for i in range(nx):
        p = REACH + i
        q = mine(ext[0, p] - dg[p] * e2[p] + off(e2, p))
        e_out[i], q_out[i], r_out[i] = mine(e2[p]), q, mine(rd[p])
        sums.append(q)
    pairs = range(0, nx, 2)
    both_low = chosen(iota((half, half), 0) // 2 == iota((half, half), 1))
    rows[...] = select_dot(jnp.concatenate([sums[i] + sums[i + 1] for i in pairs], 0), both_low)
    part = rows.shape[0] // 2
    total = rows[pl.ds(0, part, stride=2)] + rows[pl.ds(1, part, stride=2)]
    m_out[0] = faces[0] + total.reshape(m_out.shape[1:])
    m_out[1] = faces[1]


def faces_kernel(own, out, rows):
    nx, ny, half = own.shape[1:]

    def face(d, i):
        return 0.5 * own[d, i]

    pairs = range(0, nx, 2)
    fine, coarse = iota((half, half), 0), iota((half, half), 1)
    both_low, both_high = chosen(fine // 2 == coarse), chosen(fine // 2 + half // 2 == coarse)
    even_high = chosen(fine + half == 2 * coarse)
    count = len(pairs) * ny
    rows[:count] = select_dot(jnp.concatenate([face(1, i) for i in pairs], 0), both_high)
    rows[count:] = select_dot(jnp.concatenate([face(2, i) + face(2, i + 1) for i in pairs], 0), both_low) + select_dot(
        jnp.concatenate([face(3, i) + face(3, i + 1) for i in pairs], 0), even_high
    )
    part = count // 2
    even = rows[pl.ds(0, 2 * part, stride=2)]
    odd = rows[pl.ds(1, 2 * part, stride=2)]
    spot = iota((part, half), 1)
    out[0] = (even[:part] + odd[:part]).reshape(out.shape[1:])
    out[1] = (even[part:] + jnp.where(spot < half // 2, 0.0, odd[part:])).reshape(out.shape[1:])


def sweep_kernel(local, edges, e_in, q_in, r_in, t_out, k_out, *matrices):
    nx, ny, half = t_out.shape
    gz = lax.axis_index("gz")
    lane = iota((ny, half), 1)
    low_z, top_z = jnp.logical_or(lane > 0, gz > 0), lane < half - 1
    keep = jnp.where(gz == 0, 1.0, 0.0)
    inner = slice(PAD, PAD + ny)
    for i in range(nx):
        p, inv = REACH + i, r_in[i]
        fz = local[3, p, inner]
        far = keep * pltpu.roll(edges[p - 1, inner], half - 1 - 9, 1)
        high_z = jnp.where(top_z, up(fz, 1), far)
        faces = (local[1, p, inner], local[1, p + 1, inner], local[2, p, inner], local[2, p, PAD + 1 : PAD + 1 + ny])
        t_out[i] = e_in[i] + inv * q_in[i]
        for n, k in enumerate(faces + (jnp.where(low_z, fz, 0.0), high_z)):
            k_out[n, i] = inv * k
    both1, even1, both2, even2, spread3, spread2, last = matrices
    fine, coarse = iota(both1.shape, 0), iota(both1.shape, 1)
    both1[...], even1[...] = chosen(fine // 2 == coarse), chosen(fine == 2 * coarse)
    spread2[...] = chosen(coarse // 2 == fine)
    blocks = both2.shape[0] // half
    depth = half // blocks
    fine, coarse = iota(both2.shape, 0), iota(both2.shape, 1)
    block, fine = fine // half, fine % half
    valid = fine < 2 * depth
    both2[...] = chosen((fine // 2 + block * depth == coarse) & valid)
    even2[...] = chosen((fine + 2 * block * depth == 2 * coarse) & valid)
    fine, coarse = iota(spread3.shape, 1), iota(spread3.shape, 0)
    block, fine = fine // half, fine % half
    spread3[...] = chosen((fine // 2 + block * depth == coarse) & (fine < 2 * depth))
    spot = gz * half + iota(last.shape, 1) % half + (iota(last.shape, 1) // half + 1) % 3 - 1
    wanted = iota(last.shape, 0)
    last[...] = chosen((2 * wanted == spot) | (2 * wanted + 1 == spot))


def planes_of(ref):
    return [ref[p] for p in range(ref.shape[0])]


def level_parts(fx, fy, fz):
    shape = fy[0].shape
    row, lane = iota(shape, 0), iota(shape, 1)
    n = len(fx)
    zero = jnp.zeros(shape, jnp.float32)
    fym = [jnp.where(row > 0, v, 0.0) for v in fy]
    fzm = [jnp.where(lane > 0, v, 0.0) for v in fz]
    high = [fx[p + 1] if p + 1 < n else zero for p in range(n)]
    diagonal = [fx[p] + high[p] + fy[p] + up(fym[p], 0) + fz[p] + up(fzm[p], 1) for p in range(n)]

    def off(e):
        result = []
        for p in range(n):
            total = fym[p] * down(e[p], 0) + up(fym[p] * e[p], 0)
            total = total + fzm[p] * down(e[p], 1) + up(fzm[p] * e[p], 1)
            if p > 0:
                total = total + fx[p] * e[p - 1]
            if p + 1 < n:
                total = total + fx[p + 1] * e[p + 1]
            result.append(total)
        return result

    return diagonal, [inverse(d) for d in diagonal], off


def before(b, diagonal, inv, off):
    e1 = [v * r for v, r in zip(b, inv)]
    e2 = [(2.0 - damping) * e + r * o for e, r, o in zip(e1, inv, off(e1))]
    q = [v - d * e + o for v, d, e, o in zip(b, diagonal, e2, off(e2))]
    return [e + r * v for e, r, v in zip(e2, inv, q)], q


def after(t, c, inv, off):
    return [v + (1.0 - damping) * k + r * o for v, k, r, o in zip(t, c, inv, off(c))]


def coarse_operator(fx, fy, fz, depth):
    row, lane = iota(fx.shape, 0), iota(fx.shape, 1)
    fxm = jnp.where(lane >= depth, fx, 0.0)
    fym = jnp.where(row > 0, fy, 0.0)
    fzm = jnp.where(lane % depth > 0, fz, 0.0)
    wide = fx.shape[1]

    def up_x(v):
        return pltpu.roll(v, wide - depth, 1)

    hx, hy, hz = up_x(fxm), up(fym, 0), up(fzm, 1)
    diagonal = (fx + hx) + (fy + hy) + (fz + hz)

    def operate_packed(v):
        along_x = fxm * pltpu.roll(v, depth, 1) + hx * up_x(v)
        along_y = fym * down(v, 0) + hy * up(v, 0)
        along_z = fzm * down(v, 1) + hz * up(v, 1)
        return (diagonal * v - along_y) - (along_x + along_z)

    return operate_packed


def coarse_solution(rhs, operate_packed):
    def total(v):
        v = jnp.broadcast_to(jnp.sum(v, axis=1, keepdims=True), v.shape)
        for shift in (4, 2, 1):
            v = v + pltpu.roll(v, shift, 0)
        return v

    remain, search = rhs, rhs
    image = operate_packed(rhs)
    norm_now, energy = total(rhs * rhs), total(rhs * image)
    alpha = norm_now / energy
    solution = alpha * search
    for step in range(COARSE_ITERS - 1):
        inverse_norm = 1.0 / norm_now
        remain = remain - alpha * image
        across = operate_packed(remain)
        norm_next, own, mixed = total(remain * remain), total(remain * across), total(remain * image)
        beta = norm_next * inverse_norm
        energy = own + beta * (2.0 * mixed + beta * energy)
        search = remain + beta * search
        image = across + beta * image
        norm_now = norm_next
        alpha = norm_now / energy
        solution = solution + alpha * search
    return solution


def mirrored(k, count):
    result = 0
    while count > 1:
        result, k, count = 2 * result + k % 2, k // 2, count // 2
    return result


def whole_kernel(*refs):
    count = lax.axis_size("gy")
    here, there = refs[:count], refs[count : 2 * count]
    t_in, k_in, both1, even1, both2, even2, spread3, spread21, last, out, grid, fold1, folds1, fold2, folds2, spread2, held2, spread1, kept, doubled = refs[2 * count :]
    gx, gy, gz = lax.axis_index("gx"), lax.axis_index("gy"), lax.axis_index("gz")
    cx, cy = lax.axis_size("gx"), lax.axis_size("gy")
    bx, by, w1 = here[0].shape[2:]
    for k in range(cx * cy):
        x = jnp.bitwise_xor(gx, k % cx) * bx
        y = pl.multiple_of(jnp.bitwise_xor(gy, k // cx) * by, by)
        mine, other, j = k % cx, mirrored(k % cx, cx), k // cx
        for a in range(2):
            low = jnp.where(gz == 0, here[j][mine, a], there[j][mine, a]).reshape(bx * by, w1)
            top = jnp.where(gz == 0, there[j][other, a], here[j][other, a]).reshape(bx * by, w1)
            left = iota((bx * by, w1), 1) < w1 // 2
            one = jnp.where(left, low, pltpu.roll(top, w1 // 2, 1))
            two = jnp.where(left, pltpu.roll(low, w1 // 2, 1), top)
            spot = (pl.ds(x + 2, bx), pl.ds(y + TILE, by))
            grid[(2 * a, *spot)] = one.reshape(bx, by, w1)
            grid[(2 * a + 1, *spot)] = two.reshape(bx, by, w1)
    n1, m1 = cx * bx, cy * by
    inner = slice(TILE, TILE + m1)
    for ref in (grid.at[1], grid.at[2], grid.at[3], kept.at[0], kept.at[1]):
        for p in range(n1 + 4):
            if p < 2 or p >= n1 + 2:
                ref[p] = jnp.zeros((m1 + 2 * TILE, w1), jnp.float32)
            else:
                ref[p, :TILE] = jnp.zeros((TILE, w1), jnp.float32)
                ref[p, TILE + m1 :] = jnp.zeros((TILE, w1), jnp.float32)
    b1, fx1, fy1, fz1 = ([grid[a, 2 + p, inner] for p in range(n1)] for a in range(4))
    n2, m2 = n1 // 2, m1 // 2
    half = n2 * m2
    pairs = range(0, n1, 2)
    folds1[...] = jnp.concatenate(
        [0.5 * fx1[i] for i in pairs]
        + [0.5 * (fy1[i] + fy1[i + 1]) for i in pairs]
        + [0.5 * (fz1[i] + fz1[i + 1]) for i in pairs],
        0,
    )
    low, top = folds1[pl.ds(0, 3 * half, stride=2)], folds1[pl.ds(1, 3 * half, stride=2)]
    summed = select_dot(jnp.concatenate([low[:half] + top[:half], low[half : 2 * half]], 0), both1[...])

    def part(v):
        return [v[p * m2 : (p + 1) * m2] for p in range(n2)]

    fx2, fy2 = part(summed[:half]), part(summed[half:])
    fz2 = part(select_dot(low[2 * half :] + top[2 * half :], even1[...]))
    diagonal1, inv1, off1 = level_parts(fx1, fy1, fz1)
    t1, q1 = before(b1, diagonal1, inv1, off1)
    for p in range(n1):
        kept[0, 2 + p, inner] = t1[p]
        kept[1, 2 + p, inner] = inv1[p]
    diagonal2, inv2, off2 = level_parts(fx2, fy2, fz2)

    n3, m3 = n2 // 2, m2 // 2
    depth = w1 // n3
    blocks = range(0, n2, 2)
    wide = [
        jnp.concatenate([0.5 * fx2[i] for i in blocks], 1),
        jnp.concatenate([0.5 * (fy2[i] + fy2[i + 1]) for i in blocks], 1),
    ]
    thin = jnp.concatenate([0.5 * (fz2[i] + fz2[i + 1]) for i in blocks], 1)
    folds2[: 2 * m2] = select_dot(jnp.concatenate(wide, 0), both2[...])
    folds2[2 * m2 :] = select_dot(thin, even2[...])
    low, top = folds2[pl.ds(0, 3 * m3, stride=2)], folds2[pl.ds(1, 3 * m3, stride=2)]
    operate3 = coarse_operator(low[:m3] + top[:m3], low[m3 : 2 * m3], low[2 * m3 :] + top[2 * m3 :], depth)

    fold1[...] = jnp.concatenate([q1[i] + q1[i + 1] for i in pairs], 0)
    b2 = part(select_dot(fold1[pl.ds(0, half, stride=2)] + fold1[pl.ds(1, half, stride=2)], both1[...]))
    t2, q2 = before(b2, diagonal2, inv2, off2)
    fold2[...] = select_dot(jnp.concatenate([q2[i] + q2[i + 1] for i in blocks], 1), both2[...])
    c3 = coarse_solution(fold2[pl.ds(0, m3, stride=2)] + fold2[pl.ds(1, m3, stride=2)], operate3)

    row = select_dot(c3, spread3[...])
    for i in range(n3):
        spread2[pl.ds(i * m2, m3, stride=2)] = row[:, i * w1 : (i + 1) * w1]
        spread2[pl.ds(i * m2 + 1, m3, stride=2)] = row[:, i * w1 : (i + 1) * w1]
    up2 = [spread2[(p // 2) * m2 : (p // 2 + 1) * m2] for p in range(n2)]
    c2 = after(t2, up2, inv2, off2)

    held2[0] = jnp.zeros((m2, w1), jnp.float32)
    held2[n2 + 1] = jnp.zeros((m2, w1), jnp.float32)
    for p in range(n2):
        held2[1 + p] = c2[p]
    few = bx // 2 + 2
    near = held2[pl.ds(gx * (bx // 2), few)].reshape(few * m2, w1)
    row = select_dot(near, spread21[...])
    for p in range(few):
        spread1[p, :TILE] = jnp.zeros((TILE, w1), jnp.float32)
        spread1[p, TILE + m1 :] = jnp.zeros((TILE, w1), jnp.float32)
        spread1[p, pl.ds(TILE, m2, stride=2)] = row[p * m2 : (p + 1) * m2]
        spread1[p, pl.ds(TILE + 1, m2, stride=2)] = row[p * m2 : (p + 1) * m2]
    tall = by + 2 * TILE
    rows = pl.ds(pl.multiple_of(gy * by, by), tall)
    inner_z = iota((tall, w1), 1) > 0
    up1 = [spread1[p, rows] for p in range(few)]
    near = []
    for p in range(1, bx + 3):
        x = gx * bx + p
        e = up1[p // 2]
        fy, fz = grid[2, x, rows], jnp.where(inner_z, grid[3, x, rows], 0.0)
        total = grid[1, x, rows] * up1[(p - 1) // 2] + grid[1, x + 1, rows] * up1[(p + 1) // 2]
        total = total + fy * down(e, 0) + up(fy * e, 0) + fz * down(e, 1) + up(fz * e, 1)
        value = kept[0, x, rows] + (1.0 - damping) * e + kept[1, x, rows] * total
        near.append(value[TILE - 1 : TILE - 1 + by + TILE])
    tall = by + TILE
    row = select_dot(jnp.concatenate(near, 0), last[...])
    for s in range(3):
        doubled[s, pl.ds(0, (bx + 2) * tall, stride=2)] = row[:, s * w1 : (s + 1) * w1]
        doubled[s, pl.ds(1, (bx + 2) * tall, stride=2)] = row[:, s * w1 : (s + 1) * w1]
    ny = t_in.shape[1]

    def at(s, i, shift):
        first = (1 + i // 2) * 2 * tall + 2 + shift
        return doubled[s, first : first + ny]

    for i in range(t_in.shape[0]):
        value = t_in[i] + (1.0 - damping) * at(0, i, 0)
        value = value + k_in[0, i] * at(0, i - 1, 0) + k_in[1, i] * at(0, i + 1, 0)
        value = value + k_in[2, i] * at(0, i, -1) + k_in[3, i] * at(0, i, 1)
        out[i] = value + k_in[4, i] * at(2, i, 0) + k_in[5, i] * at(1, i, 0)


def traded(blocks, axis):
    count, cores = lax.axis_size(axis), lax.axis_size("gz")
    taken = []
    for kind, block in enumerate(blocks):
        route = []
        for i in range(count):
            other = i + 1 if (i + kind) % 2 == 0 else i - 1
            for c in range(cores):
                to = other * cores + c if 0 <= other < count else i * cores + cores - 1 - c
                route.append((i * cores + c, to))
        taken.append(lax.ppermute(block, (axis, "gz"), route))
    return taken


def doubled_over(block, axis):
    count, cores = lax.axis_size(axis), lax.axis_size("gz")
    steps = [1 << n for n in range(count.bit_length() - 1)]
    for up_step, down_step in zip(steps, reversed(steps)):
        route = [(i * cores + c, (i ^ (down_step if c else up_step)) * cores + c) for i in range(count) for c in range(cores)]
        block = jnp.concatenate([block, lax.ppermute(block, (axis, "gz"), route)], 0)
    return block


def f32(*shape):
    return jax.ShapeDtypeStruct(shape, jnp.float32)


def per_device_small(adjoint_residual, face_x, face_y, face_z):
    nx, ny, nz = adjoint_residual.shape
    near = [pltpu.VMEM((9, ny, nz), jnp.float32)] * 2
    cy = lax.axis_size("gy")
    own = jnp.stack((adjoint_residual, face_x, face_y, face_z))
    slabs = pl.pallas_call(
        x_kernel,
        out_shape=(f32(9, ny, nz), f32(9, ny, nz)),
        compiler_params=PARAMS,
        name="slabs_x",
    )(own)
    slabs = traded(slabs, "gx")
    faces = pl.pallas_call(
        faces_kernel,
        out_shape=f32(2, nx // 2, ny // 2, nz),
        scratch_shapes=[pltpu.VMEM((nx * ny, nz), jnp.float32)],
        compiler_params=PARAMS,
        cost_estimate=SMALL,
        name="faces",
    )(own)
    count = -(-9 * (nx + 4) // 8) * 8
    lines = pl.pallas_call(
        y_kernel,
        out_shape=(f32(count, nz), f32(count, nz)),
        scratch_shapes=near,
        compiler_params=PARAMS,
        name="slabs_y",
    )(own, *slabs)
    lines = traded(lines, "gy")
    local, edge = pl.pallas_call(
        z_kernel,
        out_shape=(f32(4, nx + 2 * REACH, ny + 2 * PAD, nz), f32(nx + 4, ny + 2 * PAD, nz)),
        scratch_shapes=near + [pltpu.VMEM((count, nz), jnp.float32)],
        compiler_params=PARAMS,
        name="edges_z",
    )(own, *slabs, *lines)
    edges = lax.ppermute(edge, "gz", [(0, 1), (1, 0)])
    ext_x, ext_y, wide = nx + 2 * REACH, ny + 2 * PAD, 2 * nz
    field = pltpu.VMEM((ext_x, ext_y, wide), jnp.float32)
    e, q, r, m = pl.pallas_call(
        fine_kernel,
        out_shape=(f32(nx, ny, nz),) * 3 + (f32(2, nx // 2, ny // 2, nz),),
        scratch_shapes=[
            pltpu.VMEM((4, ext_x, ext_y, wide), jnp.float32),
            field,
            field,
            field,
            field,
            pltpu.VMEM((nx * ny // 2, nz), jnp.float32),
        ],
        compiler_params=PARAMS,
        name="fine",
    )(local, edges, faces)
    blocks = nx * lax.axis_size("gx") // 8
    shapes = ((nz, nz), (nz, nz), (blocks * nz, nz), (blocks * nz, nz), (nz, blocks * nz), (nz, nz), (nz, 3 * nz))
    t, k, *matrices = pl.pallas_call(
        sweep_kernel,
        out_shape=(f32(nx, ny, nz), f32(6, nx, ny, nz))
        + tuple(jax.ShapeDtypeStruct(shape, jnp.bfloat16) for shape in shapes),
        compiler_params=PARAMS,
        cost_estimate=SMALL,
        name="sweep",
    )(local, edges, e, q, r)
    near = doubled_over(m[None], "gx")
    here = [near] + [
        lax.ppermute(near, "gy", [(i, i ^ n) for i in range(cy)]) for n in range(1, cy)
    ]
    there = [lax.ppermute(block, "gz", [(0, 1), (1, 0)]) for block in here]
    n1, m1 = m.shape[1] * lax.axis_size("gx"), m.shape[2] * cy
    n2, m2 = n1 // 2, m1 // 2
    tall = (nx // 2 + 2) * (ny // 2 + TILE)
    return pl.pallas_call(
        whole_kernel,
        out_shape=f32(nx, ny, nz),
        scratch_shapes=[
            pltpu.VMEM((4, n1 + 4, m1 + 2 * TILE, nz), jnp.float32),
            pltpu.VMEM((n2 * m1, nz), jnp.float32),
            pltpu.VMEM((3 * n2 * m1, nz), jnp.float32),
            pltpu.VMEM((m2, nz), jnp.float32),
            pltpu.VMEM((3 * m2, nz), jnp.float32),
            pltpu.VMEM((n1 * m1 // 8, nz), jnp.float32),
            pltpu.VMEM((n2 + 2, m2, nz), jnp.float32),
            pltpu.VMEM((nx // 4 + 2, m1 + 2 * TILE, nz), jnp.float32),
            pltpu.VMEM((2, n1 + 4, m1 + 2 * TILE, nz), jnp.float32),
            pltpu.VMEM((3, 2 * tall, nz), jnp.float32),
        ],
        compiler_params=PARAMS,
        name="whole",
    )(*here, *there, t, k, *matrices)


def extended(block, sides, width):
    for axis, dim in sides:
        count = lax.axis_size(axis)
        forward = [(i, i + 1) for i in range(count - 1)]
        backward = [(target, source) for source, target in forward]
        low = lax.ppermute(
            lax.slice_in_dim(block, block.shape[dim] - width, None, axis=dim), axis, forward
        )
        high = lax.ppermute(lax.slice_in_dim(block, 0, width, axis=dim), axis, backward)
        block = jnp.concatenate([low, block, high], axis=dim)
    return block


def from_behind(block, axis, distance):
    devices = range(lax.axis_size(axis))
    route = [(i - distance, i) for i in devices if i - distance in devices]
    return lax.ppermute(block, axis, route)


def stencil(padded, field, coefs):
    low_x, high_x, low_y, high_y, low_z, high_z = coefs
    diagonal = low_x + high_x + low_y + high_y + low_z + high_z
    result = diagonal * field - low_x * padded[:-2, 1:-1, 1:-1] - high_x * padded[2:, 1:-1, 1:-1]
    result = result - low_y * padded[1:-1, :-2, 1:-1] - high_y * padded[1:-1, 2:, 1:-1]
    return result - low_z * padded[1:-1, 1:-1, :-2] - high_z * padded[1:-1, 1:-1, 2:]


def operate(field, coefs):
    padded = extended(field, (("gx", 0), ("gy", 1), ("gz", 2)), 1)
    return stencil(padded, field, coefs)


def operate_whole(field, coefs):
    return stencil(jnp.pad(field, 1), field, coefs)


def blocked(values):
    return values.reshape(values.shape[0] // 2, 2, values.shape[1] // 2, 2, values.shape[2] // 2, 2)


def coarse_face(values, dim, parity):
    others = tuple((2 * k + 1 for k in range(3) if k != dim))
    summed = jnp.sum(blocked(values), axis=others)
    return 0.5 * lax.index_in_dim(summed, parity, dim + 1, keepdims=False)


def coarsen(coefs):
    result = []
    for dim in range(3):
        result.append(coarse_face(coefs[2 * dim], dim, 0))
        result.append(coarse_face(coefs[2 * dim + 1], dim, 1))
    return tuple(result)


def restrict(values):
    return jnp.sum(blocked(values), axis=(1, 3, 5))


def prolong(values):
    shape_out = (values.shape[0] * 2, values.shape[1] * 2, values.shape[2] * 2)
    wide = jnp.broadcast_to(
        values[:, None, :, None, :, None],
        (values.shape[0], 2, values.shape[1], 2, values.shape[2], 2),
    )
    return wide.reshape(shape_out)


def total_local(value):
    return value


def conj_grad(rhs, coefs, apply_op, total):
    solution = jnp.zeros_like(rhs)
    remain = rhs
    search = rhs
    norm_now = total(jnp.sum(remain * remain))
    for step in range(COARSE_ITERS):
        image = apply_op(search, coefs)
        alpha = norm_now / total(jnp.sum(search * image))
        solution = solution + alpha * search
        remain = remain - alpha * image
        norm_next = total(jnp.sum(remain * remain))
        search = remain + norm_next / norm_now * search
        norm_now = norm_next
    return solution


def coarse_solve(rhs, coefs):
    part_x, part_y, part_z = rhs.shape
    count_x = lax.axis_size("gx")
    count_y = lax.axis_size("gy")
    count_z = lax.axis_size("gz")
    stacked = jnp.stack((rhs,) + coefs)[None]
    whole = lax.all_gather(stacked, ("gx", "gy", "gz"), axis=0, tiled=True)
    whole = whole.reshape(count_x, count_y, count_z, 7, part_x, part_y, part_z)
    whole = whole.transpose(3, 0, 4, 1, 5, 2, 6).reshape(
        7, count_x * part_x, count_y * part_y, count_z * part_z
    )
    whole_coefs = tuple((whole[k] for k in range(1, 7)))
    solution = conj_grad(whole[0], whole_coefs, operate_whole, total_local)
    starts = (
        lax.axis_index("gx") * part_x,
        lax.axis_index("gy") * part_y,
        lax.axis_index("gz") * part_z,
    )
    return lax.dynamic_slice(solution, starts, (part_x, part_y, part_z))


def cycle(rhs, levels_left, coefs):
    if levels_left == 1:
        return coarse_solve(rhs, coefs)
    diagonal = coefs[0] + coefs[1] + coefs[2] + coefs[3] + coefs[4] + coefs[5]
    field = damping * rhs / diagonal
    field = field + damping * (rhs - operate(field, coefs)) / diagonal
    remain = rhs - operate(field, coefs)
    field = field + prolong(cycle(restrict(remain), levels_left - 1, coarsen(coefs)))
    field = field + damping * (rhs - operate(field, coefs)) / diagonal
    return field


def per_device(adjoint_residual, face_x, face_y, face_z):
    rim_x = from_behind(face_x[:1], "gx", -1)
    rim_y = from_behind(face_y[:, :1], "gy", -1)
    rim_z = from_behind(face_z[:, :, :1], "gz", -1)
    high_x = jnp.concatenate([face_x[1:], rim_x], 0)
    high_y = jnp.concatenate([face_y[:, 1:], rim_y], 1)
    high_z = jnp.concatenate([face_z[:, :, 1:], rim_z], 2)
    coefs = (face_x, high_x, face_y, high_y, face_z, high_z)
    return cycle(adjoint_residual, LEVELS, coefs)


def fits(mesh, shape):
    nx, ny, nz = shape
    cx, cy, cz = mesh.shape["gx"], mesh.shape["gy"], mesh.shape["gz"]
    powers = cx & (cx - 1) == 0 and cy & (cy - 1) == 0 and cz == 2
    blocks = nx % (8 * cx) == 0 and ny % (16 * cy) == 0 and nz == 256
    return powers and blocks and (nx // 8) * (nz // 8) == 128 and nx * ny * nz <= 2**19


def per_block(mesh, *args):
    counts = (mesh.shape["gx"], mesh.shape["gy"], mesh.shape["gz"])
    whole = tuple(n * c for n, c in zip(args[0].shape, counts))
    return (per_device_small if fits(mesh, whole) else per_device)(*args)


def solution(mesh):
    return jax.shard_map(
        functools.partial(per_block, mesh),
        mesh=mesh,
        in_specs=(
            P("gx", "gy", "gz"),
            P("gx", "gy", "gz"),
            P("gx", "gy", "gz"),
            P("gx", "gy", "gz"),
        ),
        out_specs=P("gx", "gy", "gz"),
        check_vma=False,
    )
```

```python
import functools

import jax
import jax.numpy as jnp
from jax import lax
from jax.experimental import pallas as pl
from jax.experimental.pallas import tpu as pltpu
from jax.sharding import PartitionSpec as P

LEVELS = 4
COARSE_ITERS = 6


damping = 2.0 / 3.0

REACH = 3
TILE = 8
PAD = 4
SMALL = pl.CostEstimate(flops=2**20, bytes_accessed=2**20, transcendentals=0)
PARAMS = pltpu.CompilerParams(vmem_limit_bytes=16 * 2**20)


def up(v, axis):
    return pltpu.roll(v, v.shape[axis] - 1, axis)


def down(v, axis):
    return pltpu.roll(v, 1, axis)


def iota(shape, axis):
    return lax.broadcasted_iota(jnp.int32, shape, axis)


def chosen(mask):
    return jnp.where(mask, 1.0, 0.0).astype(jnp.bfloat16)


def select_dot(values, matrix):
    count = values.shape[0]
    high = values.astype(jnp.bfloat16).astype(jnp.float32)
    rest = values - high
    mid = rest.astype(jnp.bfloat16).astype(jnp.float32)
    parts = jnp.concatenate([high, mid, rest - mid], 0).astype(jnp.bfloat16)
    product = jnp.dot(parts, matrix, preferred_element_type=jnp.float32)
    return (product[2 * count :] + product[count : 2 * count]) + product[:count]


def inverse(diagonal):
    return jnp.where(diagonal > 0.0, damping / jnp.where(diagonal > 0.0, diagonal, 1.0), 0.0)


def side(axis):
    here = lax.axis_index(axis)
    first = jnp.where(here > 0, 1.0, 0.0)
    last = jnp.where(here < lax.axis_size(axis) - 1, 1.0, 0.0)
    return (here % 2 == 1, first), (here % 2 == 0, last)


def x_kernel(own, *slabs):
    nx, gx = own.shape[1], lax.axis_index("gx")
    for kind, out in enumerate(slabs):
        start = jnp.where((gx + kind) % 2 == 0, nx - 2, 0)
        for a in range(4):
            for n in range(2):
                out[2 * a + n] = own[a, start + n]
        out[8] = own[1, 2]


def sides_x(slabs, before, behind):
    for (even, keep), out in zip(side("gx"), (before, behind)):
        for n in range(9):
            out[n] = keep * jnp.where(even, slabs[0][n], slabs[1][n])


def y_kernel(own, s0, s1, o0, o1, before, behind):
    nx, ny = own.shape[1], own.shape[2]
    gy = lax.axis_index("gy")
    sides_x((s0, s1), before, behind)
    for kind, out in enumerate((o0, o1)):
        ahead = (gy + kind) % 2 == 0
        for p in range(nx + 4):
            for a in range(4):
                if p < 2:
                    v = before[2 * a + p]
                elif p < nx + 2:
                    v = own[a, p - 2]
                else:
                    v = behind[2 * a + p - nx - 2]
                at = (a * (nx + 4) + p) * 2
                out[at : at + 2] = jnp.where(ahead, v[ny - 2 :], v[:2])
                if a == 2:
                    out[8 * (nx + 4) + p : 8 * (nx + 4) + p + 1] = v[2:3]
        used = 9 * (nx + 4)
        out[used:] = jnp.zeros((out.shape[0] - used, out.shape[1]), jnp.float32)


def z_kernel(own, s0, s1, o0, o1, ext, before, behind, lines):
    nx, ny, nz = own.shape[1:]
    gz = lax.axis_index("gz")
    sides_x((s0, s1), before, behind)
    zero = jnp.zeros((PAD, nz), jnp.float32)
    empty = jnp.zeros((ny + 2 * PAD, nz), jnp.float32)
    for a in range(4):
        for p in range(nx + 2 * REACH):
            q = p - REACH
            if 0 <= q < nx:
                v = own[a, q]
            elif -2 <= q < 0:
                v = before[2 * a + q + 2]
            elif nx <= q < nx + 2:
                v = behind[2 * a + q - nx]
            elif q == nx + 2 and a == 1:
                v = behind[8]
            else:
                ext[a, p] = empty
                continue
            ext[a, p, :PAD] = zero
            ext[a, p, PAD + ny :] = zero
            ext[a, p, PAD : PAD + ny] = v
    for (even, keep), r in zip(side("gy"), (PAD - 2, PAD + ny)):
        lines[...] = keep * jnp.where(even, o0[...], o1[...])
        for p in range(nx + 4):
            for a in range(4):
                at = (a * (nx + 4) + p) * 2
                ext[a, 1 + p, r : r + 2] = lines[at : at + 2]
            if r > PAD:
                at = 8 * (nx + 4) + p
                ext[2, 1 + p, r + 2 : r + 3] = lines[at : at + 1]


def side_by_side(values):
    gz, nz = lax.axis_index("gz"), values[0].shape[1]
    lane, packed = iota(values[0].shape, 1), values[0]
    for a in range(1, 4):
        first = jnp.where(gz == 0, nz - 3 - 3 * a, 3 * a)
        moved = pltpu.roll(values[a], jnp.where(gz == 0, nz - 3 * a, 3 * a), 1)
        packed = jnp.where((lane >= first) & (lane < first + 3), moved, packed)
    return packed


def edge_x_kernel(own, s0, s1, out, before, behind):
    nx, ny, nz = own.shape[1:]
    sides_x((s0, s1), before, behind)
    for p in range(nx + 4):
        if p < 2:
            values = [before[2 * a + p] for a in range(4)]
        elif p < nx + 2:
            values = [own[a, p - 2] for a in range(4)]
        else:
            values = [behind[2 * a + p - nx - 2] for a in range(4)]
        out[p, :PAD] = jnp.zeros((PAD, nz), jnp.float32)
        out[p, PAD + ny :] = jnp.zeros((PAD, nz), jnp.float32)
        out[p, PAD : PAD + ny] = side_by_side(values)


def edge_y_kernel(o0, o1, out):
    planes, nz = out.shape[0], o0.shape[1]
    out[...] = jnp.zeros_like(out)
    for (even, keep), r in zip(side("gy"), (PAD - 2, 2 * TILE - PAD)):
        each = 2 * planes
        lines = [
            keep * jnp.where(even, o0[a * each : (a + 1) * each], o1[a * each : (a + 1) * each]) for a in range(4)
        ]
        packed = side_by_side(lines)
        for p in range(planes):
            out[p, r : r + 2] = packed[2 * p : 2 * p + 2]


def fine_kernel(local, edges_x, edges_y, faces, e_out, q_out, r_out, m_out, halo, e1, rd, dg, e2, rows):
    nx, ny, half = e_out.shape
    nz = 2 * half
    gx, gy, gz = lax.axis_index("gx"), lax.axis_index("gy"), lax.axis_index("gz")
    spot = iota((ny + 2 * PAD, half), 1)
    given = jnp.logical_or((gz == 0) & (spot < 3), (gz == 1) & (spot >= half - 3))
    gap = jnp.zeros((ny + 2 * PAD - 2 * TILE, half), jnp.float32)
    edge = {
        1 + p: edges_x[p] + jnp.concatenate([edges_y[p, :TILE], gap, edges_y[p, TILE:]], 0) for p in range(nx + 4)
    }
    for p in range(nx + 2 * REACH):
        for a in range(4):
            if 1 <= p < nx + 5:
                v = edge[p]
                if a > 0:
                    v = pltpu.roll(v, jnp.where(gz == 0, half - 3 * a, 3 * a), 1)
                halo[a, p] = jnp.where(given, v, 0.0)
            else:
                halo[a, p] = jnp.zeros((ny + 2 * PAD, half), jnp.float32)

    def ext(a, p):
        return jnp.concatenate([local[a, p], halo[a, p]], 1)

    shape = (ny + 2 * PAD, nz)
    row, lane = iota(shape, 0), iota(shape, 1)
    inner_z = jnp.logical_or(lane > 0, gz > 0)
    in_y = jnp.logical_and(
        jnp.logical_or(gy > 0, row >= PAD),
        jnp.logical_or(gy < lax.axis_size("gy") - 1, row < PAD + ny),
    )

    def off(e, p):
        fy, fz = ext(2, p), jnp.where(inner_z, ext(3, p), 0.0)
        here = e[p]
        total = ext(1, p) * e[p - 1] + ext(1, p + 1) * e[p + 1]
        total = total + fy * down(here, 0) + up(fy * here, 0)
        return total + fz * down(here, 1) + up(fz * here, 1)

    for p in range(1, nx + 2 * REACH - 1):
        fy, fz = ext(2, p), ext(3, p)
        diagonal = ext(1, p) + ext(1, p + 1) + fy + up(fy, 0) + fz + up(jnp.where(inner_z, fz, 0.0), 1)
        inv = inverse(diagonal)
        dg[p], rd[p] = diagonal, inv
        e1[p] = ext(0, p) * inv
    for p in range(2, nx + 2 * REACH - 2):
        value = (2.0 - damping) * e1[p] + rd[p] * off(e1, p)
        inside = in_y
        if p < REACH:
            inside = jnp.logical_and(inside, gx > 0)
        if p >= REACH + nx:
            inside = jnp.logical_and(inside, gx < lax.axis_size("gx") - 1)
        e2[p] = jnp.where(inside, value, 0.0)

    def mine(v):
        return v[PAD : PAD + ny, :half]

    sums = []
    for i in range(nx):
        p = REACH + i
        q = mine(ext(0, p) - dg[p] * e2[p] + off(e2, p))
        e_out[i], q_out[i], r_out[i] = mine(e2[p]), q, mine(rd[p])
        sums.append(q)
    pairs = range(0, nx, 2)
    both_low = chosen(iota((half, half), 0) // 2 == iota((half, half), 1))
    rows[...] = select_dot(jnp.concatenate([sums[i] + sums[i + 1] for i in pairs], 0), both_low)
    part = rows.shape[0] // 2
    total = rows[pl.ds(0, part, stride=2)] + rows[pl.ds(1, part, stride=2)]
    m_out[0] = faces[0] + total.reshape(m_out.shape[1:])
    m_out[1] = faces[1]


def faces_kernel(own, out, rows):
    nx, ny, half = own.shape[1:]

    def face(d, i):
        return 0.5 * own[d, i]

    pairs = range(0, nx, 2)
    fine, coarse = iota((half, half), 0), iota((half, half), 1)
    both_low, both_high = chosen(fine // 2 == coarse), chosen(fine // 2 + half // 2 == coarse)
    even_high = chosen(fine + half == 2 * coarse)
    count = len(pairs) * ny
    rows[:count] = select_dot(jnp.concatenate([face(1, i) for i in pairs], 0), both_high)
    rows[count:] = select_dot(jnp.concatenate([face(2, i) + face(2, i + 1) for i in pairs], 0), both_low) + select_dot(
        jnp.concatenate([face(3, i) + face(3, i + 1) for i in pairs], 0), even_high
    )
    part = count // 2
    even = rows[pl.ds(0, 2 * part, stride=2)]
    odd = rows[pl.ds(1, 2 * part, stride=2)]
    spot = iota((part, half), 1)
    out[0] = (even[:part] + odd[:part]).reshape(out.shape[1:])
    out[1] = (even[part:] + jnp.where(spot < half // 2, 0.0, odd[part:])).reshape(out.shape[1:])


def sweep_kernel(local, edges_x, e_in, q_in, r_in, t_out, k_out, *matrices):
    nx, ny, half = t_out.shape
    gz = lax.axis_index("gz")
    lane = iota((ny, half), 1)
    low_z, top_z = jnp.logical_or(lane > 0, gz > 0), lane < half - 1
    keep = jnp.where(gz == 0, 1.0, 0.0)
    inner = slice(PAD, PAD + ny)
    for i in range(nx):
        p, inv = REACH + i, r_in[i]
        fz = local[3, p, inner]
        far = keep * pltpu.roll(edges_x[p - 1, inner], half - 1 - 9, 1)
        high_z = jnp.where(top_z, up(fz, 1), far)
        faces = (local[1, p, inner], local[1, p + 1, inner], local[2, p, inner], local[2, p, PAD + 1 : PAD + 1 + ny])
        t_out[i] = e_in[i] + inv * q_in[i]
        for n, k in enumerate(faces + (jnp.where(low_z, fz, 0.0), high_z)):
            k_out[n, i] = inv * k
    both1, even1, both2, even2, spread3, spread2, last = matrices
    fine, coarse = iota(both1.shape, 0), iota(both1.shape, 1)
    both1[...], even1[...] = chosen(fine // 2 == coarse), chosen(fine == 2 * coarse)
    spread2[...] = chosen(coarse // 2 == fine)
    blocks = both2.shape[0] // half
    depth = half // blocks
    fine, coarse = iota(both2.shape, 0), iota(both2.shape, 1)
    block, fine = fine // half, fine % half
    valid = fine < 2 * depth
    both2[...] = chosen((fine // 2 + block * depth == coarse) & valid)
    even2[...] = chosen((fine + 2 * block * depth == 2 * coarse) & valid)
    fine, coarse = iota(spread3.shape, 1), iota(spread3.shape, 0)
    block, fine = fine // half, fine % half
    spread3[...] = chosen((fine // 2 + block * depth == coarse) & (fine < 2 * depth))
    spot = gz * half + iota(last.shape, 1) % half + (iota(last.shape, 1) // half + 1) % 3 - 1
    wanted = iota(last.shape, 0)
    last[...] = chosen((2 * wanted == spot) | (2 * wanted + 1 == spot))


def planes_of(ref):
    return [ref[p] for p in range(ref.shape[0])]


def level_parts(fx, fy, fz):
    shape = fy[0].shape
    row, lane = iota(shape, 0), iota(shape, 1)
    n = len(fx)
    zero = jnp.zeros(shape, jnp.float32)
    fym = [jnp.where(row > 0, v, 0.0) for v in fy]
    fzm = [jnp.where(lane > 0, v, 0.0) for v in fz]
    high = [fx[p + 1] if p + 1 < n else zero for p in range(n)]
    diagonal = [fx[p] + high[p] + fy[p] + up(fym[p], 0) + fz[p] + up(fzm[p], 1) for p in range(n)]

    def off(e):
        result = []
        for p in range(n):
            total = fym[p] * down(e[p], 0) + up(fym[p] * e[p], 0)
            total = total + fzm[p] * down(e[p], 1) + up(fzm[p] * e[p], 1)
            if p > 0:
                total = total + fx[p] * e[p - 1]
            if p + 1 < n:
                total = total + fx[p + 1] * e[p + 1]
            result.append(total)
        return result

    return diagonal, [inverse(d) for d in diagonal], off


def before(b, diagonal, inv, off):
    e1 = [v * r for v, r in zip(b, inv)]
    e2 = [(2.0 - damping) * e + r * o for e, r, o in zip(e1, inv, off(e1))]
    q = [v - d * e + o for v, d, e, o in zip(b, diagonal, e2, off(e2))]
    return [e + r * v for e, r, v in zip(e2, inv, q)], q


def after(t, c, inv, off):
    return [v + (1.0 - damping) * k + r * o for v, k, r, o in zip(t, c, inv, off(c))]


def coarse_operator(fx, fy, fz, depth):
    row, lane = iota(fx.shape, 0), iota(fx.shape, 1)
    fxm = jnp.where(lane >= depth, fx, 0.0)
    fym = jnp.where(row > 0, fy, 0.0)
    fzm = jnp.where(lane % depth > 0, fz, 0.0)
    wide = fx.shape[1]

    def up_x(v):
        return pltpu.roll(v, wide - depth, 1)

    hx, hy, hz = up_x(fxm), up(fym, 0), up(fzm, 1)
    diagonal = (fx + hx) + (fy + hy) + (fz + hz)

    def operate_packed(v):
        along_x = fxm * pltpu.roll(v, depth, 1) + hx * up_x(v)
        along_y = fym * down(v, 0) + hy * up(v, 0)
        along_z = fzm * down(v, 1) + hz * up(v, 1)
        return (diagonal * v - along_y) - (along_x + along_z)

    return operate_packed


def coarse_solution(rhs, operate_packed):
    def total(v):
        v = jnp.broadcast_to(jnp.sum(v, axis=1, keepdims=True), v.shape)
        for shift in (4, 2, 1):
            v = v + pltpu.roll(v, shift, 0)
        return v

    remain, search = rhs, rhs
    image = operate_packed(rhs)
    norm_now, energy = total(rhs * rhs), total(rhs * image)
    alpha = norm_now / energy
    solution = alpha * search
    for step in range(COARSE_ITERS - 1):
        inverse_norm = 1.0 / norm_now
        remain = remain - alpha * image
        across = operate_packed(remain)
        norm_next, own, mixed = total(remain * remain), total(remain * across), total(remain * image)
        beta = norm_next * inverse_norm
        energy = own + beta * (2.0 * mixed + beta * energy)
        search = remain + beta * search
        image = across + beta * image
        norm_now = norm_next
        alpha = norm_now / energy
        solution = solution + alpha * search
    return solution


def mirrored(k, count):
    result = 0
    while count > 1:
        result, k, count = 2 * result + k % 2, k // 2, count // 2
    return result


def whole_kernel(*refs):
    count = lax.axis_size("gy")
    here, there = refs[:count], refs[count : 2 * count]
    t_in, k_in, both1, even1, both2, even2, spread3, spread21, last, out, grid, fold1, folds1, fold2, folds2, spread2, held2, spread1, kept, doubled = refs[2 * count :]
    gx, gy, gz = lax.axis_index("gx"), lax.axis_index("gy"), lax.axis_index("gz")
    cx, cy = lax.axis_size("gx"), lax.axis_size("gy")
    bx, by, w1 = here[0].shape[2:]
    for k in range(cx * cy):
        x = jnp.bitwise_xor(gx, k % cx) * bx
        y = pl.multiple_of(jnp.bitwise_xor(gy, k // cx) * by, by)
        mine, other, j = k % cx, mirrored(k % cx, cx), k // cx
        for a in range(2):
            low = jnp.where(gz == 0, here[j][mine, a], there[j][mine, a]).reshape(bx * by, w1)
            top = jnp.where(gz == 0, there[j][other, a], here[j][other, a]).reshape(bx * by, w1)
            left = iota((bx * by, w1), 1) < w1 // 2
            one = jnp.where(left, low, pltpu.roll(top, w1 // 2, 1))
            two = jnp.where(left, pltpu.roll(low, w1 // 2, 1), top)
            spot = (pl.ds(x + 2, bx), pl.ds(y + TILE, by))
            grid[(2 * a, *spot)] = one.reshape(bx, by, w1)
            grid[(2 * a + 1, *spot)] = two.reshape(bx, by, w1)
    n1, m1 = cx * bx, cy * by
    inner = slice(TILE, TILE + m1)
    for ref in (grid.at[1], grid.at[2], grid.at[3], kept.at[0], kept.at[1]):
        for p in range(n1 + 4):
            if p < 2 or p >= n1 + 2:
                ref[p] = jnp.zeros((m1 + 2 * TILE, w1), jnp.float32)
            else:
                ref[p, :TILE] = jnp.zeros((TILE, w1), jnp.float32)
                ref[p, TILE + m1 :] = jnp.zeros((TILE, w1), jnp.float32)
    b1, fx1, fy1, fz1 = ([grid[a, 2 + p, inner] for p in range(n1)] for a in range(4))
    n2, m2 = n1 // 2, m1 // 2
    half = n2 * m2
    pairs = range(0, n1, 2)
    folds1[...] = jnp.concatenate(
        [0.5 * fx1[i] for i in pairs]
        + [0.5 * (fy1[i] + fy1[i + 1]) for i in pairs]
        + [0.5 * (fz1[i] + fz1[i + 1]) for i in pairs],
        0,
    )
    low, top = folds1[pl.ds(0, 3 * half, stride=2)], folds1[pl.ds(1, 3 * half, stride=2)]
    summed = select_dot(jnp.concatenate([low[:half] + top[:half], low[half : 2 * half]], 0), both1[...])

    def part(v):
        return [v[p * m2 : (p + 1) * m2] for p in range(n2)]

    fx2, fy2 = part(summed[:half]), part(summed[half:])
    fz2 = part(select_dot(low[2 * half :] + top[2 * half :], even1[...]))
    diagonal1, inv1, off1 = level_parts(fx1, fy1, fz1)
    t1, q1 = before(b1, diagonal1, inv1, off1)
    for p in range(n1):
        kept[0, 2 + p, inner] = t1[p]
        kept[1, 2 + p, inner] = inv1[p]
    diagonal2, inv2, off2 = level_parts(fx2, fy2, fz2)

    n3, m3 = n2 // 2, m2 // 2
    depth = w1 // n3
    blocks = range(0, n2, 2)
    wide = [
        jnp.concatenate([0.5 * fx2[i] for i in blocks], 1),
        jnp.concatenate([0.5 * (fy2[i] + fy2[i + 1]) for i in blocks], 1),
    ]
    thin = jnp.concatenate([0.5 * (fz2[i] + fz2[i + 1]) for i in blocks], 1)
    folds2[: 2 * m2] = select_dot(jnp.concatenate(wide, 0), both2[...])
    folds2[2 * m2 :] = select_dot(thin, even2[...])
    low, top = folds2[pl.ds(0, 3 * m3, stride=2)], folds2[pl.ds(1, 3 * m3, stride=2)]
    operate3 = coarse_operator(low[:m3] + top[:m3], low[m3 : 2 * m3], low[2 * m3 :] + top[2 * m3 :], depth)

    fold1[...] = jnp.concatenate([q1[i] + q1[i + 1] for i in pairs], 0)
    b2 = part(select_dot(fold1[pl.ds(0, half, stride=2)] + fold1[pl.ds(1, half, stride=2)], both1[...]))
    t2, q2 = before(b2, diagonal2, inv2, off2)
    fold2[...] = select_dot(jnp.concatenate([q2[i] + q2[i + 1] for i in blocks], 1), both2[...])
    c3 = coarse_solution(fold2[pl.ds(0, m3, stride=2)] + fold2[pl.ds(1, m3, stride=2)], operate3)

    row = select_dot(c3, spread3[...])
    for i in range(n3):
        spread2[pl.ds(i * m2, m3, stride=2)] = row[:, i * w1 : (i + 1) * w1]
        spread2[pl.ds(i * m2 + 1, m3, stride=2)] = row[:, i * w1 : (i + 1) * w1]
    up2 = [spread2[(p // 2) * m2 : (p // 2 + 1) * m2] for p in range(n2)]
    c2 = after(t2, up2, inv2, off2)

    held2[0] = jnp.zeros((m2, w1), jnp.float32)
    held2[n2 + 1] = jnp.zeros((m2, w1), jnp.float32)
    for p in range(n2):
        held2[1 + p] = c2[p]
    few = bx // 2 + 2
    near = held2[pl.ds(gx * (bx // 2), few)].reshape(few * m2, w1)
    row = select_dot(near, spread21[...])
    for p in range(few):
        spread1[p, :TILE] = jnp.zeros((TILE, w1), jnp.float32)
        spread1[p, TILE + m1 :] = jnp.zeros((TILE, w1), jnp.float32)
        spread1[p, pl.ds(TILE, m2, stride=2)] = row[p * m2 : (p + 1) * m2]
        spread1[p, pl.ds(TILE + 1, m2, stride=2)] = row[p * m2 : (p + 1) * m2]
    tall = by + 2 * TILE
    rows = pl.ds(pl.multiple_of(gy * by, by), tall)
    inner_z = iota((tall, w1), 1) > 0
    up1 = [spread1[p, rows] for p in range(few)]
    near = []
    for p in range(1, bx + 3):
        x = gx * bx + p
        e = up1[p // 2]
        fy, fz = grid[2, x, rows], jnp.where(inner_z, grid[3, x, rows], 0.0)
        total = grid[1, x, rows] * up1[(p - 1) // 2] + grid[1, x + 1, rows] * up1[(p + 1) // 2]
        total = total + fy * down(e, 0) + up(fy * e, 0) + fz * down(e, 1) + up(fz * e, 1)
        value = kept[0, x, rows] + (1.0 - damping) * e + kept[1, x, rows] * total
        near.append(value[TILE - 1 : TILE - 1 + by + TILE])
    tall = by + TILE
    row = select_dot(jnp.concatenate(near, 0), last[...])
    for s in range(3):
        doubled[s, pl.ds(0, (bx + 2) * tall, stride=2)] = row[:, s * w1 : (s + 1) * w1]
        doubled[s, pl.ds(1, (bx + 2) * tall, stride=2)] = row[:, s * w1 : (s + 1) * w1]
    ny = t_in.shape[1]

    def at(s, i, shift):
        first = (1 + i // 2) * 2 * tall + 2 + shift
        return doubled[s, first : first + ny]

    for i in range(t_in.shape[0]):
        value = t_in[i] + (1.0 - damping) * at(0, i, 0)
        value = value + k_in[0, i] * at(0, i - 1, 0) + k_in[1, i] * at(0, i + 1, 0)
        value = value + k_in[2, i] * at(0, i, -1) + k_in[3, i] * at(0, i, 1)
        out[i] = value + k_in[4, i] * at(2, i, 0) + k_in[5, i] * at(1, i, 0)


def traded(blocks, axis):
    count, cores = lax.axis_size(axis), lax.axis_size("gz")
    taken = []
    for kind, block in enumerate(blocks):
        route = []
        for i in range(count):
            other = i + 1 if (i + kind) % 2 == 0 else i - 1
            for c in range(cores):
                to = other * cores + c if 0 <= other < count else i * cores + cores - 1 - c
                route.append((i * cores + c, to))
        taken.append(lax.ppermute(block, (axis, "gz"), route))
    return taken


def doubled_over(block, axis):
    count, cores = lax.axis_size(axis), lax.axis_size("gz")
    steps = [1 << n for n in range(count.bit_length() - 1)]
    for up_step, down_step in zip(steps, reversed(steps)):
        route = [(i * cores + c, (i ^ (down_step if c else up_step)) * cores + c) for i in range(count) for c in range(cores)]
        block = jnp.concatenate([block, lax.ppermute(block, (axis, "gz"), route)], 0)
    return block


def f32(*shape):
    return jax.ShapeDtypeStruct(shape, jnp.float32)


def per_device_small(adjoint_residual, face_x, face_y, face_z):
    nx, ny, nz = adjoint_residual.shape
    near = [pltpu.VMEM((9, ny, nz), jnp.float32)] * 2
    cy = lax.axis_size("gy")
    own = jnp.stack((adjoint_residual, face_x, face_y, face_z))
    slabs = pl.pallas_call(
        x_kernel,
        out_shape=(f32(9, ny, nz), f32(9, ny, nz)),
        compiler_params=PARAMS,
        name="slabs_x",
    )(own)
    slabs = traded(slabs, "gx")
    faces = pl.pallas_call(
        faces_kernel,
        out_shape=f32(2, nx // 2, ny // 2, nz),
        scratch_shapes=[pltpu.VMEM((nx * ny, nz), jnp.float32)],
        compiler_params=PARAMS,
        cost_estimate=SMALL,
        name="faces",
    )(own)
    count = -(-9 * (nx + 4) // 8) * 8
    lines = pl.pallas_call(
        y_kernel,
        out_shape=(f32(count, nz), f32(count, nz)),
        scratch_shapes=near,
        compiler_params=PARAMS,
        name="slabs_y",
    )(own, *slabs)
    edge = pl.pallas_call(
        edge_x_kernel,
        out_shape=f32(nx + 4, ny + 2 * PAD, nz),
        scratch_shapes=near,
        compiler_params=PARAMS,
        cost_estimate=SMALL,
        name="edges_x",
    )(own, *slabs)
    swap = [(0, 1), (1, 0)]
    lines = traded(lines, "gy")
    edges_x = lax.ppermute(edge, "gz", swap)
    edge = pl.pallas_call(
        edge_y_kernel,
        out_shape=f32(nx + 4, 2 * TILE, nz),
        compiler_params=PARAMS,
        name="edges_y",
    )(*lines)
    edges_y = lax.ppermute(edge, "gz", swap)
    local = pl.pallas_call(
        z_kernel,
        out_shape=f32(4, nx + 2 * REACH, ny + 2 * PAD, nz),
        scratch_shapes=near + [pltpu.VMEM((count, nz), jnp.float32)],
        compiler_params=PARAMS,
        cost_estimate=SMALL,
        name="extend",
    )(own, *slabs, *lines)
    ext_x, ext_y, wide = nx + 2 * REACH, ny + 2 * PAD, 2 * nz
    field = pltpu.VMEM((ext_x, ext_y, wide), jnp.float32)
    e, q, r, m = pl.pallas_call(
        fine_kernel,
        out_shape=(f32(nx, ny, nz),) * 3 + (f32(2, nx // 2, ny // 2, nz),),
        scratch_shapes=[
            pltpu.VMEM((4, ext_x, ext_y, nz), jnp.float32),
            field,
            field,
            field,
            field,
            pltpu.VMEM((nx * ny // 2, nz), jnp.float32),
        ],
        compiler_params=PARAMS,
        name="fine",
    )(local, edges_x, edges_y, faces)
    blocks = nx * lax.axis_size("gx") // 8
    shapes = ((nz, nz), (nz, nz), (blocks * nz, nz), (blocks * nz, nz), (nz, blocks * nz), (nz, nz), (nz, 3 * nz))
    t, k, *matrices = pl.pallas_call(
        sweep_kernel,
        out_shape=(f32(nx, ny, nz), f32(6, nx, ny, nz))
        + tuple(jax.ShapeDtypeStruct(shape, jnp.bfloat16) for shape in shapes),
        compiler_params=PARAMS,
        cost_estimate=SMALL,
        name="sweep",
    )(local, edges_x, e, q, r)
    near = doubled_over(m[None], "gx")
    here = [near] + [
        lax.ppermute(near, "gy", [(i, i ^ n) for i in range(cy)]) for n in range(1, cy)
    ]
    there = [lax.ppermute(block, "gz", [(0, 1), (1, 0)]) for block in here]
    n1, m1 = m.shape[1] * lax.axis_size("gx"), m.shape[2] * cy
    n2, m2 = n1 // 2, m1 // 2
    tall = (nx // 2 + 2) * (ny // 2 + TILE)
    return pl.pallas_call(
        whole_kernel,
        out_shape=f32(nx, ny, nz),
        scratch_shapes=[
            pltpu.VMEM((4, n1 + 4, m1 + 2 * TILE, nz), jnp.float32),
            pltpu.VMEM((n2 * m1, nz), jnp.float32),
            pltpu.VMEM((3 * n2 * m1, nz), jnp.float32),
            pltpu.VMEM((m2, nz), jnp.float32),
            pltpu.VMEM((3 * m2, nz), jnp.float32),
            pltpu.VMEM((n1 * m1 // 8, nz), jnp.float32),
            pltpu.VMEM((n2 + 2, m2, nz), jnp.float32),
            pltpu.VMEM((nx // 4 + 2, m1 + 2 * TILE, nz), jnp.float32),
            pltpu.VMEM((2, n1 + 4, m1 + 2 * TILE, nz), jnp.float32),
            pltpu.VMEM((3, 2 * tall, nz), jnp.float32),
        ],
        compiler_params=PARAMS,
        name="whole",
    )(*here, *there, t, k, *matrices)


def extended(block, sides, width):
    for axis, dim in sides:
        count = lax.axis_size(axis)
        forward = [(i, i + 1) for i in range(count - 1)]
        backward = [(target, source) for source, target in forward]
        low = lax.ppermute(
            lax.slice_in_dim(block, block.shape[dim] - width, None, axis=dim), axis, forward
        )
        high = lax.ppermute(lax.slice_in_dim(block, 0, width, axis=dim), axis, backward)
        block = jnp.concatenate([low, block, high], axis=dim)
    return block


def from_behind(block, axis, distance):
    devices = range(lax.axis_size(axis))
    route = [(i - distance, i) for i in devices if i - distance in devices]
    return lax.ppermute(block, axis, route)


def stencil(padded, field, coefs):
    low_x, high_x, low_y, high_y, low_z, high_z = coefs
    diagonal = low_x + high_x + low_y + high_y + low_z + high_z
    result = diagonal * field - low_x * padded[:-2, 1:-1, 1:-1] - high_x * padded[2:, 1:-1, 1:-1]
    result = result - low_y * padded[1:-1, :-2, 1:-1] - high_y * padded[1:-1, 2:, 1:-1]
    return result - low_z * padded[1:-1, 1:-1, :-2] - high_z * padded[1:-1, 1:-1, 2:]


def operate(field, coefs):
    padded = extended(field, (("gx", 0), ("gy", 1), ("gz", 2)), 1)
    return stencil(padded, field, coefs)


def operate_whole(field, coefs):
    return stencil(jnp.pad(field, 1), field, coefs)


def blocked(values):
    return values.reshape(values.shape[0] // 2, 2, values.shape[1] // 2, 2, values.shape[2] // 2, 2)


def coarse_face(values, dim, parity):
    others = tuple((2 * k + 1 for k in range(3) if k != dim))
    summed = jnp.sum(blocked(values), axis=others)
    return 0.5 * lax.index_in_dim(summed, parity, dim + 1, keepdims=False)


def coarsen(coefs):
    result = []
    for dim in range(3):
        result.append(coarse_face(coefs[2 * dim], dim, 0))
        result.append(coarse_face(coefs[2 * dim + 1], dim, 1))
    return tuple(result)


def restrict(values):
    return jnp.sum(blocked(values), axis=(1, 3, 5))


def prolong(values):
    shape_out = (values.shape[0] * 2, values.shape[1] * 2, values.shape[2] * 2)
    wide = jnp.broadcast_to(
        values[:, None, :, None, :, None],
        (values.shape[0], 2, values.shape[1], 2, values.shape[2], 2),
    )
    return wide.reshape(shape_out)


def total_local(value):
    return value


def conj_grad(rhs, coefs, apply_op, total):
    solution = jnp.zeros_like(rhs)
    remain = rhs
    search = rhs
    norm_now = total(jnp.sum(remain * remain))
    for step in range(COARSE_ITERS):
        image = apply_op(search, coefs)
        alpha = norm_now / total(jnp.sum(search * image))
        solution = solution + alpha * search
        remain = remain - alpha * image
        norm_next = total(jnp.sum(remain * remain))
        search = remain + norm_next / norm_now * search
        norm_now = norm_next
    return solution


def coarse_solve(rhs, coefs):
    part_x, part_y, part_z = rhs.shape
    count_x = lax.axis_size("gx")
    count_y = lax.axis_size("gy")
    count_z = lax.axis_size("gz")
    stacked = jnp.stack((rhs,) + coefs)[None]
    whole = lax.all_gather(stacked, ("gx", "gy", "gz"), axis=0, tiled=True)
    whole = whole.reshape(count_x, count_y, count_z, 7, part_x, part_y, part_z)
    whole = whole.transpose(3, 0, 4, 1, 5, 2, 6).reshape(
        7, count_x * part_x, count_y * part_y, count_z * part_z
    )
    whole_coefs = tuple((whole[k] for k in range(1, 7)))
    solution = conj_grad(whole[0], whole_coefs, operate_whole, total_local)
    starts = (
        lax.axis_index("gx") * part_x,
        lax.axis_index("gy") * part_y,
        lax.axis_index("gz") * part_z,
    )
    return lax.dynamic_slice(solution, starts, (part_x, part_y, part_z))


def cycle(rhs, levels_left, coefs):
    if levels_left == 1:
        return coarse_solve(rhs, coefs)
    diagonal = coefs[0] + coefs[1] + coefs[2] + coefs[3] + coefs[4] + coefs[5]
    field = damping * rhs / diagonal
    field = field + damping * (rhs - operate(field, coefs)) / diagonal
    remain = rhs - operate(field, coefs)
    field = field + prolong(cycle(restrict(remain), levels_left - 1, coarsen(coefs)))
    field = field + damping * (rhs - operate(field, coefs)) / diagonal
    return field


def per_device(adjoint_residual, face_x, face_y, face_z):
    rim_x = from_behind(face_x[:1], "gx", -1)
    rim_y = from_behind(face_y[:, :1], "gy", -1)
    rim_z = from_behind(face_z[:, :, :1], "gz", -1)
    high_x = jnp.concatenate([face_x[1:], rim_x], 0)
    high_y = jnp.concatenate([face_y[:, 1:], rim_y], 1)
    high_z = jnp.concatenate([face_z[:, :, 1:], rim_z], 2)
    coefs = (face_x, high_x, face_y, high_y, face_z, high_z)
    return cycle(adjoint_residual, LEVELS, coefs)


def fits(mesh, shape):
    nx, ny, nz = shape
    cx, cy, cz = mesh.shape["gx"], mesh.shape["gy"], mesh.shape["gz"]
    powers = cx & (cx - 1) == 0 and cy & (cy - 1) == 0 and cz == 2
    blocks = nx % (8 * cx) == 0 and ny % (16 * cy) == 0 and nz == 256
    return powers and blocks and (nx // 8) * (nz // 8) == 128 and nx * ny * nz <= 2**19


def per_block(mesh, *args):
    counts = (mesh.shape["gx"], mesh.shape["gy"], mesh.shape["gz"])
    whole = tuple(n * c for n, c in zip(args[0].shape, counts))
    return (per_device_small if fits(mesh, whole) else per_device)(*args)


def solution(mesh):
    return jax.shard_map(
        functools.partial(per_block, mesh),
        mesh=mesh,
        in_specs=(
            P("gx", "gy", "gz"),
            P("gx", "gy", "gz"),
            P("gx", "gy", "gz"),
            P("gx", "gy", "gz"),
        ),
        out_specs=P("gx", "gy", "gz"),
        check_vma=False,
    )
```

```python
import functools

import jax
import jax.numpy as jnp
from jax import lax
from jax.experimental import pallas as pl
from jax.experimental.pallas import tpu as pltpu
from jax.sharding import PartitionSpec as P

LEVELS = 4
COARSE_ITERS = 6


damping = 2.0 / 3.0

REACH = 3
TILE = 8
PAD = 4
SMALL = pl.CostEstimate(flops=2**20, bytes_accessed=2**20, transcendentals=0)
PARAMS = pltpu.CompilerParams(vmem_limit_bytes=16 * 2**20)
PACKED = pltpu.CompilerParams(
    vmem_limit_bytes=16 * 2**20
)


def up(v, axis):
    return pltpu.roll(v, v.shape[axis] - 1, axis)


def down(v, axis):
    return pltpu.roll(v, 1, axis)


def iota(shape, axis):
    return lax.broadcasted_iota(jnp.int32, shape, axis)


def chosen(mask):
    return jnp.where(mask, 1.0, 0.0).astype(jnp.bfloat16)


def select_dot(values, matrix):
    count = values.shape[0]
    high = values.astype(jnp.bfloat16).astype(jnp.float32)
    rest = values - high
    mid = rest.astype(jnp.bfloat16).astype(jnp.float32)
    parts = jnp.concatenate([high, mid, rest - mid], 0).astype(jnp.bfloat16)
    product = jnp.dot(parts, matrix, preferred_element_type=jnp.float32)
    return (product[2 * count :] + product[count : 2 * count]) + product[:count]


def inverse(diagonal):
    return jnp.where(diagonal > 0.0, damping / jnp.where(diagonal > 0.0, diagonal, 1.0), 0.0)


def side(axis):
    here = lax.axis_index(axis)
    first = jnp.where(here > 0, 1.0, 0.0)
    last = jnp.where(here < lax.axis_size(axis) - 1, 1.0, 0.0)
    return (here % 2 == 1, first), (here % 2 == 0, last)


def x_kernel(own, *slabs):
    nx, gx = own.shape[1], lax.axis_index("gx")
    for kind, out in enumerate(slabs):
        start = jnp.where((gx + kind) % 2 == 0, nx - 2, 0)
        for a in range(4):
            for n in range(2):
                out[2 * a + n] = own[a, start + n]
        out[8] = own[1, 2]


def sides_x(slabs, before, behind):
    for (even, keep), out in zip(side("gx"), (before, behind)):
        for n in range(9):
            out[n] = keep * jnp.where(even, slabs[0][n], slabs[1][n])


def y_kernel(own, s0, s1, o0, o1, before, behind):
    nx, ny = own.shape[1], own.shape[2]
    gy = lax.axis_index("gy")
    sides_x((s0, s1), before, behind)
    for kind, out in enumerate((o0, o1)):
        ahead = (gy + kind) % 2 == 0
        for p in range(nx + 4):
            for a in range(4):
                if p < 2:
                    v = before[2 * a + p]
                elif p < nx + 2:
                    v = own[a, p - 2]
                else:
                    v = behind[2 * a + p - nx - 2]
                at = (a * (nx + 4) + p) * 2
                out[at : at + 2] = jnp.where(ahead, v[ny - 2 :], v[:2])
                if a == 2:
                    out[8 * (nx + 4) + p : 8 * (nx + 4) + p + 1] = v[2:3]
        used = 9 * (nx + 4)
        out[used:] = jnp.zeros((out.shape[0] - used, out.shape[1]), jnp.float32)


def z_kernel(own, s0, s1, o0, o1, ext, before, behind, lines):
    nx, ny, nz = own.shape[1:]
    gz = lax.axis_index("gz")
    sides_x((s0, s1), before, behind)
    zero = jnp.zeros((PAD, nz), jnp.float32)
    empty = jnp.zeros((ny + 2 * PAD, nz), jnp.float32)
    for a in range(4):
        for p in range(nx + 2 * REACH):
            q = p - REACH
            if 0 <= q < nx:
                v = own[a, q]
            elif -2 <= q < 0:
                v = before[2 * a + q + 2]
            elif nx <= q < nx + 2:
                v = behind[2 * a + q - nx]
            elif q == nx + 2 and a == 1:
                v = behind[8]
            else:
                ext[a, p] = empty
                continue
            ext[a, p, :PAD] = zero
            ext[a, p, PAD + ny :] = zero
            ext[a, p, PAD : PAD + ny] = v
    for (even, keep), r in zip(side("gy"), (PAD - 2, PAD + ny)):
        lines[...] = keep * jnp.where(even, o0[...], o1[...])
        for p in range(nx + 4):
            for a in range(4):
                at = (a * (nx + 4) + p) * 2
                ext[a, 1 + p, r : r + 2] = lines[at : at + 2]
            if r > PAD:
                at = 8 * (nx + 4) + p
                ext[2, 1 + p, r + 2 : r + 3] = lines[at : at + 1]


def side_by_side(values):
    gz, nz = lax.axis_index("gz"), values[0].shape[1]
    lane, packed = iota(values[0].shape, 1), values[0]
    for a in range(1, 4):
        first = jnp.where(gz == 0, nz - 3 - 3 * a, 3 * a)
        moved = pltpu.roll(values[a], jnp.where(gz == 0, nz - 3 * a, 3 * a), 1)
        packed = jnp.where((lane >= first) & (lane < first + 3), moved, packed)
    return packed


def edge_x_kernel(own, s0, s1, out, before, behind):
    nx, ny, nz = own.shape[1:]
    sides_x((s0, s1), before, behind)
    for p in range(nx + 4):
        if p < 2:
            values = [before[2 * a + p] for a in range(4)]
        elif p < nx + 2:
            values = [own[a, p - 2] for a in range(4)]
        else:
            values = [behind[2 * a + p - nx - 2] for a in range(4)]
        out[p, :PAD] = jnp.zeros((PAD, nz), jnp.float32)
        out[p, PAD + ny :] = jnp.zeros((PAD, nz), jnp.float32)
        out[p, PAD : PAD + ny] = side_by_side(values)


def edge_y_kernel(o0, o1, out):
    planes, nz = out.shape[0], o0.shape[1]
    out[...] = jnp.zeros_like(out)
    for (even, keep), r in zip(side("gy"), (PAD - 2, 2 * TILE - PAD)):
        each = 2 * planes
        lines = [
            keep * jnp.where(even, o0[a * each : (a + 1) * each], o1[a * each : (a + 1) * each]) for a in range(4)
        ]
        packed = side_by_side(lines)
        for p in range(planes):
            out[p, r : r + 2] = packed[2 * p : 2 * p + 2]


def fine_kernel(local, edges_x, edges_y, faces, e_out, q_out, r_out, m_out, halo, e1, rd, dg, e2, rows):
    nx, ny, half = e_out.shape
    nz = 2 * half
    gx, gy, gz = lax.axis_index("gx"), lax.axis_index("gy"), lax.axis_index("gz")
    spot = iota((ny + 2 * PAD, half), 1)
    given = jnp.logical_or((gz == 0) & (spot < 3), (gz == 1) & (spot >= half - 3))
    gap = jnp.zeros((ny + 2 * PAD - 2 * TILE, half), jnp.float32)
    edge = {
        1 + p: edges_x[p] + jnp.concatenate([edges_y[p, :TILE], gap, edges_y[p, TILE:]], 0) for p in range(nx + 4)
    }
    for p in range(nx + 2 * REACH):
        for a in range(4):
            if 1 <= p < nx + 5:
                v = edge[p]
                if a > 0:
                    v = pltpu.roll(v, jnp.where(gz == 0, half - 3 * a, 3 * a), 1)
                halo[a, p] = jnp.where(given, v, 0.0)
            else:
                halo[a, p] = jnp.zeros((ny + 2 * PAD, half), jnp.float32)

    def ext(a, p):
        return jnp.concatenate([local[a, p], halo[a, p]], 1)

    shape = (ny + 2 * PAD, nz)
    row, lane = iota(shape, 0), iota(shape, 1)
    inner_z = jnp.logical_or(lane > 0, gz > 0)
    in_y = jnp.logical_and(
        jnp.logical_or(gy > 0, row >= PAD),
        jnp.logical_or(gy < lax.axis_size("gy") - 1, row < PAD + ny),
    )

    def off(e, p):
        fy, fz = ext(2, p), jnp.where(inner_z, ext(3, p), 0.0)
        here = e[p]
        total = ext(1, p) * e[p - 1] + ext(1, p + 1) * e[p + 1]
        total = total + fy * down(here, 0) + up(fy * here, 0)
        return total + fz * down(here, 1) + up(fz * here, 1)

    for p in range(1, nx + 2 * REACH - 1):
        fy, fz = ext(2, p), ext(3, p)
        diagonal = ext(1, p) + ext(1, p + 1) + fy + up(fy, 0) + fz + up(jnp.where(inner_z, fz, 0.0), 1)
        inv = inverse(diagonal)
        dg[p], rd[p] = diagonal, inv
        e1[p] = ext(0, p) * inv
    for p in range(2, nx + 2 * REACH - 2):
        value = (2.0 - damping) * e1[p] + rd[p] * off(e1, p)
        inside = in_y
        if p < REACH:
            inside = jnp.logical_and(inside, gx > 0)
        if p >= REACH + nx:
            inside = jnp.logical_and(inside, gx < lax.axis_size("gx") - 1)
        e2[p] = jnp.where(inside, value, 0.0)

    def mine(v):
        return v[PAD : PAD + ny, :half]

    sums = []
    for i in range(nx):
        p = REACH + i
        q = mine(ext(0, p) - dg[p] * e2[p] + off(e2, p))
        e_out[i], q_out[i], r_out[i] = mine(e2[p]), q, mine(rd[p])
        sums.append(q)
    pairs = range(0, nx, 2)
    both_low = chosen(iota((half, half), 0) // 2 == iota((half, half), 1))
    rows[...] = select_dot(jnp.concatenate([sums[i] + sums[i + 1] for i in pairs], 0), both_low)
    part = rows.shape[0] // 2
    total = rows[pl.ds(0, part, stride=2)] + rows[pl.ds(1, part, stride=2)]
    m_out[0] = faces[0] + total.reshape(m_out.shape[1:])
    m_out[1] = faces[1]


def faces_kernel(own, out, rows):
    nx, ny, half = own.shape[1:]

    def face(d, i):
        return 0.5 * own[d, i]

    pairs = range(0, nx, 2)
    fine, coarse = iota((half, half), 0), iota((half, half), 1)
    both_low, both_high = chosen(fine // 2 == coarse), chosen(fine // 2 + half // 2 == coarse)
    even_high = chosen(fine + half == 2 * coarse)
    count = len(pairs) * ny
    rows[:count] = select_dot(jnp.concatenate([face(1, i) for i in pairs], 0), both_high)
    rows[count:] = select_dot(jnp.concatenate([face(2, i) + face(2, i + 1) for i in pairs], 0), both_low) + select_dot(
        jnp.concatenate([face(3, i) + face(3, i + 1) for i in pairs], 0), even_high
    )
    part = count // 2
    even = rows[pl.ds(0, 2 * part, stride=2)]
    odd = rows[pl.ds(1, 2 * part, stride=2)]
    spot = iota((part, half), 1)
    out[0] = (even[:part] + odd[:part]).reshape(out.shape[1:])
    out[1] = (even[part:] + jnp.where(spot < half // 2, 0.0, odd[part:])).reshape(out.shape[1:])


def sweep_kernel(local, edges_x, e_in, q_in, r_in, t_out, k_out, *matrices):
    nx, ny, half = t_out.shape
    gz = lax.axis_index("gz")
    lane = iota((ny, half), 1)
    low_z, top_z = jnp.logical_or(lane > 0, gz > 0), lane < half - 1
    keep = jnp.where(gz == 0, 1.0, 0.0)
    inner = slice(PAD, PAD + ny)
    for i in range(nx):
        p, inv = REACH + i, r_in[i]
        fz = local[3, p, inner]
        far = keep * pltpu.roll(edges_x[p - 1, inner], half - 1 - 9, 1)
        high_z = jnp.where(top_z, up(fz, 1), far)
        faces = (local[1, p, inner], local[1, p + 1, inner], local[2, p, inner], local[2, p, PAD + 1 : PAD + 1 + ny])
        t_out[i] = e_in[i] + inv * q_in[i]
        for n, k in enumerate(faces + (jnp.where(low_z, fz, 0.0), high_z)):
            k_out[n, i] = inv * k
    both1, even1, both2, even2, spread3, spread2, last = matrices
    fine, coarse = iota(both1.shape, 0), iota(both1.shape, 1)
    both1[...], even1[...] = chosen(fine // 2 == coarse), chosen(fine == 2 * coarse)
    spread2[...] = chosen(coarse // 2 == fine)
    blocks = both2.shape[0] // half
    depth = half // blocks
    fine, coarse = iota(both2.shape, 0), iota(both2.shape, 1)
    block, fine = fine // half, fine % half
    valid = fine < 2 * depth
    both2[...] = chosen((fine // 2 + block * depth == coarse) & valid)
    even2[...] = chosen((fine + 2 * block * depth == 2 * coarse) & valid)
    fine, coarse = iota(spread3.shape, 1), iota(spread3.shape, 0)
    block, fine = fine // half, fine % half
    spread3[...] = chosen((fine // 2 + block * depth == coarse) & (fine < 2 * depth))
    spot = gz * half + iota(last.shape, 1) % half + (iota(last.shape, 1) // half + 1) % 3 - 1
    wanted = iota(last.shape, 0)
    last[...] = chosen((2 * wanted == spot) | (2 * wanted + 1 == spot))


def planes_of(ref):
    return [ref[p] for p in range(ref.shape[0])]


def level_parts(fx, fy, fz):
    shape = fy[0].shape
    row, lane = iota(shape, 0), iota(shape, 1)
    n = len(fx)
    zero = jnp.zeros(shape, jnp.float32)
    fym = [jnp.where(row > 0, v, 0.0) for v in fy]
    fzm = [jnp.where(lane > 0, v, 0.0) for v in fz]
    high = [fx[p + 1] if p + 1 < n else zero for p in range(n)]
    diagonal = [fx[p] + high[p] + fy[p] + up(fym[p], 0) + fz[p] + up(fzm[p], 1) for p in range(n)]

    def off(e):
        result = []
        for p in range(n):
            total = fym[p] * down(e[p], 0) + up(fym[p] * e[p], 0)
            total = total + fzm[p] * down(e[p], 1) + up(fzm[p] * e[p], 1)
            if p > 0:
                total = total + fx[p] * e[p - 1]
            if p + 1 < n:
                total = total + fx[p + 1] * e[p + 1]
            result.append(total)
        return result

    return diagonal, [inverse(d) for d in diagonal], off


def before(b, diagonal, inv, off):
    e1 = [v * r for v, r in zip(b, inv)]
    e2 = [(2.0 - damping) * e + r * o for e, r, o in zip(e1, inv, off(e1))]
    q = [v - d * e + o for v, d, e, o in zip(b, diagonal, e2, off(e2))]
    return [e + r * v for e, r, v in zip(e2, inv, q)], q


def after(t, c, inv, off):
    return [v + (1.0 - damping) * k + r * o for v, k, r, o in zip(t, c, inv, off(c))]


def coarse_operator(fx, fy, fz, depth):
    row, lane = iota(fx.shape, 0), iota(fx.shape, 1)
    fxm = jnp.where(lane >= depth, fx, 0.0)
    fym = jnp.where(row > 0, fy, 0.0)
    fzm = jnp.where(lane % depth > 0, fz, 0.0)
    wide = fx.shape[1]

    def up_x(v):
        return pltpu.roll(v, wide - depth, 1)

    hx, hy, hz = up_x(fxm), up(fym, 0), up(fzm, 1)
    diagonal = (fx + hx) + (fy + hy) + (fz + hz)

    def operate_packed(v):
        along_x = fxm * pltpu.roll(v, depth, 1) + hx * up_x(v)
        along_y = fym * down(v, 0) + hy * up(v, 0)
        along_z = fzm * down(v, 1) + hz * up(v, 1)
        return (diagonal * v - along_y) - (along_x + along_z)

    return operate_packed


def coarse_solution(rhs, operate_packed):
    def total(v):
        v = jnp.broadcast_to(jnp.sum(v, axis=1, keepdims=True), v.shape)
        for shift in (4, 2, 1):
            v = v + pltpu.roll(v, shift, 0)
        return v

    remain, search = rhs, rhs
    image = operate_packed(rhs)
    norm_now, energy = total(rhs * rhs), total(rhs * image)
    alpha = norm_now / energy
    solution = alpha * search
    for step in range(COARSE_ITERS - 1):
        inverse_norm = 1.0 / norm_now
        remain = remain - alpha * image
        across = operate_packed(remain)
        norm_next, own, mixed = total(remain * remain), total(remain * across), total(remain * image)
        beta = norm_next * inverse_norm
        energy = own + beta * (2.0 * mixed + beta * energy)
        search = remain + beta * search
        image = across + beta * image
        norm_now = norm_next
        alpha = norm_now / energy
        solution = solution + alpha * search
    return solution


def mirrored(k, count):
    result = 0
    while count > 1:
        result, k, count = 2 * result + k % 2, k // 2, count // 2
    return result


def whole_kernel(*refs):
    count = lax.axis_size("gy")
    here, there = refs[:count], refs[count : 2 * count]
    t_in, k_in, both1, even1, both2, even2, spread3, spread21, last, out, grid, fold1, folds1, fold2, folds2, spread2, held2, spread1, kept, doubled = refs[2 * count :]
    gx, gy, gz = lax.axis_index("gx"), lax.axis_index("gy"), lax.axis_index("gz")
    cx, cy = lax.axis_size("gx"), lax.axis_size("gy")
    bx, by, w1 = here[0].shape[2:]
    for k in range(cx * cy):
        x = jnp.bitwise_xor(gx, k % cx) * bx
        y = pl.multiple_of(jnp.bitwise_xor(gy, k // cx) * by, by)
        mine, other, j = k % cx, mirrored(k % cx, cx), k // cx
        for a in range(2):
            low = jnp.where(gz == 0, here[j][mine, a], there[j][mine, a]).reshape(bx * by, w1)
            top = jnp.where(gz == 0, there[j][other, a], here[j][other, a]).reshape(bx * by, w1)
            left = iota((bx * by, w1), 1) < w1 // 2
            one = jnp.where(left, low, pltpu.roll(top, w1 // 2, 1))
            two = jnp.where(left, pltpu.roll(low, w1 // 2, 1), top)
            spot = (pl.ds(x + 2, bx), pl.ds(y + TILE, by))
            grid[(2 * a, *spot)] = one.reshape(bx, by, w1)
            grid[(2 * a + 1, *spot)] = two.reshape(bx, by, w1)
    n1, m1 = cx * bx, cy * by
    inner = slice(TILE, TILE + m1)
    for ref in (grid.at[1], grid.at[2], grid.at[3], kept.at[0], kept.at[1]):
        for p in range(n1 + 4):
            if p < 2 or p >= n1 + 2:
                ref[p] = jnp.zeros((m1 + 2 * TILE, w1), jnp.float32)
            else:
                ref[p, :TILE] = jnp.zeros((TILE, w1), jnp.float32)
                ref[p, TILE + m1 :] = jnp.zeros((TILE, w1), jnp.float32)
    b1, fx1, fy1, fz1 = ([grid[a, 2 + p, inner] for p in range(n1)] for a in range(4))
    n2, m2 = n1 // 2, m1 // 2
    half = n2 * m2
    pairs = range(0, n1, 2)
    folds1[...] = jnp.concatenate(
        [0.5 * fx1[i] for i in pairs]
        + [0.5 * (fy1[i] + fy1[i + 1]) for i in pairs]
        + [0.5 * (fz1[i] + fz1[i + 1]) for i in pairs],
        0,
    )
    low, top = folds1[pl.ds(0, 3 * half, stride=2)], folds1[pl.ds(1, 3 * half, stride=2)]
    summed = select_dot(jnp.concatenate([low[:half] + top[:half], low[half : 2 * half]], 0), both1[...])

    def part(v):
        return [v[p * m2 : (p + 1) * m2] for p in range(n2)]

    fx2, fy2 = part(summed[:half]), part(summed[half:])
    fz2 = part(select_dot(low[2 * half :] + top[2 * half :], even1[...]))
    diagonal1, inv1, off1 = level_parts(fx1, fy1, fz1)
    t1, q1 = before(b1, diagonal1, inv1, off1)
    for p in range(n1):
        kept[0, 2 + p, inner] = t1[p]
        kept[1, 2 + p, inner] = inv1[p]
    diagonal2, inv2, off2 = level_parts(fx2, fy2, fz2)

    n3, m3 = n2 // 2, m2 // 2
    depth = w1 // n3
    blocks = range(0, n2, 2)
    wide = [
        jnp.concatenate([0.5 * fx2[i] for i in blocks], 1),
        jnp.concatenate([0.5 * (fy2[i] + fy2[i + 1]) for i in blocks], 1),
    ]
    thin = jnp.concatenate([0.5 * (fz2[i] + fz2[i + 1]) for i in blocks], 1)
    folds2[: 2 * m2] = select_dot(jnp.concatenate(wide, 0), both2[...])
    folds2[2 * m2 :] = select_dot(thin, even2[...])
    low, top = folds2[pl.ds(0, 3 * m3, stride=2)], folds2[pl.ds(1, 3 * m3, stride=2)]
    operate3 = coarse_operator(low[:m3] + top[:m3], low[m3 : 2 * m3], low[2 * m3 :] + top[2 * m3 :], depth)

    fold1[...] = jnp.concatenate([q1[i] + q1[i + 1] for i in pairs], 0)
    b2 = part(select_dot(fold1[pl.ds(0, half, stride=2)] + fold1[pl.ds(1, half, stride=2)], both1[...]))
    t2, q2 = before(b2, diagonal2, inv2, off2)
    fold2[...] = select_dot(jnp.concatenate([q2[i] + q2[i + 1] for i in blocks], 1), both2[...])
    c3 = coarse_solution(fold2[pl.ds(0, m3, stride=2)] + fold2[pl.ds(1, m3, stride=2)], operate3)

    row = select_dot(c3, spread3[...])
    for i in range(n3):
        spread2[pl.ds(i * m2, m3, stride=2)] = row[:, i * w1 : (i + 1) * w1]
        spread2[pl.ds(i * m2 + 1, m3, stride=2)] = row[:, i * w1 : (i + 1) * w1]
    up2 = [spread2[(p // 2) * m2 : (p // 2 + 1) * m2] for p in range(n2)]
    c2 = after(t2, up2, inv2, off2)

    held2[0] = jnp.zeros((m2, w1), jnp.float32)
    held2[n2 + 1] = jnp.zeros((m2, w1), jnp.float32)
    for p in range(n2):
        held2[1 + p] = c2[p]
    few = bx // 2 + 2
    near = held2[pl.ds(gx * (bx // 2), few)].reshape(few * m2, w1)
    row = select_dot(near, spread21[...])
    for p in range(few):
        spread1[p, :TILE] = jnp.zeros((TILE, w1), jnp.float32)
        spread1[p, TILE + m1 :] = jnp.zeros((TILE, w1), jnp.float32)
        spread1[p, pl.ds(TILE, m2, stride=2)] = row[p * m2 : (p + 1) * m2]
        spread1[p, pl.ds(TILE + 1, m2, stride=2)] = row[p * m2 : (p + 1) * m2]
    tall = by + 2 * TILE
    rows = pl.ds(pl.multiple_of(gy * by, by), tall)
    inner_z = iota((tall, w1), 1) > 0
    up1 = [spread1[p, rows] for p in range(few)]
    near = []
    for p in range(1, bx + 3):
        x = gx * bx + p
        e = up1[p // 2]
        fy, fz = grid[2, x, rows], jnp.where(inner_z, grid[3, x, rows], 0.0)
        total = grid[1, x, rows] * up1[(p - 1) // 2] + grid[1, x + 1, rows] * up1[(p + 1) // 2]
        total = total + fy * down(e, 0) + up(fy * e, 0) + fz * down(e, 1) + up(fz * e, 1)
        value = kept[0, x, rows] + (1.0 - damping) * e + kept[1, x, rows] * total
        near.append(value[TILE - 1 : TILE - 1 + by + TILE])
    tall = by + TILE
    row = select_dot(jnp.concatenate(near, 0), last[...])
    for s in range(3):
        doubled[s, pl.ds(0, (bx + 2) * tall, stride=2)] = row[:, s * w1 : (s + 1) * w1]
        doubled[s, pl.ds(1, (bx + 2) * tall, stride=2)] = row[:, s * w1 : (s + 1) * w1]
    ny = t_in.shape[1]

    def at(s, i, shift):
        first = (1 + i // 2) * 2 * tall + 2 + shift
        return doubled[s, first : first + ny]

    for i in range(t_in.shape[0]):
        value = t_in[i] + (1.0 - damping) * at(0, i, 0)
        value = value + k_in[0, i] * at(0, i - 1, 0) + k_in[1, i] * at(0, i + 1, 0)
        value = value + k_in[2, i] * at(0, i, -1) + k_in[3, i] * at(0, i, 1)
        out[i] = value + k_in[4, i] * at(2, i, 0) + k_in[5, i] * at(1, i, 0)


def traded(blocks, axis):
    count, cores = lax.axis_size(axis), lax.axis_size("gz")
    taken = []
    for kind, block in enumerate(blocks):
        route = []
        for i in range(count):
            other = i + 1 if (i + kind) % 2 == 0 else i - 1
            for c in range(cores):
                to = other * cores + c if 0 <= other < count else i * cores + cores - 1 - c
                route.append((i * cores + c, to))
        taken.append(lax.ppermute(block, (axis, "gz"), route))
    return taken


def doubled_over(block, axis):
    count, cores = lax.axis_size(axis), lax.axis_size("gz")
    steps = [1 << n for n in range(count.bit_length() - 1)]
    for up_step, down_step in zip(steps, reversed(steps)):
        route = [(i * cores + c, (i ^ (down_step if c else up_step)) * cores + c) for i in range(count) for c in range(cores)]
        block = jnp.concatenate([block, lax.ppermute(block, (axis, "gz"), route)], 0)
    return block


def f32(*shape):
    return jax.ShapeDtypeStruct(shape, jnp.float32)


def per_device_small(adjoint_residual, face_x, face_y, face_z):
    nx, ny, nz = adjoint_residual.shape
    near = [pltpu.VMEM((9, ny, nz), jnp.float32)] * 2
    cy = lax.axis_size("gy")
    own = jnp.stack((adjoint_residual, face_x, face_y, face_z))
    slabs = pl.pallas_call(
        x_kernel,
        out_shape=(f32(9, ny, nz), f32(9, ny, nz)),
        compiler_params=PARAMS,
        name="slabs_x",
    )(own)
    slabs = traded(slabs, "gx")
    faces = pl.pallas_call(
        faces_kernel,
        out_shape=f32(2, nx // 2, ny // 2, nz),
        scratch_shapes=[pltpu.VMEM((nx * ny, nz), jnp.float32)],
        compiler_params=PARAMS,
        cost_estimate=SMALL,
        name="faces",
    )(own)
    count = -(-9 * (nx + 4) // 8) * 8
    lines = pl.pallas_call(
        y_kernel,
        out_shape=(f32(count, nz), f32(count, nz)),
        scratch_shapes=near,
        compiler_params=PARAMS,
        name="slabs_y",
    )(own, *slabs)
    edge = pl.pallas_call(
        edge_x_kernel,
        out_shape=f32(nx + 4, ny + 2 * PAD, nz),
        scratch_shapes=near,
        compiler_params=PARAMS,
        cost_estimate=SMALL,
        name="edges_x",
    )(own, *slabs)
    swap = [(0, 1), (1, 0)]
    lines = traded(lines, "gy")
    edges_x = lax.ppermute(edge, "gz", swap)
    edge = pl.pallas_call(
        edge_y_kernel,
        out_shape=f32(nx + 4, 2 * TILE, nz),
        compiler_params=PARAMS,
        name="edges_y",
    )(*lines)
    edges_y = lax.ppermute(edge, "gz", swap)
    local = pl.pallas_call(
        z_kernel,
        out_shape=f32(4, nx + 2 * REACH, ny + 2 * PAD, nz),
        scratch_shapes=near + [pltpu.VMEM((count, nz), jnp.float32)],
        compiler_params=PARAMS,
        cost_estimate=SMALL,
        name="extend",
    )(own, *slabs, *lines)
    ext_x, ext_y, wide = nx + 2 * REACH, ny + 2 * PAD, 2 * nz
    field = pltpu.VMEM((ext_x, ext_y, wide), jnp.float32)
    e, q, r, m = pl.pallas_call(
        fine_kernel,
        out_shape=(f32(nx, ny, nz),) * 3 + (f32(2, nx // 2, ny // 2, nz),),
        scratch_shapes=[
            pltpu.VMEM((4, ext_x, ext_y, nz), jnp.float32),
            field,
            field,
            field,
            field,
            pltpu.VMEM((nx * ny // 2, nz), jnp.float32),
        ],
        compiler_params=PARAMS,
        name="fine",
    )(local, edges_x, edges_y, faces)
    blocks = nx * lax.axis_size("gx") // 8
    shapes = ((nz, nz), (nz, nz), (blocks * nz, nz), (blocks * nz, nz), (nz, blocks * nz), (nz, nz), (nz, 3 * nz))
    t, k, *matrices = pl.pallas_call(
        sweep_kernel,
        out_shape=(f32(nx, ny, nz), f32(6, nx, ny, nz))
        + tuple(jax.ShapeDtypeStruct(shape, jnp.bfloat16) for shape in shapes),
        compiler_params=PARAMS,
        cost_estimate=SMALL,
        name="sweep",
    )(local, edges_x, e, q, r)
    near = doubled_over(m[None], "gx")
    here = [near] + [
        lax.ppermute(near, "gy", [(i, i ^ n) for i in range(cy)]) for n in range(1, cy)
    ]
    there = [lax.ppermute(block, "gz", [(0, 1), (1, 0)]) for block in here]
    n1, m1 = m.shape[1] * lax.axis_size("gx"), m.shape[2] * cy
    n2, m2 = n1 // 2, m1 // 2
    tall = (nx // 2 + 2) * (ny // 2 + TILE)
    return pl.pallas_call(
        whole_kernel,
        out_shape=f32(nx, ny, nz),
        scratch_shapes=[
            pltpu.VMEM((4, n1 + 4, m1 + 2 * TILE, nz), jnp.float32),
            pltpu.VMEM((n2 * m1, nz), jnp.float32),
            pltpu.VMEM((3 * n2 * m1, nz), jnp.float32),
            pltpu.VMEM((m2, nz), jnp.float32),
            pltpu.VMEM((3 * m2, nz), jnp.float32),
            pltpu.VMEM((n1 * m1 // 8, nz), jnp.float32),
            pltpu.VMEM((n2 + 2, m2, nz), jnp.float32),
            pltpu.VMEM((nx // 4 + 2, m1 + 2 * TILE, nz), jnp.float32),
            pltpu.VMEM((2, n1 + 4, m1 + 2 * TILE, nz), jnp.float32),
            pltpu.VMEM((3, 2 * tall, nz), jnp.float32),
        ],
        compiler_params=PACKED,
        name="whole",
    )(*here, *there, t, k, *matrices)


def extended(block, sides, width):
    for axis, dim in sides:
        count = lax.axis_size(axis)
        forward = [(i, i + 1) for i in range(count - 1)]
        backward = [(target, source) for source, target in forward]
        low = lax.ppermute(
            lax.slice_in_dim(block, block.shape[dim] - width, None, axis=dim), axis, forward
        )
        high = lax.ppermute(lax.slice_in_dim(block, 0, width, axis=dim), axis, backward)
        block = jnp.concatenate([low, block, high], axis=dim)
    return block


def from_behind(block, axis, distance):
    devices = range(lax.axis_size(axis))
    route = [(i - distance, i) for i in devices if i - distance in devices]
    return lax.ppermute(block, axis, route)


def stencil(padded, field, coefs):
    low_x, high_x, low_y, high_y, low_z, high_z = coefs
    diagonal = low_x + high_x + low_y + high_y + low_z + high_z
    result = diagonal * field - low_x * padded[:-2, 1:-1, 1:-1] - high_x * padded[2:, 1:-1, 1:-1]
    result = result - low_y * padded[1:-1, :-2, 1:-1] - high_y * padded[1:-1, 2:, 1:-1]
    return result - low_z * padded[1:-1, 1:-1, :-2] - high_z * padded[1:-1, 1:-1, 2:]


def operate(field, coefs):
    padded = extended(field, (("gx", 0), ("gy", 1), ("gz", 2)), 1)
    return stencil(padded, field, coefs)


def operate_whole(field, coefs):
    return stencil(jnp.pad(field, 1), field, coefs)


def blocked(values):
    return values.reshape(values.shape[0] // 2, 2, values.shape[1] // 2, 2, values.shape[2] // 2, 2)


def coarse_face(values, dim, parity):
    others = tuple((2 * k + 1 for k in range(3) if k != dim))
    summed = jnp.sum(blocked(values), axis=others)
    return 0.5 * lax.index_in_dim(summed, parity, dim + 1, keepdims=False)


def coarsen(coefs):
    result = []
    for dim in range(3):
        result.append(coarse_face(coefs[2 * dim], dim, 0))
        result.append(coarse_face(coefs[2 * dim + 1], dim, 1))
    return tuple(result)


def restrict(values):
    return jnp.sum(blocked(values), axis=(1, 3, 5))


def prolong(values):
    shape_out = (values.shape[0] * 2, values.shape[1] * 2, values.shape[2] * 2)
    wide = jnp.broadcast_to(
        values[:, None, :, None, :, None],
        (values.shape[0], 2, values.shape[1], 2, values.shape[2], 2),
    )
    return wide.reshape(shape_out)


def total_local(value):
    return value


def conj_grad(rhs, coefs, apply_op, total):
    solution = jnp.zeros_like(rhs)
    remain = rhs
    search = rhs
    norm_now = total(jnp.sum(remain * remain))
    for step in range(COARSE_ITERS):
        image = apply_op(search, coefs)
        alpha = norm_now / total(jnp.sum(search * image))
        solution = solution + alpha * search
        remain = remain - alpha * image
        norm_next = total(jnp.sum(remain * remain))
        search = remain + norm_next / norm_now * search
        norm_now = norm_next
    return solution


def coarse_solve(rhs, coefs):
    part_x, part_y, part_z = rhs.shape
    count_x = lax.axis_size("gx")
    count_y = lax.axis_size("gy")
    count_z = lax.axis_size("gz")
    stacked = jnp.stack((rhs,) + coefs)[None]
    whole = lax.all_gather(stacked, ("gx", "gy", "gz"), axis=0, tiled=True)
    whole = whole.reshape(count_x, count_y, count_z, 7, part_x, part_y, part_z)
    whole = whole.transpose(3, 0, 4, 1, 5, 2, 6).reshape(
        7, count_x * part_x, count_y * part_y, count_z * part_z
    )
    whole_coefs = tuple((whole[k] for k in range(1, 7)))
    solution = conj_grad(whole[0], whole_coefs, operate_whole, total_local)
    starts = (
        lax.axis_index("gx") * part_x,
        lax.axis_index("gy") * part_y,
        lax.axis_index("gz") * part_z,
    )
    return lax.dynamic_slice(solution, starts, (part_x, part_y, part_z))


def cycle(rhs, levels_left, coefs):
    if levels_left == 1:
        return coarse_solve(rhs, coefs)
    diagonal = coefs[0] + coefs[1] + coefs[2] + coefs[3] + coefs[4] + coefs[5]
    field = damping * rhs / diagonal
    field = field + damping * (rhs - operate(field, coefs)) / diagonal
    remain = rhs - operate(field, coefs)
    field = field + prolong(cycle(restrict(remain), levels_left - 1, coarsen(coefs)))
    field = field + damping * (rhs - operate(field, coefs)) / diagonal
    return field


def per_device(adjoint_residual, face_x, face_y, face_z):
    rim_x = from_behind(face_x[:1], "gx", -1)
    rim_y = from_behind(face_y[:, :1], "gy", -1)
    rim_z = from_behind(face_z[:, :, :1], "gz", -1)
    high_x = jnp.concatenate([face_x[1:], rim_x], 0)
    high_y = jnp.concatenate([face_y[:, 1:], rim_y], 1)
    high_z = jnp.concatenate([face_z[:, :, 1:], rim_z], 2)
    coefs = (face_x, high_x, face_y, high_y, face_z, high_z)
    return cycle(adjoint_residual, LEVELS, coefs)


def fits(mesh, shape):
    nx, ny, nz = shape
    cx, cy, cz = mesh.shape["gx"], mesh.shape["gy"], mesh.shape["gz"]
    powers = cx & (cx - 1) == 0 and cy & (cy - 1) == 0 and cz == 2
    blocks = nx % (8 * cx) == 0 and ny % (16 * cy) == 0 and nz == 256
    return powers and blocks and (nx // 8) * (nz // 8) == 128 and nx * ny * nz <= 2**19


def per_block(mesh, *args):
    counts = (mesh.shape["gx"], mesh.shape["gy"], mesh.shape["gz"])
    whole = tuple(n * c for n, c in zip(args[0].shape, counts))
    return (per_device_small if fits(mesh, whole) else per_device)(*args)


def solution(mesh):
    return jax.shard_map(
        functools.partial(per_block, mesh),
        mesh=mesh,
        in_specs=(
            P("gx", "gy", "gz"),
            P("gx", "gy", "gz"),
            P("gx", "gy", "gz"),
            P("gx", "gy", "gz"),
        ),
        out_specs=P("gx", "gy", "gz"),
        check_vma=False,
    )
```

```python
import functools

import jax
import jax.numpy as jnp
from jax import lax
from jax.experimental import pallas as pl
from jax.experimental.pallas import tpu as pltpu
from jax.sharding import PartitionSpec as P

LEVELS = 4
COARSE_ITERS = 6


damping = 2.0 / 3.0

REACH = 3
TILE = 8
PAD = 4
SMALL = pl.CostEstimate(flops=2**20, bytes_accessed=2**20, transcendentals=0)
PARAMS = pltpu.CompilerParams(vmem_limit_bytes=16 * 2**20)
PACKED = pltpu.CompilerParams(
    vmem_limit_bytes=16 * 2**20
)


def up(v, axis):
    return pltpu.roll(v, v.shape[axis] - 1, axis)


def down(v, axis):
    return pltpu.roll(v, 1, axis)


def iota(shape, axis):
    return lax.broadcasted_iota(jnp.int32, shape, axis)


def chosen(mask):
    return jnp.where(mask, 1.0, 0.0).astype(jnp.bfloat16)


def select_dot(values, matrix):
    count = values.shape[0]
    high = values.astype(jnp.bfloat16).astype(jnp.float32)
    rest = values - high
    mid = rest.astype(jnp.bfloat16).astype(jnp.float32)
    parts = jnp.concatenate([high, mid, rest - mid], 0).astype(jnp.bfloat16)
    product = jnp.dot(parts, matrix, preferred_element_type=jnp.float32)
    return (product[2 * count :] + product[count : 2 * count]) + product[:count]


def inverse(diagonal):
    return jnp.where(diagonal > 0.0, damping / jnp.where(diagonal > 0.0, diagonal, 1.0), 0.0)


def side(axis):
    here = lax.axis_index(axis)
    first = jnp.where(here > 0, 1.0, 0.0)
    last = jnp.where(here < lax.axis_size(axis) - 1, 1.0, 0.0)
    return (here % 2 == 1, first), (here % 2 == 0, last)


def x_kernel(own, *slabs):
    nx, gx = own.shape[1], lax.axis_index("gx")
    for kind, out in enumerate(slabs):
        start = jnp.where((gx + kind) % 2 == 0, nx - 2, 0)
        for a in range(4):
            for n in range(2):
                out[2 * a + n] = own[a, start + n]
        out[8] = own[1, 2]


def sides_x(slabs, before, behind):
    for (even, keep), out in zip(side("gx"), (before, behind)):
        for n in range(9):
            out[n] = keep * jnp.where(even, slabs[0][n], slabs[1][n])


def y_kernel(own, s0, s1, o0, o1, before, behind):
    nx, ny = own.shape[1], own.shape[2]
    gy = lax.axis_index("gy")
    sides_x((s0, s1), before, behind)
    for kind, out in enumerate((o0, o1)):
        ahead = (gy + kind) % 2 == 0
        for p in range(nx + 4):
            for a in range(4):
                if p < 2:
                    v = before[2 * a + p]
                elif p < nx + 2:
                    v = own[a, p - 2]
                else:
                    v = behind[2 * a + p - nx - 2]
                at = (a * (nx + 4) + p) * 2
                out[at : at + 2] = jnp.where(ahead, v[ny - 2 :], v[:2])
                if a == 2:
                    out[8 * (nx + 4) + p : 8 * (nx + 4) + p + 1] = v[2:3]
        used = 9 * (nx + 4)
        out[used:] = jnp.zeros((out.shape[0] - used, out.shape[1]), jnp.float32)


def z_kernel(own, s0, s1, o0, o1, ext, before, behind, lines):
    nx, ny, nz = own.shape[1:]
    gz = lax.axis_index("gz")
    sides_x((s0, s1), before, behind)
    zero = jnp.zeros((PAD, nz), jnp.float32)
    empty = jnp.zeros((ny + 2 * PAD, nz), jnp.float32)
    for a in range(4):
        for p in range(nx + 2 * REACH):
            q = p - REACH
            if 0 <= q < nx:
                v = own[a, q]
            elif -2 <= q < 0:
                v = before[2 * a + q + 2]
            elif nx <= q < nx + 2:
                v = behind[2 * a + q - nx]
            elif q == nx + 2 and a == 1:
                v = behind[8]
            else:
                ext[a, p] = empty
                continue
            ext[a, p, :PAD] = zero
            ext[a, p, PAD + ny :] = zero
            ext[a, p, PAD : PAD + ny] = v
    for (even, keep), r in zip(side("gy"), (PAD - 2, PAD + ny)):
        lines[...] = keep * jnp.where(even, o0[...], o1[...])
        for p in range(nx + 4):
            for a in range(4):
                at = (a * (nx + 4) + p) * 2
                ext[a, 1 + p, r : r + 2] = lines[at : at + 2]
            if r > PAD:
                at = 8 * (nx + 4) + p
                ext[2, 1 + p, r + 2 : r + 3] = lines[at : at + 1]


def side_by_side(values):
    gz, nz = lax.axis_index("gz"), values[0].shape[1]
    lane, packed = iota(values[0].shape, 1), values[0]
    for a in range(1, 4):
        first = jnp.where(gz == 0, nz - 3 - 3 * a, 3 * a)
        moved = pltpu.roll(values[a], jnp.where(gz == 0, nz - 3 * a, 3 * a), 1)
        packed = jnp.where((lane >= first) & (lane < first + 3), moved, packed)
    return packed


def edge_x_kernel(own, s0, s1, out, before, behind):
    nx, ny, nz = own.shape[1:]
    sides_x((s0, s1), before, behind)
    for p in range(nx + 4):
        if p < 2:
            values = [before[2 * a + p] for a in range(4)]
        elif p < nx + 2:
            values = [own[a, p - 2] for a in range(4)]
        else:
            values = [behind[2 * a + p - nx - 2] for a in range(4)]
        out[p, :PAD] = jnp.zeros((PAD, nz), jnp.float32)
        out[p, PAD + ny :] = jnp.zeros((PAD, nz), jnp.float32)
        out[p, PAD : PAD + ny] = side_by_side(values)


def edge_y_kernel(o0, o1, out):
    planes, nz = out.shape[0], o0.shape[1]
    out[...] = jnp.zeros_like(out)
    for (even, keep), r in zip(side("gy"), (PAD - 2, 2 * TILE - PAD)):
        each = 2 * planes
        lines = [
            keep * jnp.where(even, o0[a * each : (a + 1) * each], o1[a * each : (a + 1) * each]) for a in range(4)
        ]
        packed = side_by_side(lines)
        for p in range(planes):
            out[p, r : r + 2] = packed[2 * p : 2 * p + 2]


def fine_kernel(local, edges_x, edges_y, faces, e_out, q_out, r_out, m_out, halo, e1, rd, dg, e2, rows):
    nx, ny, half = e_out.shape
    nz = 2 * half
    gx, gy, gz = lax.axis_index("gx"), lax.axis_index("gy"), lax.axis_index("gz")
    spot = iota((ny + 2 * PAD, half), 1)
    given = jnp.logical_or((gz == 0) & (spot < 3), (gz == 1) & (spot >= half - 3))
    gap = jnp.zeros((ny + 2 * PAD - 2 * TILE, half), jnp.float32)
    edge = {
        1 + p: edges_x[p] + jnp.concatenate([edges_y[p, :TILE], gap, edges_y[p, TILE:]], 0) for p in range(nx + 4)
    }
    for p in range(nx + 2 * REACH):
        for a in range(4):
            if 1 <= p < nx + 5:
                v = edge[p]
                if a > 0:
                    v = pltpu.roll(v, jnp.where(gz == 0, half - 3 * a, 3 * a), 1)
                halo[a, p] = jnp.where(given, v, 0.0)
            else:
                halo[a, p] = jnp.zeros((ny + 2 * PAD, half), jnp.float32)

    def ext(a, p):
        return jnp.concatenate([local[a, p], halo[a, p]], 1)

    shape = (ny + 2 * PAD, nz)
    row, lane = iota(shape, 0), iota(shape, 1)
    inner_z = jnp.logical_or(lane > 0, gz > 0)
    in_y = jnp.logical_and(
        jnp.logical_or(gy > 0, row >= PAD),
        jnp.logical_or(gy < lax.axis_size("gy") - 1, row < PAD + ny),
    )

    def off(e, p):
        fy, fz = ext(2, p), jnp.where(inner_z, ext(3, p), 0.0)
        here = e[p]
        total = ext(1, p) * e[p - 1] + ext(1, p + 1) * e[p + 1]
        total = total + fy * down(here, 0) + up(fy * here, 0)
        return total + fz * down(here, 1) + up(fz * here, 1)

    for p in range(1, nx + 2 * REACH - 1):
        fy, fz = ext(2, p), ext(3, p)
        diagonal = ext(1, p) + ext(1, p + 1) + fy + up(fy, 0) + fz + up(jnp.where(inner_z, fz, 0.0), 1)
        inv = inverse(diagonal)
        dg[p], rd[p] = diagonal, inv
        e1[p] = ext(0, p) * inv
    for p in range(2, nx + 2 * REACH - 2):
        value = (2.0 - damping) * e1[p] + rd[p] * off(e1, p)
        inside = in_y
        if p < REACH:
            inside = jnp.logical_and(inside, gx > 0)
        if p >= REACH + nx:
            inside = jnp.logical_and(inside, gx < lax.axis_size("gx") - 1)
        e2[p] = jnp.where(inside, value, 0.0)

    def mine(v):
        return v[PAD : PAD + ny, :half]

    sums = []
    for i in range(nx):
        p = REACH + i
        q = mine(ext(0, p) - dg[p] * e2[p] + off(e2, p))
        e_out[i], q_out[i], r_out[i] = mine(e2[p]), q, mine(rd[p])
        sums.append(q)
    pairs = range(0, nx, 2)
    both_low = chosen(iota((half, half), 0) // 2 == iota((half, half), 1))
    rows[...] = select_dot(jnp.concatenate([sums[i] + sums[i + 1] for i in pairs], 0), both_low)
    part = rows.shape[0] // 2
    total = rows[pl.ds(0, part, stride=2)] + rows[pl.ds(1, part, stride=2)]
    m_out[0] = faces[0] + total.reshape(m_out.shape[1:])
    m_out[1] = faces[1]


def faces_kernel(own, out, rows):
    nx, ny, half = own.shape[1:]

    def face(d, i):
        return 0.5 * own[d, i]

    pairs = range(0, nx, 2)
    fine, coarse = iota((half, half), 0), iota((half, half), 1)
    both_low, both_high = chosen(fine // 2 == coarse), chosen(fine // 2 + half // 2 == coarse)
    even_high = chosen(fine + half == 2 * coarse)
    count = len(pairs) * ny
    rows[:count] = select_dot(jnp.concatenate([face(1, i) for i in pairs], 0), both_high)
    rows[count:] = select_dot(jnp.concatenate([face(2, i) + face(2, i + 1) for i in pairs], 0), both_low) + select_dot(
        jnp.concatenate([face(3, i) + face(3, i + 1) for i in pairs], 0), even_high
    )
    part = count // 2
    even = rows[pl.ds(0, 2 * part, stride=2)]
    odd = rows[pl.ds(1, 2 * part, stride=2)]
    spot = iota((part, half), 1)
    out[0] = (even[:part] + odd[:part]).reshape(out.shape[1:])
    out[1] = (even[part:] + jnp.where(spot < half // 2, 0.0, odd[part:])).reshape(out.shape[1:])


def sweep_kernel(local, edges_x, e_in, q_in, r_in, t_out, k_out, *matrices):
    nx, ny, half = t_out.shape
    gz = lax.axis_index("gz")
    lane = iota((ny, half), 1)
    low_z, top_z = jnp.logical_or(lane > 0, gz > 0), lane < half - 1
    keep = jnp.where(gz == 0, 1.0, 0.0)
    inner = slice(PAD, PAD + ny)
    for i in range(nx):
        p, inv = REACH + i, r_in[i]
        fz = local[3, p, inner]
        far = keep * pltpu.roll(edges_x[p - 1, inner], half - 1 - 9, 1)
        high_z = jnp.where(top_z, up(fz, 1), far)
        faces = (local[1, p, inner], local[1, p + 1, inner], local[2, p, inner], local[2, p, PAD + 1 : PAD + 1 + ny])
        t_out[i] = e_in[i] + inv * q_in[i]
        for n, k in enumerate(faces + (jnp.where(low_z, fz, 0.0), high_z)):
            k_out[n, i] = inv * k
    both1, even1, both2, even2, spread3, spread2, last = matrices
    fine, coarse = iota(both1.shape, 0), iota(both1.shape, 1)
    both1[...], even1[...] = chosen(fine // 2 == coarse), chosen(fine == 2 * coarse)
    spread2[...] = chosen(coarse // 2 == fine)
    blocks = both2.shape[0] // half
    depth = half // blocks
    fine, coarse = iota(both2.shape, 0), iota(both2.shape, 1)
    block, fine = fine // half, fine % half
    valid = fine < 2 * depth
    both2[...] = chosen((fine // 2 + block * depth == coarse) & valid)
    even2[...] = chosen((fine + 2 * block * depth == 2 * coarse) & valid)
    fine, coarse = iota(spread3.shape, 1), iota(spread3.shape, 0)
    block, fine = fine // half, fine % half
    spread3[...] = chosen((fine // 2 + block * depth == coarse) & (fine < 2 * depth))
    spot = gz * half + iota(last.shape, 1) % half + (iota(last.shape, 1) // half + 1) % 3 - 1
    wanted = iota(last.shape, 0)
    last[...] = chosen((2 * wanted == spot) | (2 * wanted + 1 == spot))


def planes_of(ref):
    return [ref[p] for p in range(ref.shape[0])]


def level_parts(fx, fy, fz):
    shape = fy[0].shape
    row, lane = iota(shape, 0), iota(shape, 1)
    n = len(fx)
    zero = jnp.zeros(shape, jnp.float32)
    fym = [jnp.where(row > 0, v, 0.0) for v in fy]
    fzm = [jnp.where(lane > 0, v, 0.0) for v in fz]
    high = [fx[p + 1] if p + 1 < n else zero for p in range(n)]
    diagonal = [fx[p] + high[p] + fy[p] + up(fym[p], 0) + fz[p] + up(fzm[p], 1) for p in range(n)]

    def off(e):
        result = []
        for p in range(n):
            total = fym[p] * down(e[p], 0) + up(fym[p] * e[p], 0)
            total = total + fzm[p] * down(e[p], 1) + up(fzm[p] * e[p], 1)
            if p > 0:
                total = total + fx[p] * e[p - 1]
            if p + 1 < n:
                total = total + fx[p + 1] * e[p + 1]
            result.append(total)
        return result

    return diagonal, [inverse(d) for d in diagonal], off


def before(b, diagonal, inv, off):
    e1 = [v * r for v, r in zip(b, inv)]
    e2 = [(2.0 - damping) * e + r * o for e, r, o in zip(e1, inv, off(e1))]
    q = [v - d * e + o for v, d, e, o in zip(b, diagonal, e2, off(e2))]
    return [e + r * v for e, r, v in zip(e2, inv, q)], q


def after(t, c, inv, off):
    return [v + (1.0 - damping) * k + r * o for v, k, r, o in zip(t, c, inv, off(c))]


def coarse_operator(fx, fy, fz, depth):
    row, lane = iota(fx.shape, 0), iota(fx.shape, 1)
    fxm = jnp.where(lane >= depth, fx, 0.0)
    fym = jnp.where(row > 0, fy, 0.0)
    fzm = jnp.where(lane % depth > 0, fz, 0.0)
    wide = fx.shape[1]

    def up_x(v):
        return pltpu.roll(v, wide - depth, 1)

    hx, hy, hz = up_x(fxm), up(fym, 0), up(fzm, 1)
    diagonal = (fx + hx) + (fy + hy) + (fz + hz)

    def operate_packed(v):
        along_x = fxm * pltpu.roll(v, depth, 1) + hx * up_x(v)
        along_y = fym * down(v, 0) + hy * up(v, 0)
        along_z = fzm * down(v, 1) + hz * up(v, 1)
        return (diagonal * v - along_y) - (along_x + along_z)

    return operate_packed


def coarse_solution(rhs, operate_packed):
    def total(v):
        v = jnp.broadcast_to(jnp.sum(v, axis=1, keepdims=True), v.shape)
        for shift in (4, 2, 1):
            v = v + pltpu.roll(v, shift, 0)
        return v

    remain, search = rhs, rhs
    image = operate_packed(rhs)
    norm_now, energy = total(rhs * rhs), total(rhs * image)
    alpha = norm_now / energy
    solution = alpha * search
    for step in range(COARSE_ITERS - 1):
        inverse_norm = 1.0 / norm_now
        remain = remain - alpha * image
        across = operate_packed(remain)
        norm_next, own, mixed = total(remain * remain), total(remain * across), total(remain * image)
        beta = norm_next * inverse_norm
        energy = own + beta * (2.0 * mixed + beta * energy)
        search = remain + beta * search
        image = across + beta * image
        norm_now = norm_next
        alpha = norm_now / energy
        solution = solution + alpha * search
    return solution


def mirrored(k, count):
    result = 0
    while count > 1:
        result, k, count = 2 * result + k % 2, k // 2, count // 2
    return result


def whole_kernel(*refs):
    count = lax.axis_size("gy")
    here, there = refs[:count], refs[count : 2 * count]
    t_in, k_in, both1, even1, both2, even2, spread3, spread21, last, out, grid, fold1, folds1, fold2, folds2, spread2, held2, spread1, kept, doubled = refs[2 * count :]
    gx, gy, gz = lax.axis_index("gx"), lax.axis_index("gy"), lax.axis_index("gz")
    cx, cy = lax.axis_size("gx"), lax.axis_size("gy")
    bx, by, w1 = here[0].shape[2:]
    for k in range(cx * cy):
        x = jnp.bitwise_xor(gx, k % cx) * bx
        y = pl.multiple_of(jnp.bitwise_xor(gy, k // cx) * by, by)
        mine, other, j = k % cx, k % cx, k // cx
        for a in range(2):
            low = jnp.where(gz == 0, here[j][mine, a], there[j][mine, a]).reshape(bx * by, w1)
            top = jnp.where(gz == 0, there[j][other, a], here[j][other, a]).reshape(bx * by, w1)
            left = iota((bx * by, w1), 1) < w1 // 2
            one = jnp.where(left, low, pltpu.roll(top, w1 // 2, 1))
            two = jnp.where(left, pltpu.roll(low, w1 // 2, 1), top)
            spot = (pl.ds(x + 2, bx), pl.ds(y + TILE, by))
            grid[(2 * a, *spot)] = one.reshape(bx, by, w1)
            grid[(2 * a + 1, *spot)] = two.reshape(bx, by, w1)
    n1, m1 = cx * bx, cy * by
    inner = slice(TILE, TILE + m1)
    for ref in (grid.at[1], grid.at[2], grid.at[3], kept.at[0], kept.at[1]):
        for p in range(n1 + 4):
            if p < 2 or p >= n1 + 2:
                ref[p] = jnp.zeros((m1 + 2 * TILE, w1), jnp.float32)
            else:
                ref[p, :TILE] = jnp.zeros((TILE, w1), jnp.float32)
                ref[p, TILE + m1 :] = jnp.zeros((TILE, w1), jnp.float32)
    b1, fx1, fy1, fz1 = ([grid[a, 2 + p, inner] for p in range(n1)] for a in range(4))
    n2, m2 = n1 // 2, m1 // 2
    half = n2 * m2
    pairs = range(0, n1, 2)
    folds1[...] = jnp.concatenate(
        [0.5 * fx1[i] for i in pairs]
        + [0.5 * (fy1[i] + fy1[i + 1]) for i in pairs]
        + [0.5 * (fz1[i] + fz1[i + 1]) for i in pairs],
        0,
    )
    low, top = folds1[pl.ds(0, 3 * half, stride=2)], folds1[pl.ds(1, 3 * half, stride=2)]
    summed = select_dot(jnp.concatenate([low[:half] + top[:half], low[half : 2 * half]], 0), both1[...])

    def part(v):
        return [v[p * m2 : (p + 1) * m2] for p in range(n2)]

    fx2, fy2 = part(summed[:half]), part(summed[half:])
    fz2 = part(select_dot(low[2 * half :] + top[2 * half :], even1[...]))
    diagonal1, inv1, off1 = level_parts(fx1, fy1, fz1)
    t1, q1 = before(b1, diagonal1, inv1, off1)
    for p in range(n1):
        kept[0, 2 + p, inner] = t1[p]
        kept[1, 2 + p, inner] = inv1[p]
    diagonal2, inv2, off2 = level_parts(fx2, fy2, fz2)

    n3, m3 = n2 // 2, m2 // 2
    depth = w1 // n3
    blocks = range(0, n2, 2)
    wide = [
        jnp.concatenate([0.5 * fx2[i] for i in blocks], 1),
        jnp.concatenate([0.5 * (fy2[i] + fy2[i + 1]) for i in blocks], 1),
    ]
    thin = jnp.concatenate([0.5 * (fz2[i] + fz2[i + 1]) for i in blocks], 1)
    folds2[: 2 * m2] = select_dot(jnp.concatenate(wide, 0), both2[...])
    folds2[2 * m2 :] = select_dot(thin, even2[...])
    low, top = folds2[pl.ds(0, 3 * m3, stride=2)], folds2[pl.ds(1, 3 * m3, stride=2)]
    operate3 = coarse_operator(low[:m3] + top[:m3], low[m3 : 2 * m3], low[2 * m3 :] + top[2 * m3 :], depth)

    fold1[...] = jnp.concatenate([q1[i] + q1[i + 1] for i in pairs], 0)
    b2 = part(select_dot(fold1[pl.ds(0, half, stride=2)] + fold1[pl.ds(1, half, stride=2)], both1[...]))
    t2, q2 = before(b2, diagonal2, inv2, off2)
    fold2[...] = select_dot(jnp.concatenate([q2[i] + q2[i + 1] for i in blocks], 1), both2[...])
    c3 = coarse_solution(fold2[pl.ds(0, m3, stride=2)] + fold2[pl.ds(1, m3, stride=2)], operate3)

    row = select_dot(c3, spread3[...])
    for i in range(n3):
        spread2[pl.ds(i * m2, m3, stride=2)] = row[:, i * w1 : (i + 1) * w1]
        spread2[pl.ds(i * m2 + 1, m3, stride=2)] = row[:, i * w1 : (i + 1) * w1]
    up2 = [spread2[(p // 2) * m2 : (p // 2 + 1) * m2] for p in range(n2)]
    c2 = after(t2, up2, inv2, off2)

    held2[0] = jnp.zeros((m2, w1), jnp.float32)
    held2[n2 + 1] = jnp.zeros((m2, w1), jnp.float32)
    for p in range(n2):
        held2[1 + p] = c2[p]
    few = bx // 2 + 2
    near = held2[pl.ds(gx * (bx // 2), few)].reshape(few * m2, w1)
    row = select_dot(near, spread21[...])
    for p in range(few):
        spread1[p, :TILE] = jnp.zeros((TILE, w1), jnp.float32)
        spread1[p, TILE + m1 :] = jnp.zeros((TILE, w1), jnp.float32)
        spread1[p, pl.ds(TILE, m2, stride=2)] = row[p * m2 : (p + 1) * m2]
        spread1[p, pl.ds(TILE + 1, m2, stride=2)] = row[p * m2 : (p + 1) * m2]
    tall = by + 2 * TILE
    rows = pl.ds(pl.multiple_of(gy * by, by), tall)
    inner_z = iota((tall, w1), 1) > 0
    up1 = [spread1[p, rows] for p in range(few)]
    near = []
    for p in range(1, bx + 3):
        x = gx * bx + p
        e = up1[p // 2]
        fy, fz = grid[2, x, rows], jnp.where(inner_z, grid[3, x, rows], 0.0)
        total = grid[1, x, rows] * up1[(p - 1) // 2] + grid[1, x + 1, rows] * up1[(p + 1) // 2]
        total = total + fy * down(e, 0) + up(fy * e, 0) + fz * down(e, 1) + up(fz * e, 1)
        value = kept[0, x, rows] + (1.0 - damping) * e + kept[1, x, rows] * total
        near.append(value[TILE - 1 : TILE - 1 + by + TILE])
    tall = by + TILE
    row = select_dot(jnp.concatenate(near, 0), last[...])
    for s in range(3):
        doubled[s, pl.ds(0, (bx + 2) * tall, stride=2)] = row[:, s * w1 : (s + 1) * w1]
        doubled[s, pl.ds(1, (bx + 2) * tall, stride=2)] = row[:, s * w1 : (s + 1) * w1]
    ny = t_in.shape[1]

    def at(s, i, shift):
        first = (1 + i // 2) * 2 * tall + 2 + shift
        return doubled[s, first : first + ny]

    for i in range(t_in.shape[0]):
        value = t_in[i] + (1.0 - damping) * at(0, i, 0)
        value = value + k_in[0, i] * at(0, i - 1, 0) + k_in[1, i] * at(0, i + 1, 0)
        value = value + k_in[2, i] * at(0, i, -1) + k_in[3, i] * at(0, i, 1)
        out[i] = value + k_in[4, i] * at(2, i, 0) + k_in[5, i] * at(1, i, 0)


def traded(blocks, axis):
    count, cores = lax.axis_size(axis), lax.axis_size("gz")
    taken = []
    for kind, block in enumerate(blocks):
        route = []
        for i in range(count):
            other = i + 1 if (i + kind) % 2 == 0 else i - 1
            for c in range(cores):
                to = other * cores + c if 0 <= other < count else i * cores + cores - 1 - c
                route.append((i * cores + c, to))
        taken.append(lax.ppermute(block, (axis, "gz"), route))
    return taken


def doubled_over(block, axis):
    count, cores = lax.axis_size(axis), lax.axis_size("gz")
    steps = [1 << n for n in range(count.bit_length() - 1)]
    for up_step, down_step in zip(steps, reversed(steps)):
        route = [(i * cores + c, (i ^ (down_step if c else up_step)) * cores + c) for i in range(count) for c in range(cores)]
        block = jnp.concatenate([block, lax.ppermute(block, (axis, "gz"), route)], 0)
    return block


def f32(*shape):
    return jax.ShapeDtypeStruct(shape, jnp.float32)


def per_device_small(adjoint_residual, face_x, face_y, face_z):
    nx, ny, nz = adjoint_residual.shape
    near = [pltpu.VMEM((9, ny, nz), jnp.float32)] * 2
    cy = lax.axis_size("gy")
    own = jnp.stack((adjoint_residual, face_x, face_y, face_z))
    slabs = pl.pallas_call(
        x_kernel,
        out_shape=(f32(9, ny, nz), f32(9, ny, nz)),
        compiler_params=PARAMS,
        name="slabs_x",
    )(own)
    slabs = traded(slabs, "gx")
    faces = pl.pallas_call(
        faces_kernel,
        out_shape=f32(2, nx // 2, ny // 2, nz),
        scratch_shapes=[pltpu.VMEM((nx * ny, nz), jnp.float32)],
        compiler_params=PARAMS,
        cost_estimate=SMALL,
        name="faces",
    )(own)
    count = -(-9 * (nx + 4) // 8) * 8
    lines = pl.pallas_call(
        y_kernel,
        out_shape=(f32(count, nz), f32(count, nz)),
        scratch_shapes=near,
        compiler_params=PARAMS,
        name="slabs_y",
    )(own, *slabs)
    edge = pl.pallas_call(
        edge_x_kernel,
        out_shape=f32(nx + 4, ny + 2 * PAD, nz),
        scratch_shapes=near,
        compiler_params=PARAMS,
        cost_estimate=SMALL,
        name="edges_x",
    )(own, *slabs)
    swap = [(0, 1), (1, 0)]
    lines = traded(lines, "gy")
    edges_x = lax.ppermute(edge, "gz", swap)
    edge = pl.pallas_call(
        edge_y_kernel,
        out_shape=f32(nx + 4, 2 * TILE, nz),
        compiler_params=PARAMS,
        name="edges_y",
    )(*lines)
    edges_y = lax.ppermute(edge, "gz", swap)
    local = pl.pallas_call(
        z_kernel,
        out_shape=f32(4, nx + 2 * REACH, ny + 2 * PAD, nz),
        scratch_shapes=near + [pltpu.VMEM((count, nz), jnp.float32)],
        compiler_params=PARAMS,
        cost_estimate=SMALL,
        name="extend",
    )(own, *slabs, *lines)
    ext_x, ext_y, wide = nx + 2 * REACH, ny + 2 * PAD, 2 * nz
    field = pltpu.VMEM((ext_x, ext_y, wide), jnp.float32)
    e, q, r, m = pl.pallas_call(
        fine_kernel,
        out_shape=(f32(nx, ny, nz),) * 3 + (f32(2, nx // 2, ny // 2, nz),),
        scratch_shapes=[
            pltpu.VMEM((4, ext_x, ext_y, nz), jnp.float32),
            field,
            field,
            field,
            field,
            pltpu.VMEM((nx * ny // 2, nz), jnp.float32),
        ],
        compiler_params=PARAMS,
        name="fine",
    )(local, edges_x, edges_y, faces)
    blocks = nx * lax.axis_size("gx") // 8
    shapes = ((nz, nz), (nz, nz), (blocks * nz, nz), (blocks * nz, nz), (nz, blocks * nz), (nz, nz), (nz, 3 * nz))
    t, k, *matrices = pl.pallas_call(
        sweep_kernel,
        out_shape=(f32(nx, ny, nz), f32(6, nx, ny, nz))
        + tuple(jax.ShapeDtypeStruct(shape, jnp.bfloat16) for shape in shapes),
        compiler_params=PARAMS,
        cost_estimate=SMALL,
        name="sweep",
    )(local, edges_x, e, q, r)
    cx = lax.axis_size("gx")
    near = [lax.ppermute(m[None], "gx", [(i, i ^ n) for i in range(cx)]) for n in range(1, cx)]
    near = jnp.concatenate([m[None]] + near, 0)
    here = [near] + [
        lax.ppermute(near, "gy", [(i, i ^ n) for i in range(cy)]) for n in range(1, cy)
    ]
    there = [lax.ppermute(block, "gz", [(0, 1), (1, 0)]) for block in here]
    n1, m1 = m.shape[1] * lax.axis_size("gx"), m.shape[2] * cy
    n2, m2 = n1 // 2, m1 // 2
    tall = (nx // 2 + 2) * (ny // 2 + TILE)
    return pl.pallas_call(
        whole_kernel,
        out_shape=f32(nx, ny, nz),
        scratch_shapes=[
            pltpu.VMEM((4, n1 + 4, m1 + 2 * TILE, nz), jnp.float32),
            pltpu.VMEM((n2 * m1, nz), jnp.float32),
            pltpu.VMEM((3 * n2 * m1, nz), jnp.float32),
            pltpu.VMEM((m2, nz), jnp.float32),
            pltpu.VMEM((3 * m2, nz), jnp.float32),
            pltpu.VMEM((n1 * m1 // 8, nz), jnp.float32),
            pltpu.VMEM((n2 + 2, m2, nz), jnp.float32),
            pltpu.VMEM((nx // 4 + 2, m1 + 2 * TILE, nz), jnp.float32),
            pltpu.VMEM((2, n1 + 4, m1 + 2 * TILE, nz), jnp.float32),
            pltpu.VMEM((3, 2 * tall, nz), jnp.float32),
        ],
        compiler_params=PACKED,
        name="whole",
    )(*here, *there, t, k, *matrices)


def extended(block, sides, width):
    for axis, dim in sides:
        count = lax.axis_size(axis)
        forward = [(i, i + 1) for i in range(count - 1)]
        backward = [(target, source) for source, target in forward]
        low = lax.ppermute(
            lax.slice_in_dim(block, block.shape[dim] - width, None, axis=dim), axis, forward
        )
        high = lax.ppermute(lax.slice_in_dim(block, 0, width, axis=dim), axis, backward)
        block = jnp.concatenate([low, block, high], axis=dim)
    return block


def from_behind(block, axis, distance):
    devices = range(lax.axis_size(axis))
    route = [(i - distance, i) for i in devices if i - distance in devices]
    return lax.ppermute(block, axis, route)


def stencil(padded, field, coefs):
    low_x, high_x, low_y, high_y, low_z, high_z = coefs
    diagonal = low_x + high_x + low_y + high_y + low_z + high_z
    result = diagonal * field - low_x * padded[:-2, 1:-1, 1:-1] - high_x * padded[2:, 1:-1, 1:-1]
    result = result - low_y * padded[1:-1, :-2, 1:-1] - high_y * padded[1:-1, 2:, 1:-1]
    return result - low_z * padded[1:-1, 1:-1, :-2] - high_z * padded[1:-1, 1:-1, 2:]


def operate(field, coefs):
    padded = extended(field, (("gx", 0), ("gy", 1), ("gz", 2)), 1)
    return stencil(padded, field, coefs)


def operate_whole(field, coefs):
    return stencil(jnp.pad(field, 1), field, coefs)


def blocked(values):
    return values.reshape(values.shape[0] // 2, 2, values.shape[1] // 2, 2, values.shape[2] // 2, 2)


def coarse_face(values, dim, parity):
    others = tuple((2 * k + 1 for k in range(3) if k != dim))
    summed = jnp.sum(blocked(values), axis=others)
    return 0.5 * lax.index_in_dim(summed, parity, dim + 1, keepdims=False)


def coarsen(coefs):
    result = []
    for dim in range(3):
        result.append(coarse_face(coefs[2 * dim], dim, 0))
        result.append(coarse_face(coefs[2 * dim + 1], dim, 1))
    return tuple(result)


def restrict(values):
    return jnp.sum(blocked(values), axis=(1, 3, 5))


def prolong(values):
    shape_out = (values.shape[0] * 2, values.shape[1] * 2, values.shape[2] * 2)
    wide = jnp.broadcast_to(
        values[:, None, :, None, :, None],
        (values.shape[0], 2, values.shape[1], 2, values.shape[2], 2),
    )
    return wide.reshape(shape_out)


def total_local(value):
    return value


def conj_grad(rhs, coefs, apply_op, total):
    solution = jnp.zeros_like(rhs)
    remain = rhs
    search = rhs
    norm_now = total(jnp.sum(remain * remain))
    for step in range(COARSE_ITERS):
        image = apply_op(search, coefs)
        alpha = norm_now / total(jnp.sum(search * image))
        solution = solution + alpha * search
        remain = remain - alpha * image
        norm_next = total(jnp.sum(remain * remain))
        search = remain + norm_next / norm_now * search
        norm_now = norm_next
    return solution


def coarse_solve(rhs, coefs):
    part_x, part_y, part_z = rhs.shape
    count_x = lax.axis_size("gx")
    count_y = lax.axis_size("gy")
    count_z = lax.axis_size("gz")
    stacked = jnp.stack((rhs,) + coefs)[None]
    whole = lax.all_gather(stacked, ("gx", "gy", "gz"), axis=0, tiled=True)
    whole = whole.reshape(count_x, count_y, count_z, 7, part_x, part_y, part_z)
    whole = whole.transpose(3, 0, 4, 1, 5, 2, 6).reshape(
        7, count_x * part_x, count_y * part_y, count_z * part_z
    )
    whole_coefs = tuple((whole[k] for k in range(1, 7)))
    solution = conj_grad(whole[0], whole_coefs, operate_whole, total_local)
    starts = (
        lax.axis_index("gx") * part_x,
        lax.axis_index("gy") * part_y,
        lax.axis_index("gz") * part_z,
    )
    return lax.dynamic_slice(solution, starts, (part_x, part_y, part_z))


def cycle(rhs, levels_left, coefs):
    if levels_left == 1:
        return coarse_solve(rhs, coefs)
    diagonal = coefs[0] + coefs[1] + coefs[2] + coefs[3] + coefs[4] + coefs[5]
    field = damping * rhs / diagonal
    field = field + damping * (rhs - operate(field, coefs)) / diagonal
    remain = rhs - operate(field, coefs)
    field = field + prolong(cycle(restrict(remain), levels_left - 1, coarsen(coefs)))
    field = field + damping * (rhs - operate(field, coefs)) / diagonal
    return field


def per_device(adjoint_residual, face_x, face_y, face_z):
    rim_x = from_behind(face_x[:1], "gx", -1)
    rim_y = from_behind(face_y[:, :1], "gy", -1)
    rim_z = from_behind(face_z[:, :, :1], "gz", -1)
    high_x = jnp.concatenate([face_x[1:], rim_x], 0)
    high_y = jnp.concatenate([face_y[:, 1:], rim_y], 1)
    high_z = jnp.concatenate([face_z[:, :, 1:], rim_z], 2)
    coefs = (face_x, high_x, face_y, high_y, face_z, high_z)
    return cycle(adjoint_residual, LEVELS, coefs)


def fits(mesh, shape):
    nx, ny, nz = shape
    cx, cy, cz = mesh.shape["gx"], mesh.shape["gy"], mesh.shape["gz"]
    powers = cx & (cx - 1) == 0 and cy & (cy - 1) == 0 and cz == 2
    blocks = nx % (8 * cx) == 0 and ny % (16 * cy) == 0 and nz == 256
    return powers and blocks and (nx // 8) * (nz // 8) == 128 and nx * ny * nz <= 2**19


def per_block(mesh, *args):
    counts = (mesh.shape["gx"], mesh.shape["gy"], mesh.shape["gz"])
    whole = tuple(n * c for n, c in zip(args[0].shape, counts))
    return (per_device_small if fits(mesh, whole) else per_device)(*args)


def solution(mesh):
    return jax.shard_map(
        functools.partial(per_block, mesh),
        mesh=mesh,
        in_specs=(
            P("gx", "gy", "gz"),
            P("gx", "gy", "gz"),
            P("gx", "gy", "gz"),
            P("gx", "gy", "gz"),
        ),
        out_specs=P("gx", "gy", "gz"),
        check_vma=False,
    )
```
